128 devices in a mesh: row: 16 (over y_lo, z, core), col: 8 (over x, y_hi).
Axes of the slice: x: 4, y: 4 (y_hi: 2, y_lo: 2; y = y_hi * 2 + y_lo), z: 4, core: 2. Of those that a mesh axis runs over, the one named last changes fastest.
Arguments:
- covariance: float32 [1, 8192, 8192], P(None, 'row', 'col'), may hold values from -120 to 120, as said below
- latitude_offset: int32 [1, 1, 8192], replicated, may hold values from -2 to 2
- longitude_offset: int32 [1, 1, 8192], replicated, may hold values from -3 to 3
- upwind: int32 [1, 1, 8192], replicated, may hold values from 0 to 3
- courant: float32 [1, 1, 8192], replicated, may hold values from 0.05 to 0.45
- longitude_diffusion: float32 [1, 8192], replicated, may hold values from 0.01 to 0.08
- latitude_diffusion: float32 [1, 8192], replicated, may hold values from 0.01 to 0.08
Outputs:
- forecast_cov: float32 [1, 8192, 8192], P(None, 'row', 'col')
The draws below stay inside these ranges and needn't reach their ends.
Inputs may be any that keep to these rules, and one draw needn't show every extreme that they name: `covariance`: each level's matrix is symmetric up to rounding.
All inputs are finite; a program needn't handle non-finite values.
Results may differ from the reference program's by a relative error of at most 0.0003.
Values sent between devices are 32-bit elements; how exact they have to be, the bound alone decides.
No kernel may reach another device: no remote copies, remote signals or barrier semaphores. Data moves between devices by JAX's collectives and lax.ppermute only.
A program may use at most 128 MiB of HBM per device.

```python
import jax
import jax.numpy as jnp
from jax import lax

NLAT = 64
NLON = 128
NV = 8192
STEPS = 1
LEV = 1


def draw_covariance(key, part):
    base_key = jax.random.fold_in(key, 7)
    key_noise, key_diag = jax.random.split(base_key, 2)
    noise_part = 3.0 * jax.random.truncated_normal(key_noise, -4.0, 4.0, (LEV, NV, NV), jnp.float32)
    symmetric = (noise_part + jnp.swapaxes(noise_part, 1, 2)) * 0.7071
    diagonal_part = jax.random.uniform(key_diag, (LEV, NV), jnp.float32, 4.0, 12.0)
    matrix = symmetric + jnp.eye(NV, dtype=jnp.float32)[None] * diagonal_part[:, :, None]
    return matrix


def touch_ends(entries, own_key, low, top_value):
    shape = entries.shape
    spot = [jax.random.randint(jax.random.fold_in(own_key, axis), (), 0, shape[axis]) for axis in range(len(shape))]
    entries = entries.at[tuple(spot)].set(low)
    longest = shape.index(max(shape))
    spot[longest] = (spot[longest] + 1) % shape[longest]
    return entries.at[tuple(spot)].set(top_value)


def setup_inputs(seed: int = 0) -> dict:
    seeds = jax.random.split(jax.random.key(seed), 8)
    return {
        "covariance": draw_covariance(jax.random.fold_in(seeds[7], 71), 0),
        "latitude_offset": touch_ends(jax.random.randint(seeds[1], (LEV, STEPS, NV), -2, 3), jax.random.fold_in(seeds[1], 1), -2, 2).astype(jnp.int32),
        "longitude_offset": touch_ends(jax.random.randint(seeds[2], (LEV, STEPS, NV), -3, 4), jax.random.fold_in(seeds[2], 1), -3, 3).astype(jnp.int32),
        "upwind": touch_ends(jax.random.randint(seeds[3], (LEV, STEPS, NV), 0, 4), jax.random.fold_in(seeds[3], 1), 0, 3).astype(jnp.int32),
        "courant": jnp.clip(jax.random.uniform(seeds[4], (LEV, STEPS, NV), jnp.float32, 0.05, 0.45), 0.05, 0.45),
        "longitude_diffusion": jnp.clip(jax.random.uniform(seeds[5], (LEV, NV), jnp.float32, 0.01, 0.08), 0.01, 0.08),
        "latitude_diffusion": jnp.clip(jax.random.uniform(seeds[6], (LEV, NV), jnp.float32, 0.01, 0.08), 0.01, 0.08),
    }


def predicted_covariance(field_stack, latitude_offset, longitude_offset, upwind, courant, longitude_diffusion, latitude_diffusion):
    cell_index = jnp.arange(NLAT * NLON, dtype=jnp.int32)
    lat_cell = cell_index // NLON
    lon_cell = cell_index % NLON
    lon_coeff = longitude_diffusion.reshape(NLAT, NLON)
    lat_coeff = latitude_diffusion.reshape(NLAT, NLON)
    cells_total = NLAT * NLON
    for substep in range(STEPS):
        lat_depart = jnp.clip(lat_cell + latitude_offset[substep], 0, NLAT - 1)
        lon_depart = (lon_cell + longitude_offset[substep]) % NLON
        up_code = upwind[substep]
        lat_near = jnp.clip(lat_depart + (up_code == 2).astype(jnp.int32) - (up_code == 3).astype(jnp.int32), 0, NLAT - 1)
        lon_near = (lon_depart + (up_code == 0).astype(jnp.int32) - (up_code == 1).astype(jnp.int32)) % NLON
        depart = (lat_depart * NLON + lon_depart).astype(jnp.int32)
        near = (lat_near * NLON + lon_near).astype(jnp.int32)
        both_index = jnp.concatenate([depart, near]).astype(jnp.int32)
        picked = jnp.take(field_stack, both_index, axis=1)
        weight = courant[substep]
        shifted = (1.0 - weight) * picked[:, :cells_total] + weight * picked[:, cells_total:]
        grid_view = shifted.reshape(shifted.shape[0], NLAT, NLON)
        east_side = jnp.roll(grid_view, -1, axis=2)
        west_side = jnp.roll(grid_view, 1, axis=2)
        north_side = jnp.concatenate([grid_view[:, 1:], grid_view[:, -1:]], axis=1)
        south_side = jnp.concatenate([grid_view[:, :1], grid_view[:, :-1]], axis=1)
        grid_view = grid_view + lon_coeff * (east_side + west_side - 2.0 * grid_view) + lat_coeff * (north_side + south_side - 2.0 * grid_view)
        field_stack = grid_view.reshape(shifted.shape[0], NLAT * NLON)
    return field_stack


def apply_rows(matrix, latitude_offset, longitude_offset, upwind, courant, longitude_diffusion, latitude_diffusion):
    block_rows = min(512, NV)
    block_groups = matrix.reshape(NV // block_rows, block_rows, NV)
    finished_work = lax.map(lambda block_portion: predicted_covariance(block_portion, latitude_offset, longitude_offset, upwind, courant, longitude_diffusion, latitude_diffusion), block_groups)
    return finished_work.reshape(NV, NV)


def reference(covariance, latitude_offset, longitude_offset, upwind, courant, longitude_diffusion, latitude_diffusion):
    def one_level(operands):
        matrix, lat_one, lon_one, up_one, cour_one, flon_one, flat_one = operands
        half_done = apply_rows(matrix, lat_one, lon_one, up_one, cour_one, flon_one, flat_one)
        full_done = apply_rows(half_done.T, lat_one, lon_one, up_one, cour_one, flon_one, flat_one)
        return full_done.T

    return lax.map(one_level, (covariance, latitude_offset, longitude_offset, upwind, courant, longitude_diffusion, latitude_diffusion))
```

```python
import functools

import jax
import jax.numpy as jnp
from jax import lax
from jax.experimental import pallas as pl
from jax.experimental.pallas import tpu as pltpu
from jax.sharding import PartitionSpec as P

NLAT = 64
NLON = 128
HALO = 4
SPAN = 10 * NLON
PAIR = 2 * NLON
CHUNKS = 2


def split(x):
    high = x.astype(jnp.bfloat16)
    low = (x - high.astype(jnp.float32)).astype(jnp.bfloat16)
    return high, low


def dot3(a_high, a_low, b_high, b_low):
    dot = functools.partial(jnp.dot, preferred_element_type=jnp.float32)
    return dot(a_high, b_high) + (dot(a_high, b_low) + dot(a_low, b_high))


def band_kernel(
    place, lat_off, lon_off, upwind, courant, lon_diff, lat_diff,
    right_high, right_low, left_high, left_low,
    depart_lat, depart_lon, near_lat, near_lon, block,
):
    shape = (NLAT, NLON)
    lat = lax.broadcasted_iota(jnp.int32, shape, 0)
    lon = lax.broadcasted_iota(jnp.int32, shape, 1)
    up = upwind[...]
    one = jnp.ones(shape, jnp.int32)
    zero = jnp.zeros(shape, jnp.int32)
    d_lat = jnp.clip(lat + lat_off[...], 0, NLAT - 1)
    d_lon = (lon + lon_off[...]) & (NLON - 1)
    depart_lat[...] = d_lat
    depart_lon[...] = d_lon
    near_lat[...] = jnp.clip(
        d_lat + jnp.where(up == 2, one, zero) - jnp.where(up == 3, one, zero), 0, NLAT - 1
    )
    near_lon[...] = (
        d_lon + jnp.where(up == 0, one, zero) - jnp.where(up == 1, one, zero)
    ) & (NLON - 1)

    sub = lax.broadcasted_iota(jnp.int32, (NLON, NLON), 0)

    def advect_block(y, in_lat):
        row = pl.ds(y, 1)
        w = courant[row, :]
        none = jnp.zeros_like(w)
        keep = jnp.where(depart_lat[row, :] == in_lat, 1.0 - w, none)
        take = jnp.where(near_lat[row, :] == in_lat, w, none)
        empty = jnp.zeros((NLON, NLON), jnp.float32)
        return jnp.where(sub == depart_lon[row, :], keep, empty) + jnp.where(
            sub == near_lon[row, :], take, empty
        )

    def model_block(y, in_lat):
        lx = lon_diff[pl.ds(y, 1), :]
        ly = lat_diff[pl.ds(y, 1), :]
        here = advect_block(y, in_lat)
        north = advect_block(jnp.minimum(y + 1, NLAT - 1), in_lat)
        south = advect_block(jnp.maximum(y - 1, 0), in_lat)
        beside = pltpu.roll(here, 1, 1) + pltpu.roll(here, NLON - 1, 1)
        return here + lx * (beside - 2.0 * here) + ly * (north + south - 2.0 * here)

    def fill(first, pair, transposed, high, low):
        def step(t, carry):
            for half in range(2):
                value = model_block(first + half, first - HALO + t)
                if transposed:
                    value = value.T
                h, l = split(value)
                rows = pl.ds(pl.multiple_of(t * NLON, NLON), NLON)
                cols = pl.ds(half * NLON, NLON)
                if transposed:
                    high[pair, cols, rows] = h
                    low[pair, cols, rows] = l
                else:
                    high[pair, rows, cols] = h
                    low[pair, rows, cols] = l
            return carry

        lax.fori_loop(0, SPAN // NLON, step, 0)

    row_first = place[0]
    col_first = place[1]
    for pair in range(right_high.shape[0]):
        fill(col_first + 2 * pair, pair, False, right_high, right_low)
    for pair in range(left_high.shape[0]):
        fill(row_first + 2 * pair, pair, True, left_high, left_low)


def build_bands(place, fields, row_pairs, col_pairs):
    right = jax.ShapeDtypeStruct((col_pairs, SPAN, PAIR), jnp.bfloat16)
    left = jax.ShapeDtypeStruct((row_pairs, PAIR, SPAN), jnp.bfloat16)
    vmem = pl.BlockSpec(memory_space=pltpu.VMEM)
    grid_i32 = pltpu.VMEM((NLAT, NLON), jnp.int32)
    return pl.pallas_call(
        band_kernel,
        out_shape=(right, right, left, left),
        in_specs=[pl.BlockSpec(memory_space=pltpu.SMEM)] + [vmem] * 6,
        out_specs=(vmem,) * 4,
        scratch_shapes=[grid_i32] * 4 + [pltpu.VMEM((NLON, NLON), jnp.float32)],
        name="bands",
    )(place, *fields)


def cols_kernel(own, west, east, band_high, band_low, out, high, low):
    side = HALO * NLON
    width = own.shape[1]
    for ref, at in ((west, 0), (own, side), (east, side + width)):
        h, l = split(ref[...])
        high[:, at : at + ref.shape[1]] = h
        low[:, at : at + ref.shape[1]] = l
    for pair in range(width // PAIR):
        at = pair * PAIR
        out[:, at : at + PAIR] = dot3(
            high[:, at : at + SPAN], low[:, at : at + SPAN], band_high[pair], band_low[pair]
        )


def apply_cols(own, chunk, rows, west, east, band_high, band_low):
    width = own.shape[1]
    whole = lambda a: pl.BlockSpec(a.shape, lambda i: (0,) * a.ndim)
    ext = pltpu.VMEM((rows, width + 2 * HALO * NLON), jnp.bfloat16)
    return pl.pallas_call(
        cols_kernel,
        grid=(1,),
        out_shape=jax.ShapeDtypeStruct((rows, width), jnp.float32),
        in_specs=[
            pl.BlockSpec((rows, width), lambda i: (chunk, 0)),
            whole(west), whole(east), whole(band_high), whole(band_low),
        ],
        out_specs=pl.BlockSpec((rows, width), lambda i: (0, 0)),
        scratch_shapes=[ext, ext],
        name="cols",
    )(own, west, east, band_high, band_low)


def rows_kernel(*refs):
    parts = refs[:-5]
    band_high, band_low, out, high, low = refs[-5:]
    at = 0
    for ref in parts:
        h, l = split(ref[...])
        high[at : at + ref.shape[0], :] = h
        low[at : at + ref.shape[0], :] = l
        at += ref.shape[0]
    for pair in range(out.shape[0] // PAIR):
        at = pair * PAIR
        out[at : at + PAIR, :] = dot3(
            band_high[pair], band_low[pair], high[at : at + SPAN, :], low[at : at + SPAN, :]
        )


def apply_rows(parts, rows, band_high, band_low, tile=256):
    width = parts[0].shape[1]
    total = sum(p.shape[0] for p in parts)
    ext = pltpu.VMEM((total, tile), jnp.bfloat16)
    whole = lambda a: pl.BlockSpec(a.shape, lambda i: (0,) * a.ndim)
    return pl.pallas_call(
        rows_kernel,
        grid=(width // tile,),
        out_shape=jax.ShapeDtypeStruct((rows, width), jnp.float32),
        in_specs=[pl.BlockSpec((p.shape[0], tile), lambda i: (0, i)) for p in parts]
        + [whole(band_high), whole(band_low)],
        out_specs=pl.BlockSpec((rows, tile), lambda i: (0, i)),
        scratch_shapes=[ext, ext],
        name="rows",
    )(*parts, band_high, band_low)


def body(
    covariance, latitude_offset, longitude_offset, upwind, courant,
    longitude_diffusion, latitude_diffusion,
):
    own = covariance[0]
    rows, width = own.shape
    row_count, col_count = lax.axis_size("row"), lax.axis_size("col")
    side = HALO * NLON
    piece = rows // CHUNKS
    forward = lambda n: [(i, i + 1) for i in range(n - 1)]
    backward = lambda n: [(i + 1, i) for i in range(n - 1)]

    west, east = [], []
    for k in range(CHUNKS):
        part = own[k * piece : (k + 1) * piece]
        west.append(lax.ppermute(part[:, width - side :], "col", forward(col_count)))
        east.append(lax.ppermute(part[:, :side], "col", backward(col_count)))

    place = jnp.stack(
        [
            lax.axis_index("row") * (rows // NLON),
            lax.axis_index("col") * (width // NLON),
        ]
    ).astype(jnp.int32)
    fields = [
        a.reshape(NLAT, NLON)
        for a in (
            latitude_offset, longitude_offset, upwind, courant,
            longitude_diffusion, latitude_diffusion,
        )
    ]
    col_high, col_low, row_high, row_low = build_bands(
        place, fields, rows // PAIR, width // PAIR
    )

    north, half, south = [], [], []
    for k in range(CHUNKS):
        piece_half = apply_cols(own, k, piece, west[k], east[k], col_high, col_low)
        half.append(piece_half)
        north.append(lax.ppermute(piece_half, "row", forward(row_count)))
        south.append(lax.ppermute(piece_half, "row", backward(row_count)))
    return apply_rows(north + half + south, rows, row_high, row_low)[None]


def solution(mesh):
    in_specs = (P(None, "row", "col"), P(), P(), P(), P(), P(), P())
    out_specs = P(None, "row", "col")
    return jax.shard_map(body, mesh=mesh, in_specs=in_specs, out_specs=out_specs, check_vma=False)
```

```python
import functools

import jax
import jax.numpy as jnp
from jax import lax
from jax.experimental import pallas as pl
from jax.experimental.pallas import tpu as pltpu
from jax.sharding import PartitionSpec as P


NLAT = 64
NLON = 128
HALO = 4
SPAN = 10 * NLON
PAIR = 2 * NLON


def split(x):
    high = x.astype(jnp.bfloat16)
    low = (x - high.astype(jnp.float32)).astype(jnp.bfloat16)
    return high, low


def dot3(a_high, a_low, b_high, b_low):
    dot = functools.partial(jnp.dot, preferred_element_type=jnp.float32)
    return dot(a_high, b_high) + (dot(a_high, b_low) + dot(a_low, b_high))


def band_kernel(
    transposed, place, lat_off, lon_off, upwind, courant, lon_diff, lat_diff,
    high, low, depart_lat, depart_lon, near_lat, near_lon,
):
    shape = (NLAT, NLON)
    lat = lax.broadcasted_iota(jnp.int32, shape, 0)
    lon = lax.broadcasted_iota(jnp.int32, shape, 1)
    up = upwind[...]
    one = jnp.ones(shape, jnp.int32)
    zero = jnp.zeros(shape, jnp.int32)
    d_lat = jnp.clip(lat + lat_off[...], 0, NLAT - 1)
    d_lon = (lon + lon_off[...]) & (NLON - 1)
    depart_lat[...] = d_lat
    depart_lon[...] = d_lon
    near_lat[...] = jnp.clip(
        d_lat + jnp.where(up == 2, one, zero) - jnp.where(up == 3, one, zero), 0, NLAT - 1
    )
    near_lon[...] = (
        d_lon + jnp.where(up == 0, one, zero) - jnp.where(up == 1, one, zero)
    ) & (NLON - 1)

    sub = lax.broadcasted_iota(jnp.int32, (NLON, NLON), 0)

    def advect_block(y, in_lat):
        row = pl.ds(y, 1)
        w = courant[row, :]
        none = jnp.zeros_like(w)
        keep = jnp.where(depart_lat[row, :] == in_lat, 1.0 - w, none)
        take = jnp.where(near_lat[row, :] == in_lat, w, none)
        empty = jnp.zeros((NLON, NLON), jnp.float32)
        return jnp.where(sub == depart_lon[row, :], keep, empty) + jnp.where(
            sub == near_lon[row, :], take, empty
        )

    def model_block(y, in_lat):
        lx = lon_diff[pl.ds(y, 1), :]
        ly = lat_diff[pl.ds(y, 1), :]
        here = advect_block(y, in_lat)
        north = advect_block(jnp.minimum(y + 1, NLAT - 1), in_lat)
        south = advect_block(jnp.maximum(y - 1, 0), in_lat)
        beside = pltpu.roll(here, 1, 1) + pltpu.roll(here, NLON - 1, 1)
        return here + lx * (beside - 2.0 * here) + ly * (north + south - 2.0 * here)

    first = place[0]
    for pair in range(high.shape[0]):

        def step(t, carry, pair=pair):
            for half in range(2):
                y = first + 2 * pair + half
                value = model_block(y, first + 2 * pair - HALO + t)
                if transposed:
                    value = value.T
                h, l = split(value)
                rows = pl.ds(pl.multiple_of(t * NLON, NLON), NLON)
                cols = pl.ds(half * NLON, NLON)
                at = (pair, cols, rows) if transposed else (pair, rows, cols)
                high[at] = h
                low[at] = l
            return carry

        lax.fori_loop(0, SPAN // NLON, step, 0)


VMEM_SPEC = pl.BlockSpec(memory_space=pltpu.VMEM)


def held(x):
    return pltpu.with_memory_space_constraint(x, pltpu.VMEM)


def build_bands(place, fields, pairs, transposed):
    shape = (pairs, PAIR, SPAN) if transposed else (pairs, SPAN, PAIR)
    band = pltpu.VMEM(shape, jnp.bfloat16)
    return pl.pallas_call(
        functools.partial(band_kernel, transposed),
        out_shape=(band, band),
        in_specs=[pl.BlockSpec(memory_space=pltpu.SMEM)] + [VMEM_SPEC] * 6,
        out_specs=(VMEM_SPEC,) * 2,
        scratch_shapes=[pltpu.VMEM((NLAT, NLON), jnp.int32)] * 4,
        compiler_params=pltpu.CompilerParams(vmem_limit_bytes=24 << 20),
        name="row_bands" if transposed else "col_bands",
    )(place, *fields)


def rows_kernel(north, own, south, band_high, band_low, left, right, high, low):
    at = 0
    for ref in (north, own, south):
        h, l = split(ref[...])
        high[at : at + ref.shape[0], :] = h
        low[at : at + ref.shape[0], :] = l
        at += ref.shape[0]
    width = left.shape[1]
    for pair in range(left.shape[0] // PAIR):
        at = pair * PAIR
        value = dot3(
            band_high[pair], band_low[pair], high[at : at + SPAN, :], low[at : at + SPAN, :]
        )
        left[at : at + PAIR, :] = value[:, :width]
        right[at : at + PAIR, :] = value[:, width:]


def apply_rows(north, own, south, bands):
    rows, width = own.shape
    ext = pltpu.VMEM((3 * rows, width), jnp.bfloat16)
    half = pltpu.VMEM((rows, width // 2), jnp.float32)
    args = [held(a) for a in (north, own, south, *bands)]
    return pl.pallas_call(
        rows_kernel,
        out_shape=(half, half),
        in_specs=[VMEM_SPEC] * 5,
        out_specs=(VMEM_SPEC,) * 2,
        scratch_shapes=[ext, ext],
        compiler_params=pltpu.CompilerParams(vmem_limit_bytes=16 << 20),
        name="rows",
    )(*args)


def cols_kernel(*refs):
    parts = refs[:-5]
    band_high, band_low, out, high, low = refs[-5:]
    at = 0
    for ref in parts:
        h, l = split(ref[...])
        high[:, at : at + ref.shape[1]] = h
        low[:, at : at + ref.shape[1]] = l
        at += ref.shape[1]
    for pair in range(out.shape[1] // PAIR):
        begin = (pair - 1) * PAIR
        skip = max(0, -begin)
        stop = min(at, begin + SPAN)
        ext = slice(begin + skip, stop)
        band = slice(skip, stop - begin)
        out[:, pair * PAIR : (pair + 1) * PAIR] = dot3(
            high[:, ext], low[:, ext], band_high[pair, band], band_low[pair, band]
        )


def apply_cols(parts, bands, width):
    rows = parts[0].shape[0]
    ext = pltpu.VMEM((rows, sum(p.shape[1] for p in parts)), jnp.bfloat16)
    args = [held(a) for a in (*parts, *bands)]
    return pl.pallas_call(
        cols_kernel,
        out_shape=jax.ShapeDtypeStruct((rows, width), jnp.float32),
        in_specs=[VMEM_SPEC] * len(args),
        out_specs=VMEM_SPEC,
        scratch_shapes=[ext, ext],
        compiler_params=pltpu.CompilerParams(vmem_limit_bytes=32 << 20),
        name="cols",
    )(*args)


def tail_kernel(west, east, band_high, band_low, part, out):
    last = band_high.shape[0] - 1

    def add(ref, pair, rows):
        h, l = split(ref[...])
        out[...] = part[...] + dot3(h, l, band_high[pair, rows], band_low[pair, rows])

    @pl.when(pl.program_id(0) == 0)
    def _():
        add(west, 0, slice(0, west.shape[1]))

    @pl.when(pl.program_id(0) == 1)
    def _():
        add(east, last, slice(SPAN - east.shape[1], SPAN))


def apply_tail(west, east, bands, part):
    rows, width = part.shape
    block = pl.BlockSpec((rows, PAIR), lambda i: (0, i * (width // PAIR - 1)))
    args = [held(a) for a in (west, east, *bands)]
    return pl.pallas_call(
        tail_kernel,
        grid=(2,),
        out_shape=jax.ShapeDtypeStruct((rows, width), jnp.float32),
        in_specs=[VMEM_SPEC] * 4 + [block],
        out_specs=block,
        input_output_aliases={4: 0},
        compiler_params=pltpu.CompilerParams(vmem_limit_bytes=16 << 20),
        name="tail",
    )(*args, part)


def body(
    covariance, latitude_offset, longitude_offset, upwind, courant,
    longitude_diffusion, latitude_diffusion,
):
    own = covariance[0]
    rows, width = own.shape
    row_count, col_count = lax.axis_size("row"), lax.axis_size("col")
    forward = lambda n: [(i, i + 1) for i in range(n - 1)]
    backward = lambda n: [(i + 1, i) for i in range(n - 1)]

    def columns(first, stop):
        west = own[:, first * NLON : stop * NLON]
        east = own[:, width - stop * NLON : width - first * NLON]
        return jnp.concatenate([west, east], axis=1)

    def from_rows(x):
        return (
            lax.ppermute(x, "row", forward(row_count)),
            lax.ppermute(x, "row", backward(row_count)),
        )

    def from_cols(left, right):
        return (
            lax.ppermute(right, "col", forward(col_count)),
            lax.ppermute(left, "col", backward(col_count)),
        )

    fields = [
        a.reshape(NLAT, NLON)
        for a in (
            latitude_offset, longitude_offset, upwind, courant,
            longitude_diffusion, latitude_diffusion,
        )
    ]
    lat_row = (lax.axis_index("row") * (rows // NLON)).astype(jnp.int32).reshape(1)
    lat_col = (lax.axis_index("col") * (width // NLON)).astype(jnp.int32).reshape(1)

    own0, own1, own2 = columns(0, 1), columns(1, 2), columns(2, 4)
    north0, south0 = from_rows(own0)
    row_bands = build_bands(lat_row, fields, rows // PAIR, True)
    north1, south1 = from_rows(own1)
    left0, right0 = apply_rows(north0, own0, south0, row_bands)
    west0, east0 = from_cols(left0, right0)
    north2, south2 = from_rows(own2)
    left1, right1 = apply_rows(north1, own1, south1, row_bands)
    west1, east1 = from_cols(left1, right1)
    col_bands = build_bands(lat_col, fields, width // PAIR, False)
    left2, right2 = apply_rows(north2, own2, south2, row_bands)
    west2, east2 = from_cols(left2, right2)
    parts = [west1, west0, left0, left1, left2, right2, right1, right0, east0, east1]
    part = apply_cols(parts, col_bands, width)
    return apply_tail(west2, east2, col_bands, part)[None]


def solution(mesh):
    in_specs = (P(None, "row", "col"), P(), P(), P(), P(), P(), P())
    out_specs = P(None, "row", "col")
    return jax.shard_map(
        body, mesh=mesh, in_specs=in_specs, out_specs=out_specs, check_vma=False
    )
```

```python
import functools

import jax
import jax.numpy as jnp
from jax import lax
from jax.experimental import pallas as pl
from jax.experimental.pallas import tpu as pltpu
from jax.sharding import PartitionSpec as P


NLAT = 64
NLON = 128
HALO = 4
SPAN = 10 * NLON
PAIR = 2 * NLON


def split(x):
    high = x.astype(jnp.bfloat16)
    low = (x - high.astype(jnp.float32)).astype(jnp.bfloat16)
    return high, low


def dot3(a_high, a_low, b_high, b_low):
    dot = functools.partial(jnp.dot, preferred_element_type=jnp.float32)
    return dot(a_high, b_high) + (dot(a_high, b_low) + dot(a_low, b_high))


def band_kernel(
    transposed, place, lat_off, lon_off, upwind, courant, lon_diff, lat_diff,
    high, low, depart_lat, depart_lon, near_lat, near_lon,
):
    shape = (NLAT, NLON)
    lat = lax.broadcasted_iota(jnp.int32, shape, 0)
    lon = lax.broadcasted_iota(jnp.int32, shape, 1)
    up = upwind[...]
    one = jnp.ones(shape, jnp.int32)
    zero = jnp.zeros(shape, jnp.int32)
    d_lat = jnp.clip(lat + lat_off[...], 0, NLAT - 1)
    d_lon = (lon + lon_off[...]) & (NLON - 1)
    depart_lat[...] = d_lat
    depart_lon[...] = d_lon
    near_lat[...] = jnp.clip(
        d_lat + jnp.where(up == 2, one, zero) - jnp.where(up == 3, one, zero), 0, NLAT - 1
    )
    near_lon[...] = (
        d_lon + jnp.where(up == 0, one, zero) - jnp.where(up == 1, one, zero)
    ) & (NLON - 1)

    sub = lax.broadcasted_iota(jnp.int32, (NLON, NLON), 0)

    def advect_block(y, in_lat):
        row = pl.ds(y, 1)
        w = courant[row, :]
        none = jnp.zeros_like(w)
        keep = jnp.where(depart_lat[row, :] == in_lat, 1.0 - w, none)
        take = jnp.where(near_lat[row, :] == in_lat, w, none)
        empty = jnp.zeros((NLON, NLON), jnp.float32)
        return jnp.where(sub == depart_lon[row, :], keep, empty) + jnp.where(
            sub == near_lon[row, :], take, empty
        )

    def model_block(y, in_lat):
        lx = lon_diff[pl.ds(y, 1), :]
        ly = lat_diff[pl.ds(y, 1), :]
        here = advect_block(y, in_lat)
        north = advect_block(jnp.minimum(y + 1, NLAT - 1), in_lat)
        south = advect_block(jnp.maximum(y - 1, 0), in_lat)
        beside = pltpu.roll(here, 1, 1) + pltpu.roll(here, NLON - 1, 1)
        return here + lx * (beside - 2.0 * here) + ly * (north + south - 2.0 * here)

    first = place[0]
    for pair in range(high.shape[0]):

        def step(t, carry, pair=pair):
            for half in range(2):
                y = first + 2 * pair + half
                value = model_block(y, first + 2 * pair - HALO + t)
                if transposed:
                    value = value.T
                h, l = split(value)
                rows = pl.ds(pl.multiple_of(t * NLON, NLON), NLON)
                cols = pl.ds(half * NLON, NLON)
                at = (pair, cols, rows) if transposed else (pair, rows, cols)
                high[at] = h
                low[at] = l
            return carry

        lax.fori_loop(0, SPAN // NLON, step, 0)


VMEM_SPEC = pl.BlockSpec(memory_space=pltpu.VMEM)


def held(x):
    return pltpu.with_memory_space_constraint(x, pltpu.VMEM)


def build_bands(place, fields, pairs, transposed):
    shape = (pairs, PAIR, SPAN) if transposed else (pairs, SPAN, PAIR)
    band = pltpu.VMEM(shape, jnp.bfloat16)
    return pl.pallas_call(
        functools.partial(band_kernel, transposed),
        out_shape=(band, band),
        in_specs=[pl.BlockSpec(memory_space=pltpu.SMEM)] + [VMEM_SPEC] * 6,
        out_specs=(VMEM_SPEC,) * 2,
        scratch_shapes=[pltpu.VMEM((NLAT, NLON), jnp.int32)] * 4,
        compiler_params=pltpu.CompilerParams(vmem_limit_bytes=24 << 20),
        name="row_bands" if transposed else "col_bands",
    )(place, *fields)


def take_kernel(starts, source, *refs):
    outs, sems = refs[:-1], refs[-1]
    copies = [
        pltpu.make_async_copy(source.at[:, pl.ds(at, out.shape[1])], out, sems.at[i])
        for i, (at, out) in enumerate(zip(starts, outs))
    ]
    for copy in copies:
        copy.start()
    for copy in copies:
        copy.wait()


def take_columns(source, starts, width):
    out = pltpu.VMEM((source.shape[0], width), jnp.float32)
    return pl.pallas_call(
        functools.partial(take_kernel, starts),
        out_shape=(out,) * len(starts),
        in_specs=[pl.BlockSpec(memory_space=pltpu.HBM)],
        out_specs=(VMEM_SPEC,) * len(starts),
        scratch_shapes=[pltpu.SemaphoreType.DMA((len(starts),))],
        compiler_params=pltpu.CompilerParams(vmem_limit_bytes=8 << 20),
        name="take",
    )(pltpu.with_memory_space_constraint(source, pltpu.HBM))


def rows_kernel(place, chip, own, cross, band_high, band_low, out, high, low):
    rows = own.shape[0]
    odd = (place[0] // HALO) & 1
    to_chip = pl.multiple_of((1 - odd) * 2 * rows, rows)
    to_cross = pl.multiple_of(odd * 2 * rows, rows)
    for ref, at in ((own, rows), (chip, to_chip), (cross, to_cross)):
        h, l = split(ref[...])
        high[pl.ds(at, rows), :] = h
        low[pl.ds(at, rows), :] = l
    for pair in range(rows // PAIR):
        at = pair * PAIR
        out[at : at + PAIR, :] = dot3(
            band_high[pair], band_low[pair], high[at : at + SPAN, :], low[at : at + SPAN, :]
        )


def apply_rows(place, chip, own, cross, bands):
    rows, width = own.shape
    ext = pltpu.VMEM((3 * rows, width), jnp.bfloat16)
    args = [held(a) for a in (chip, own, cross, *bands)]
    return pl.pallas_call(
        rows_kernel,
        out_shape=pltpu.VMEM((rows, width), jnp.float32),
        in_specs=[pl.BlockSpec(memory_space=pltpu.SMEM)] + [VMEM_SPEC] * 5,
        out_specs=VMEM_SPEC,
        scratch_shapes=[ext, ext],
        compiler_params=pltpu.CompilerParams(vmem_limit_bytes=16 << 20),
        name="rows",
    )(place, *args)


def cols_kernel(*refs):
    parts = refs[:-5]
    band_high, band_low, out, high, low = refs[-5:]
    at = 0
    for ref in parts:
        h, l = split(ref[...])
        high[:, at : at + ref.shape[1]] = h
        low[:, at : at + ref.shape[1]] = l
        at += ref.shape[1]
    for pair in range(out.shape[1] // PAIR):
        begin = (pair - 1) * PAIR
        skip = max(0, -begin)
        stop = min(at, begin + SPAN)
        ext = slice(begin + skip, stop)
        band = slice(skip, stop - begin)
        out[:, pair * PAIR : (pair + 1) * PAIR] = dot3(
            high[:, ext], low[:, ext], band_high[pair, band], band_low[pair, band]
        )


def apply_cols(parts, bands, width):
    rows = parts[0].shape[0]
    ext = pltpu.VMEM((rows, sum(p.shape[1] for p in parts)), jnp.bfloat16)
    args = [held(a) for a in (*parts, *bands)]
    return pl.pallas_call(
        cols_kernel,
        out_shape=jax.ShapeDtypeStruct((rows, width), jnp.float32),
        in_specs=[VMEM_SPEC] * len(args),
        out_specs=VMEM_SPEC,
        scratch_shapes=[ext, ext],
        compiler_params=pltpu.CompilerParams(vmem_limit_bytes=32 << 20),
        name="cols",
    )(*args)


def tail_kernel(west, band_high, band_low, part, out):
    h, l = split(west[...])
    band = slice(0, west.shape[1])
    out[...] = part[...] + dot3(h, l, band_high[0, band], band_low[0, band])


def apply_tail(west, bands, part):
    rows, width = part.shape
    block = pl.BlockSpec((rows, PAIR), lambda i: (0, 0))
    args = [held(a) for a in (west, *bands)]
    return pl.pallas_call(
        tail_kernel,
        grid=(1,),
        out_shape=jax.ShapeDtypeStruct((rows, width), jnp.float32),
        in_specs=[VMEM_SPEC] * 3 + [block],
        out_specs=block,
        input_output_aliases={3: 0},
        compiler_params=pltpu.CompilerParams(vmem_limit_bytes=16 << 20),
        name="tail",
    )(*args, part)


def body(
    covariance, latitude_offset, longitude_offset, upwind, courant,
    longitude_diffusion, latitude_diffusion,
):
    block = covariance[0]
    rows, width = block.shape
    row_count, col_count = lax.axis_size("row"), lax.axis_size("col")
    forward = lambda n: [(i, i + 1) for i in range(n - 1)]
    backward = lambda n: [(i + 1, i) for i in range(n - 1)]

    def from_rows(x):
        chip = [(i, i ^ 1) for i in range(row_count)]
        cross = [((i + 1 ^ 1) - 1, i) for i in range(1, row_count - 1)]
        return lax.ppermute(x, "row", chip), lax.ppermute(x, "row", cross)

    fields = [
        a.reshape(NLAT, NLON)
        for a in (
            latitude_offset, longitude_offset, upwind, courant,
            longitude_diffusion, latitude_diffusion,
        )
    ]
    lat_row = (lax.axis_index("row") * (rows // NLON)).astype(jnp.int32).reshape(1)
    lat_col = (lax.axis_index("col") * (width // NLON)).astype(jnp.int32).reshape(1)

    starts = (0, width - PAIR, PAIR, width - 2 * PAIR)
    own = list(take_columns(block, starts[:1], PAIR))
    near = [from_rows(own[0])]
    row_bands = build_bands(lat_row, fields, rows // PAIR, True)
    own += take_columns(block, starts[1:], PAIR)
    near += [from_rows(own[k]) for k in range(1, 4)]
    half, side = [], []
    for k in range(4):
        chip, cross = near[k]
        half.append(apply_rows(lat_row, chip, own[k], cross, row_bands))
        pairs = forward(col_count) if k % 2 else backward(col_count)
        side.append(lax.ppermute(half[k], "col", pairs))
    col_bands = build_bands(lat_col, fields, width // PAIR, False)
    parts = [side[1], half[0], half[2], half[3], half[1], side[0], side[2]]
    part = apply_cols(parts, col_bands, width)
    return apply_tail(side[3], col_bands, part)[None]


def solution(mesh):
    in_specs = (P(None, "row", "col"), P(), P(), P(), P(), P(), P())
    out_specs = P(None, "row", "col")
    return jax.shard_map(body, mesh=mesh, in_specs=in_specs, out_specs=out_specs, check_vma=False)
```

```python
import functools

import jax
import jax.numpy as jnp
from jax import lax
from jax.experimental import pallas as pl
from jax.experimental.pallas import tpu as pltpu
from jax.sharding import PartitionSpec as P


NLAT = 64
NLON = 128
HALO = 4
SPAN = 10 * NLON
PAIR = 2 * NLON


def split(x):
    high = x.astype(jnp.bfloat16)
    low = (x - high.astype(jnp.float32)).astype(jnp.bfloat16)
    return high, low


def dot3(a_high, a_low, b_high, b_low):
    dot = functools.partial(jnp.dot, preferred_element_type=jnp.float32)
    return dot(a_high, b_high) + (dot(a_high, b_low) + dot(a_low, b_high))


def band_kernel(
    transposed, place, lat_off, lon_off, upwind, courant, lon_diff, lat_diff,
    high, low, depart_lat, depart_lon, near_lat, near_lon, hot,
):
    shape = (NLAT, NLON)
    lat = lax.broadcasted_iota(jnp.int32, shape, 0)
    lon = lax.broadcasted_iota(jnp.int32, shape, 1)
    up = upwind[...]
    one = jnp.ones(shape, jnp.int32)
    zero = jnp.zeros(shape, jnp.int32)
    d_lat = jnp.clip(lat + lat_off[...], 0, NLAT - 1)
    d_lon = (lon + lon_off[...]) & (NLON - 1)
    depart_lat[...] = d_lat
    depart_lon[...] = d_lon
    near_lat[...] = jnp.clip(
        d_lat + jnp.where(up == 2, one, zero) - jnp.where(up == 3, one, zero), 0, NLAT - 1
    )
    near_lon[...] = (
        d_lon + jnp.where(up == 0, one, zero) - jnp.where(up == 1, one, zero)
    ) & (NLON - 1)

    sub = lax.broadcasted_iota(jnp.int32, (NLON, NLON), 0)
    first = place[0]
    pairs = high.shape[0]

    def put(pair, half, t, value):
        if transposed:
            value = value.T
        h, l = split(value)
        cells = pl.ds(t * NLON, NLON)
        cols = pl.ds(half * NLON, NLON)
        at = (pair, cols, cells) if transposed else (pair, cells, cols)
        high[at] = h
        low[at] = l

    def fill(pair, half):
        y = first + 2 * pair + half
        lx = lon_diff[pl.ds(y, 1), :]
        ly = lat_diff[pl.ds(y, 1), :]
        core = 1.0 - 2.0 * lx - 2.0 * ly
        none = jnp.zeros_like(lx)
        reach = ((0, 0), (0, 1), (-1, 0))
        rows = (y, jnp.minimum(y + 1, NLAT - 1), jnp.maximum(y - 1, 0))
        rows = [pl.ds(r, 1) for r in rows]
        for k, row in enumerate(rows):
            on = jnp.ones((NLON, NLON), jnp.float32)
            off = jnp.zeros((NLON, NLON), jnp.float32)
            hot[2 * k] = jnp.where(sub == depart_lon[row, :], on, off)
            hot[2 * k + 1] = jnp.where(sub == near_lon[row, :], on, off)
        for t in range(2 * HALO + 1):
            far = t - HALO
            in_lat = y + far
            value = None
            for k, row in enumerate(rows):
                w = courant[row, :]
                below, above = reach[k]
                scale = ly if k else jnp.ones_like(lx)
                terms = []
                if -2 + below <= far <= 2 + above:
                    keep = jnp.where(depart_lat[row, :] == in_lat, scale * (1.0 - w), none)
                    terms.append(keep * hot[2 * k])
                if -3 + below <= far <= 3 + above:
                    take = jnp.where(near_lat[row, :] == in_lat, scale * w, none)
                    terms.append(take * hot[2 * k + 1])
                if not terms:
                    continue
                total = sum(terms[1:], terms[0])
                if k == 0:
                    beside = pltpu.roll(total, 1, 1) + pltpu.roll(total, NLON - 1, 1)
                    total = core * total + lx * beside
                value = total if value is None else value + total
            put(pair, half, t + half, value)
        put(pair, half, 0 if half else 2 * HALO + 1, jnp.zeros((NLON, NLON), jnp.float32))

    def step(pair, carry):
        fill(pair, 0)
        fill(pair, 1)
        return carry

    lax.fori_loop(0, pairs, step, 0)


VMEM_SPEC = pl.BlockSpec(memory_space=pltpu.VMEM)


def held(x):
    return pltpu.with_memory_space_constraint(x, pltpu.VMEM)


def build_bands(place, fields, pairs, transposed):
    shape = (pairs, PAIR, SPAN) if transposed else (pairs, SPAN, PAIR)
    band = pltpu.VMEM(shape, jnp.bfloat16)
    return pl.pallas_call(
        functools.partial(band_kernel, transposed),
        out_shape=(band, band),
        in_specs=[pl.BlockSpec(memory_space=pltpu.SMEM)] + [VMEM_SPEC] * 6,
        out_specs=(VMEM_SPEC,) * 2,
        scratch_shapes=[pltpu.VMEM((NLAT, NLON), jnp.int32)] * 4
        + [pltpu.VMEM((6, NLON, NLON), jnp.float32)],
        compiler_params=pltpu.CompilerParams(vmem_limit_bytes=24 << 20),
        name="row_bands" if transposed else "col_bands",
    )(place, *fields)


def take_kernel(starts, source, *refs):
    outs, sems = refs[:-1], refs[-1]
    copies = [
        pltpu.make_async_copy(source.at[:, pl.ds(at, out.shape[1])], out, sems.at[i])
        for i, (at, out) in enumerate(zip(starts, outs))
    ]
    for copy in copies:
        copy.start()
    for copy in copies:
        copy.wait()


def take_columns(source, starts, width):
    out = pltpu.VMEM((source.shape[0], width), jnp.float32)
    return pl.pallas_call(
        functools.partial(take_kernel, starts),
        out_shape=(out,) * len(starts),
        in_specs=[pl.BlockSpec(memory_space=pltpu.HBM)],
        out_specs=(VMEM_SPEC,) * len(starts),
        scratch_shapes=[pltpu.SemaphoreType.DMA((len(starts),))],
        compiler_params=pltpu.CompilerParams(vmem_limit_bytes=8 << 20),
        name="take",
    )(pltpu.with_memory_space_constraint(source, pltpu.HBM))


def rows_kernel(place, chip, own, *refs):
    *cross, band_high, band_low, out, high, low = refs
    rows = own.shape[0]
    odd = (place[0] // HALO) & 1
    to_chip = pl.multiple_of((1 - odd) * 2 * rows, rows)
    to_cross = pl.multiple_of(odd * 2 * rows, rows)
    for parts, at in (((own,), rows), ((chip,), to_chip), (cross, to_cross)):
        h, l = split(sum((ref[...] for ref in parts[1:]), parts[0][...]))
        high[pl.ds(at, rows), :] = h
        low[pl.ds(at, rows), :] = l
    for pair in range(rows // PAIR):
        at = pair * PAIR
        out[at : at + PAIR, :] = dot3(
            band_high[pair], band_low[pair], high[at : at + SPAN, :], low[at : at + SPAN, :]
        )


def apply_rows(place, chip, own, cross, bands):
    rows, width = own.shape
    ext = pltpu.VMEM((3 * rows, width), jnp.bfloat16)
    args = [held(a) for a in (chip, own, *cross, *bands)]
    return pl.pallas_call(
        rows_kernel,
        out_shape=pltpu.VMEM((rows, width), jnp.float32),
        in_specs=[pl.BlockSpec(memory_space=pltpu.SMEM)] + [VMEM_SPEC] * len(args),
        out_specs=VMEM_SPEC,
        scratch_shapes=[ext, ext],
        compiler_params=pltpu.CompilerParams(vmem_limit_bytes=16 << 20),
        name="rows",
    )(place, *args)


def cols_kernel(*refs):
    parts = refs[:-5]
    band_high, band_low, out, high, low = refs[-5:]
    at = 0
    for ref in parts:
        h, l = split(ref[...])
        high[:, at : at + ref.shape[1]] = h
        low[:, at : at + ref.shape[1]] = l
        at += ref.shape[1]
    for pair in range(out.shape[1] // PAIR):
        begin = (pair - 1) * PAIR
        skip = max(0, -begin)
        stop = min(at, begin + SPAN)
        ext = slice(begin + skip, stop)
        band = slice(skip, stop - begin)
        out[:, pair * PAIR : (pair + 1) * PAIR] = dot3(
            high[:, ext], low[:, ext], band_high[pair, band], band_low[pair, band]
        )


def apply_cols(parts, bands, width):
    rows = parts[0].shape[0]
    ext = pltpu.VMEM((rows, sum(p.shape[1] for p in parts)), jnp.bfloat16)
    args = [held(a) for a in (*parts, *bands)]
    return pl.pallas_call(
        cols_kernel,
        out_shape=jax.ShapeDtypeStruct((rows, width), jnp.float32),
        in_specs=[VMEM_SPEC] * len(args),
        out_specs=VMEM_SPEC,
        scratch_shapes=[ext, ext],
        compiler_params=pltpu.CompilerParams(vmem_limit_bytes=32 << 20),
        name="cols",
    )(*args)


def tail_kernel(west, band_high, band_low, part, out):
    h, l = split(west[...])
    band = slice(0, west.shape[1])
    out[...] = part[...] + dot3(h, l, band_high[0, band], band_low[0, band])


def apply_tail(west, bands, part):
    rows, width = part.shape
    block = pl.BlockSpec((rows, PAIR), lambda i: (0, 0))
    args = [held(a) for a in (west, *bands)]
    return pl.pallas_call(
        tail_kernel,
        grid=(1,),
        out_shape=jax.ShapeDtypeStruct((rows, width), jnp.float32),
        in_specs=[VMEM_SPEC] * 3 + [block],
        out_specs=block,
        input_output_aliases={3: 0},
        compiler_params=pltpu.CompilerParams(vmem_limit_bytes=16 << 20),
        name="tail",
    )(*args, part)


def body(
    covariance, latitude_offset, longitude_offset, upwind, courant,
    longitude_diffusion, latitude_diffusion,
):
    block = covariance[0]
    rows, width = block.shape
    row_count, col_count = lax.axis_size("row"), lax.axis_size("col")
    forward = lambda n: [(i, i + 1) for i in range(n - 1)]
    backward = lambda n: [(i + 1, i) for i in range(n - 1)]

    def shift(x, axis, pairs):
        return lax.ppermute(x, axis, pairs)

    last = row_count - 1
    middle = row_count // 2
    chip_pairs = [(i, i ^ 1) for i in range(row_count)]
    cross_pairs = [((i + 1 ^ 1) - 1, i) for i in range(1, last)]
    middle_pairs = [(middle - 1, middle), (middle, middle - 1)]

    def from_rows(k, x):
        chip = shift(x, "row", chip_pairs)
        if k < 3:
            return chip, [shift(x, "row", cross_pairs)]
        ways = [pair for pair in cross_pairs if pair not in middle_pairs]
        cross = shift(x, "row", ways + [(middle - 1, 0), (middle, last)])
        return chip, [cross, shift(cross, "row", [(0, middle), (last, middle - 1)])]

    fields = [
        a.reshape(NLAT, NLON)
        for a in (
            latitude_offset, longitude_offset, upwind, courant,
            longitude_diffusion, latitude_diffusion,
        )
    ]
    lat_row = (lax.axis_index("row") * (rows // NLON)).astype(jnp.int32).reshape(1)
    lat_col = (lax.axis_index("col") * (width // NLON)).astype(jnp.int32).reshape(1)

    starts = (0, width - PAIR, PAIR, width - 2 * PAIR)
    own = list(take_columns(block, starts[:2], PAIR))
    own += take_columns(block, starts[2:], PAIR)
    near = [from_rows(k, own[k]) for k in range(4)]
    row_bands = build_bands(lat_row, fields, rows // PAIR, True)
    half, side = [], []
    for k in range(4):
        chip, cross = near[k]
        half.append(apply_rows(lat_row, chip, own[k], cross, row_bands))
        pairs = forward(col_count) if k % 2 else backward(col_count)
        side.append(shift(half[k], "col", pairs))
    col_bands = build_bands(lat_col, fields, width // PAIR, False)
    parts = [side[1], half[0], half[2], half[3], half[1], side[0], side[2]]
    part = apply_cols(parts, col_bands, width)
    return apply_tail(side[3], col_bands, part)[None]


def solution(mesh):
    in_specs = (P(None, "row", "col"), P(), P(), P(), P(), P(), P())
    out_specs = P(None, "row", "col")
    return jax.shard_map(body, mesh=mesh, in_specs=in_specs, out_specs=out_specs, check_vma=False)
```

```python
import functools

import jax
import jax.numpy as jnp
from jax import lax
from jax.experimental import pallas as pl
from jax.experimental.pallas import tpu as pltpu
from jax.sharding import PartitionSpec as P


NLAT = 64
NLON = 128
HALO = 4
SPAN = 10 * NLON
PAIR = 2 * NLON


def split(x):
    high = x.astype(jnp.bfloat16)
    low = (x - high.astype(jnp.float32)).astype(jnp.bfloat16)
    return high, low


def dot3(a_high, a_low, b_high, b_low):
    dot = functools.partial(jnp.dot, preferred_element_type=jnp.float32)
    return dot(a_high, b_high) + (dot(a_high, b_low) + dot(a_low, b_high))


def band_kernel(
    transposed, place, lat_off, lon_off, upwind, courant, lon_diff, lat_diff,
    high, low, depart_lat, depart_lon, near_lat, near_lon, hot,
):
    shape = (NLAT, NLON)
    lat = lax.broadcasted_iota(jnp.int32, shape, 0)
    lon = lax.broadcasted_iota(jnp.int32, shape, 1)
    up = upwind[...]
    one = jnp.ones(shape, jnp.int32)
    zero = jnp.zeros(shape, jnp.int32)
    d_lat = jnp.clip(lat + lat_off[...], 0, NLAT - 1)
    d_lon = (lon + lon_off[...]) & (NLON - 1)
    depart_lat[...] = d_lat
    depart_lon[...] = d_lon
    near_lat[...] = jnp.clip(
        d_lat + jnp.where(up == 2, one, zero) - jnp.where(up == 3, one, zero), 0, NLAT - 1
    )
    near_lon[...] = (
        d_lon + jnp.where(up == 0, one, zero) - jnp.where(up == 1, one, zero)
    ) & (NLON - 1)

    sub = lax.broadcasted_iota(jnp.int32, (NLON, NLON), 0)
    first = place[0]
    pairs = high.shape[0]

    def put(pair, half, t, value):
        if transposed:
            value = value.T
        h, l = split(value)
        cells = pl.ds(t * NLON, NLON)
        cols = pl.ds(half * NLON, NLON)
        at = (pair, cols, cells) if transposed else (pair, cells, cols)
        high[at] = h
        low[at] = l

    def fill(pair, half):
        y = first + 2 * pair + half
        lx = lon_diff[pl.ds(y, 1), :]
        ly = lat_diff[pl.ds(y, 1), :]
        core = 1.0 - 2.0 * lx - 2.0 * ly
        none = jnp.zeros_like(lx)
        reach = ((0, 0), (0, 1), (-1, 0))
        rows = (y, jnp.minimum(y + 1, NLAT - 1), jnp.maximum(y - 1, 0))
        rows = [pl.ds(r, 1) for r in rows]
        for k, row in enumerate(rows):
            on = jnp.ones((NLON, NLON), jnp.float32)
            off = jnp.zeros((NLON, NLON), jnp.float32)
            hot[2 * k] = jnp.where(sub == depart_lon[row, :], on, off)
            hot[2 * k + 1] = jnp.where(sub == near_lon[row, :], on, off)
        for t in range(2 * HALO + 1):
            far = t - HALO
            in_lat = y + far
            value = None
            for k, row in enumerate(rows):
                w = courant[row, :]
                below, above = reach[k]
                scale = ly if k else jnp.ones_like(lx)
                terms = []
                if -2 + below <= far <= 2 + above:
                    keep = jnp.where(depart_lat[row, :] == in_lat, scale * (1.0 - w), none)
                    terms.append(keep * hot[2 * k])
                if -3 + below <= far <= 3 + above:
                    take = jnp.where(near_lat[row, :] == in_lat, scale * w, none)
                    terms.append(take * hot[2 * k + 1])
                if not terms:
                    continue
                total = sum(terms[1:], terms[0])
                if k == 0:
                    beside = pltpu.roll(total, 1, 1) + pltpu.roll(total, NLON - 1, 1)
                    total = core * total + lx * beside
                value = total if value is None else value + total
            put(pair, half, t + half, value)
        put(pair, half, 0 if half else 2 * HALO + 1, jnp.zeros((NLON, NLON), jnp.float32))

    def step(pair, carry):
        fill(pair, 0)
        fill(pair, 1)
        return carry

    lax.fori_loop(0, pairs, step, 0)


VMEM_SPEC = pl.BlockSpec(memory_space=pltpu.VMEM)


def held(x):
    return pltpu.with_memory_space_constraint(x, pltpu.VMEM)


def build_bands(place, fields, pairs, transposed):
    shape = (pairs, PAIR, SPAN) if transposed else (pairs, SPAN, PAIR)
    band = pltpu.VMEM(shape, jnp.bfloat16)
    return pl.pallas_call(
        functools.partial(band_kernel, transposed),
        out_shape=(band, band),
        in_specs=[pl.BlockSpec(memory_space=pltpu.SMEM)] + [VMEM_SPEC] * 6,
        out_specs=(VMEM_SPEC,) * 2,
        scratch_shapes=[pltpu.VMEM((NLAT, NLON), jnp.int32)] * 4
        + [pltpu.VMEM((6, NLON, NLON), jnp.float32)],
        compiler_params=pltpu.CompilerParams(vmem_limit_bytes=24 << 20),
        name="row_bands" if transposed else "col_bands",
    )(place, *fields)


def take_kernel(starts, source, *refs):
    outs, sems = refs[:-1], refs[-1]
    copies = [
        pltpu.make_async_copy(source.at[:, pl.ds(at, out.shape[1])], out, sems.at[i])
        for i, (at, out) in enumerate(zip(starts, outs))
    ]
    for copy in copies:
        copy.start()
    for copy in copies:
        copy.wait()


def take_columns(source, starts, width):
    hbm = pl.BlockSpec(memory_space=pltpu.HBM)
    out = jax.ShapeDtypeStruct((source.shape[0], width), jnp.float32)
    return pl.pallas_call(
        functools.partial(take_kernel, starts),
        out_shape=(out,) * len(starts),
        in_specs=[hbm],
        out_specs=(hbm,) * len(starts),
        scratch_shapes=[pltpu.SemaphoreType.DMA((len(starts),))],
        compiler_params=pltpu.CompilerParams(vmem_limit_bytes=8 << 20),
        name="take",
    )(in_hbm(source))


def rows_kernel(start, place, own, chip, *refs):
    *cross, band_high, band_low, out, high, low, landed, sems = refs
    rows, width = out.shape
    sources = [ref.at[:, pl.ds(start, width)] for ref in (own, chip)] + list(cross)
    copies = [
        pltpu.make_async_copy(source, landed.at[i], sems.at[i])
        for i, source in enumerate(sources)
    ]
    for copy in copies:
        copy.start()
    odd = (place[0] // HALO) & 1
    to_chip = pl.multiple_of((1 - odd) * 2 * rows, rows)
    to_cross = pl.multiple_of(odd * 2 * rows, rows)

    def put(value, at):
        h, l = split(value)
        high[pl.ds(at, rows), :] = h
        low[pl.ds(at, rows), :] = l

    copies[0].wait()
    put(landed[0], rows)
    copies[1].wait()
    put(landed[1], to_chip)
    for copy in copies[2:]:
        copy.wait()
    put(sum((landed[i] for i in range(3, len(copies))), landed[2]), to_cross)
    for pair in range(rows // PAIR):
        at = pair * PAIR
        out[at : at + PAIR, :] = dot3(
            band_high[pair], band_low[pair], high[at : at + SPAN, :], low[at : at + SPAN, :]
        )


def in_hbm(x):
    return pltpu.with_memory_space_constraint(x, pltpu.HBM)


def apply_rows(place, start, own, chip, cross, bands):
    rows, width = cross[0].shape
    ext = pltpu.VMEM((3 * rows, width), jnp.bfloat16)
    hbm = [in_hbm(a) for a in (own, chip, *cross)]
    landed = pltpu.VMEM((len(hbm), rows, width), jnp.float32)
    return pl.pallas_call(
        functools.partial(rows_kernel, start),
        out_shape=pltpu.VMEM((rows, width), jnp.float32),
        in_specs=[pl.BlockSpec(memory_space=pltpu.SMEM)]
        + [pl.BlockSpec(memory_space=pltpu.HBM)] * len(hbm)
        + [VMEM_SPEC] * 2,
        out_specs=VMEM_SPEC,
        scratch_shapes=[ext, ext, landed, pltpu.SemaphoreType.DMA((len(hbm),))],
        compiler_params=pltpu.CompilerParams(vmem_limit_bytes=16 << 20),
        name="rows",
    )(place, *hbm, *(held(a) for a in bands))


def cols_kernel(*refs):
    parts = refs[:-5]
    band_high, band_low, out, high, low = refs[-5:]
    at = 0
    for ref in parts:
        h, l = split(ref[...])
        high[:, at : at + ref.shape[1]] = h
        low[:, at : at + ref.shape[1]] = l
        at += ref.shape[1]
    for pair in range(out.shape[1] // PAIR):
        begin = (pair - 1) * PAIR
        skip = max(0, -begin)
        stop = min(at, begin + SPAN)
        ext = slice(begin + skip, stop)
        band = slice(skip, stop - begin)
        out[:, pair * PAIR : (pair + 1) * PAIR] = dot3(
            high[:, ext], low[:, ext], band_high[pair, band], band_low[pair, band]
        )


def apply_cols(parts, bands, width):
    rows = parts[0].shape[0]
    ext = pltpu.VMEM((rows, sum(p.shape[1] for p in parts)), jnp.bfloat16)
    args = [held(a) for a in (*parts, *bands)]
    return pl.pallas_call(
        cols_kernel,
        out_shape=jax.ShapeDtypeStruct((rows, width), jnp.float32),
        in_specs=[VMEM_SPEC] * len(args),
        out_specs=VMEM_SPEC,
        scratch_shapes=[ext, ext],
        compiler_params=pltpu.CompilerParams(vmem_limit_bytes=32 << 20),
        name="cols",
    )(*args)


def tail_kernel(west, band_high, band_low, part, out):
    h, l = split(west[...])
    band = slice(0, west.shape[1])
    out[...] = part[...] + dot3(h, l, band_high[0, band], band_low[0, band])


def apply_tail(west, bands, part):
    rows, width = part.shape
    block = pl.BlockSpec((rows, PAIR), lambda i: (0, 0))
    args = [held(a) for a in (west, *bands)]
    return pl.pallas_call(
        tail_kernel,
        grid=(1,),
        out_shape=jax.ShapeDtypeStruct((rows, width), jnp.float32),
        in_specs=[VMEM_SPEC] * 3 + [block],
        out_specs=block,
        input_output_aliases={3: 0},
        compiler_params=pltpu.CompilerParams(vmem_limit_bytes=16 << 20),
        name="tail",
    )(*args, part)


def body(
    covariance, latitude_offset, longitude_offset, upwind, courant,
    longitude_diffusion, latitude_diffusion,
):
    block = covariance[0]
    rows, width = block.shape
    row_count, col_count = lax.axis_size("row"), lax.axis_size("col")
    forward = lambda n: [(i, i + 1) for i in range(n - 1)]
    backward = lambda n: [(i + 1, i) for i in range(n - 1)]

    last = row_count - 1
    middle = row_count // 2
    chip_pairs = [(i, i ^ 1) for i in range(row_count)]
    cross_pairs = [((i + 1 ^ 1) - 1, i) for i in range(1, last)]
    middle_pairs = [(middle - 1, middle), (middle, middle - 1)]

    def from_across(k, x):
        if k < 3:
            return [lax.ppermute(x, "row", cross_pairs)]
        ways = [pair for pair in cross_pairs if pair not in middle_pairs]
        cross = lax.ppermute(x, "row", ways + [(middle - 1, 0), (middle, last)])
        return [cross, lax.ppermute(cross, "row", [(0, middle), (last, middle - 1)])]

    fields = [
        a.reshape(NLAT, NLON)
        for a in (
            latitude_offset, longitude_offset, upwind, courant,
            longitude_diffusion, latitude_diffusion,
        )
    ]
    lat_row = (lax.axis_index("row") * (rows // NLON)).astype(jnp.int32).reshape(1)
    lat_col = (lax.axis_index("col") * (width // NLON)).astype(jnp.int32).reshape(1)

    starts = (0, width - PAIR, PAIR, width - 2 * PAIR)
    chip = lax.ppermute(block, "row", chip_pairs)
    own = list(take_columns(block, starts[:1], PAIR))
    own += take_columns(block, starts[1:], PAIR)
    across = [from_across(k, own[k]) for k in range(4)]
    row_bands = build_bands(lat_row, fields, rows // PAIR, True)
    half, side = [], []
    for k in range(4):
        half.append(apply_rows(lat_row, starts[k], block, chip, across[k], row_bands))
        pairs = forward(col_count) if k % 2 else backward(col_count)
        side.append(lax.ppermute(half[k], "col", pairs))
    col_bands = build_bands(lat_col, fields, width // PAIR, False)
    parts = [side[1], half[0], half[2], half[3], half[1], side[0], side[2]]
    part = apply_cols(parts, col_bands, width)
    return apply_tail(side[3], col_bands, part)[None]


def solution(mesh):
    in_specs = (P(None, "row", "col"), P(), P(), P(), P(), P(), P())
    out_specs = P(None, "row", "col")
    return jax.shard_map(body, mesh=mesh, in_specs=in_specs, out_specs=out_specs, check_vma=False)
```

```python
import functools

import jax
import jax.numpy as jnp
from jax import lax
from jax.experimental import pallas as pl
from jax.experimental.pallas import tpu as pltpu
from jax.sharding import PartitionSpec as P


NLAT = 64
NLON = 128
HALO = 4
SPAN = 10 * NLON
PAIR = 2 * NLON


def split(x):
    high = x.astype(jnp.bfloat16)
    low = (x - high.astype(jnp.float32)).astype(jnp.bfloat16)
    return high, low


def dot3(a_high, a_low, b_high, b_low):
    dot = functools.partial(jnp.dot, preferred_element_type=jnp.float32)
    return dot(a_high, b_high) + (dot(a_high, b_low) + dot(a_low, b_high))


def band_kernel(
    transposed, place, lat_off, lon_off, upwind, courant, lon_diff, lat_diff,
    high, low, depart_lat, depart_lon, near_lat, near_lon, hot,
):
    shape = (NLAT, NLON)
    lat = lax.broadcasted_iota(jnp.int32, shape, 0)
    lon = lax.broadcasted_iota(jnp.int32, shape, 1)
    up = upwind[...]
    one = jnp.ones(shape, jnp.int32)
    zero = jnp.zeros(shape, jnp.int32)
    d_lat = jnp.clip(lat + lat_off[...], 0, NLAT - 1)
    d_lon = (lon + lon_off[...]) & (NLON - 1)
    depart_lat[...] = d_lat
    depart_lon[...] = d_lon
    near_lat[...] = jnp.clip(
        d_lat + jnp.where(up == 2, one, zero) - jnp.where(up == 3, one, zero), 0, NLAT - 1
    )
    near_lon[...] = (
        d_lon + jnp.where(up == 0, one, zero) - jnp.where(up == 1, one, zero)
    ) & (NLON - 1)

    sub = lax.broadcasted_iota(jnp.int32, (NLON, NLON), 0)
    first = place[0]
    pairs = high.shape[0]

    def put(pair, half, t, value):
        if transposed:
            value = value.T
        h, l = split(value)
        cells = pl.ds(t * NLON, NLON)
        cols = pl.ds(half * NLON, NLON)
        at = (pair, cols, cells) if transposed else (pair, cells, cols)
        high[at] = h
        low[at] = l

    def fill(pair, half):
        y = first + 2 * pair + half
        lx = lon_diff[pl.ds(y, 1), :]
        ly = lat_diff[pl.ds(y, 1), :]
        core = 1.0 - 2.0 * lx - 2.0 * ly
        none = jnp.zeros_like(lx)
        reach = ((0, 0), (0, 1), (-1, 0))
        rows = (y, jnp.minimum(y + 1, NLAT - 1), jnp.maximum(y - 1, 0))
        rows = [pl.ds(r, 1) for r in rows]
        for k, row in enumerate(rows):
            on = jnp.ones((NLON, NLON), jnp.float32)
            off = jnp.zeros((NLON, NLON), jnp.float32)
            hot[2 * k] = jnp.where(sub == depart_lon[row, :], on, off)
            hot[2 * k + 1] = jnp.where(sub == near_lon[row, :], on, off)
        for t in range(2 * HALO + 1):
            far = t - HALO
            in_lat = y + far
            value = None
            for k, row in enumerate(rows):
                w = courant[row, :]
                below, above = reach[k]
                scale = ly if k else jnp.ones_like(lx)
                terms = []
                if -2 + below <= far <= 2 + above:
                    keep = jnp.where(depart_lat[row, :] == in_lat, scale * (1.0 - w), none)
                    terms.append(keep * hot[2 * k])
                if -3 + below <= far <= 3 + above:
                    take = jnp.where(near_lat[row, :] == in_lat, scale * w, none)
                    terms.append(take * hot[2 * k + 1])
                if not terms:
                    continue
                total = sum(terms[1:], terms[0])
                if k == 0:
                    beside = pltpu.roll(total, 1, 1) + pltpu.roll(total, NLON - 1, 1)
                    total = core * total + lx * beside
                value = total if value is None else value + total
            put(pair, half, t + half, value)
        put(pair, half, 0 if half else 2 * HALO + 1, jnp.zeros((NLON, NLON), jnp.float32))

    def step(pair, carry):
        fill(pair, 0)
        fill(pair, 1)
        return carry

    lax.fori_loop(0, pairs, step, 0)


VMEM_SPEC = pl.BlockSpec(memory_space=pltpu.VMEM)


def held(x):
    return pltpu.with_memory_space_constraint(x, pltpu.VMEM)


def in_hbm(x):
    return pltpu.with_memory_space_constraint(x, pltpu.HBM)


def build_bands(place, fields, pairs, transposed):
    shape = (pairs, PAIR, SPAN) if transposed else (pairs, SPAN, PAIR)
    band = pltpu.VMEM(shape, jnp.bfloat16)
    return pl.pallas_call(
        functools.partial(band_kernel, transposed),
        out_shape=(band, band),
        in_specs=[pl.BlockSpec(memory_space=pltpu.SMEM)] + [VMEM_SPEC] * 6,
        out_specs=(VMEM_SPEC,) * 2,
        scratch_shapes=[pltpu.VMEM((NLAT, NLON), jnp.int32)] * 4
        + [pltpu.VMEM((6, NLON, NLON), jnp.float32)],
        compiler_params=pltpu.CompilerParams(vmem_limit_bytes=24 << 20),
        name="row_bands" if transposed else "col_bands",
    )(place, *fields)


def take_kernel(starts, source, *refs):
    outs, sems = refs[:-1], refs[-1]
    count = sems.shape[1]
    piece = source.shape[0] // count
    copies = []
    for i, (at, out) in enumerate(zip(starts, outs)):
        for j in range(count):
            rows = pl.ds(j * piece, piece)
            copies.append(
                pltpu.make_async_copy(
                    source.at[rows, pl.ds(at, out.shape[1])], out.at[rows], sems.at[i, j]
                )
            )
    for copy in copies:
        copy.start()
    for copy in copies:
        copy.wait()


def take_columns(source, ranges):
    rows = source.shape[0]
    starts = [start for start, _ in ranges]
    return pl.pallas_call(
        functools.partial(take_kernel, starts),
        out_shape=tuple(pltpu.VMEM((rows, stop - start), jnp.float32) for start, stop in ranges),
        in_specs=[pl.BlockSpec(memory_space=pltpu.HBM)],
        out_specs=(VMEM_SPEC,) * len(ranges),
        scratch_shapes=[pltpu.SemaphoreType.DMA((len(ranges), 4))],
        compiler_params=pltpu.CompilerParams(vmem_limit_bytes=8 << 20),
        name="take",
    )(in_hbm(source))


def rows_kernel(starts, place, *refs):
    *sources, band_high, band_low, out, high, low, landed, sems = refs
    rows, width = out.shape
    copies = [
        pltpu.make_async_copy(ref.at[:, pl.ds(start, width)], landed.at[i], sems.at[i])
        for i, (start, ref) in enumerate(zip(starts, sources))
    ]
    for copy in copies:
        copy.start()
    odd = (place[0] // HALO) & 1
    to_chip = pl.multiple_of((1 - odd) * 2 * rows, rows)
    to_cross = pl.multiple_of(odd * 2 * rows, rows)

    def put(value, at):
        h, l = split(value)
        high[pl.ds(at, rows), :] = h
        low[pl.ds(at, rows), :] = l

    copies[0].wait()
    put(landed[0], rows)
    copies[1].wait()
    put(landed[1], to_chip)
    for copy in copies[2:]:
        copy.wait()
    put(sum((landed[i] for i in range(3, len(copies))), landed[2]), to_cross)
    for pair in range(rows // PAIR):
        at = pair * PAIR
        out[at : at + PAIR, :] = dot3(
            band_high[pair], band_low[pair], high[at : at + SPAN, :], low[at : at + SPAN, :]
        )


def apply_rows(place, width, sources, starts, bands):
    rows = sources[0].shape[0]
    ext = pltpu.VMEM((3 * rows, width), jnp.bfloat16)
    hbm = [in_hbm(a) for a in sources]
    landed = pltpu.VMEM((len(hbm), rows, width), jnp.float32)
    return pl.pallas_call(
        functools.partial(rows_kernel, starts),
        out_shape=pltpu.VMEM((rows, width), jnp.float32),
        in_specs=[pl.BlockSpec(memory_space=pltpu.SMEM)]
        + [pl.BlockSpec(memory_space=pltpu.HBM)] * len(hbm)
        + [VMEM_SPEC] * 2,
        out_specs=VMEM_SPEC,
        scratch_shapes=[ext, ext, landed, pltpu.SemaphoreType.DMA((len(hbm),))],
        compiler_params=pltpu.CompilerParams(vmem_limit_bytes=16 << 20),
        name="rows",
    )(place, *hbm, *(held(a) for a in bands))


def cols_kernel(*refs):
    parts = refs[:-5]
    band_high, band_low, out, high, low = refs[-5:]
    at = 0
    for ref in parts:
        h, l = split(ref[...])
        high[:, at : at + ref.shape[1]] = h
        low[:, at : at + ref.shape[1]] = l
        at += ref.shape[1]
    for pair in range(out.shape[1] // PAIR):
        begin = (pair - 1) * PAIR
        skip = max(0, -begin)
        stop = min(at, begin + SPAN)
        ext = slice(begin + skip, stop)
        band = slice(skip, stop - begin)
        out[:, pair * PAIR : (pair + 1) * PAIR] = dot3(
            high[:, ext], low[:, ext], band_high[pair, band], band_low[pair, band]
        )


def apply_cols(parts, bands, width):
    rows = parts[0].shape[0]
    ext = pltpu.VMEM((rows, sum(p.shape[1] for p in parts)), jnp.bfloat16)
    args = [held(a) for a in (*parts, *bands)]
    return pl.pallas_call(
        cols_kernel,
        out_shape=jax.ShapeDtypeStruct((rows, width), jnp.float32),
        in_specs=[VMEM_SPEC] * len(args),
        out_specs=VMEM_SPEC,
        scratch_shapes=[ext, ext],
        compiler_params=pltpu.CompilerParams(vmem_limit_bytes=32 << 20),
        name="cols",
    )(*args)


def tail_kernel(west, band_high, band_low, part, out):
    h, l = split(west[...])
    band = slice(0, west.shape[1])
    out[...] = part[...] + dot3(h, l, band_high[0, band], band_low[0, band])


def apply_tail(west, bands, part):
    rows, width = part.shape
    block = pl.BlockSpec((rows, PAIR), lambda i: (0, 0))
    args = [held(a) for a in (west, *bands)]
    return pl.pallas_call(
        tail_kernel,
        grid=(1,),
        out_shape=jax.ShapeDtypeStruct((rows, width), jnp.float32),
        in_specs=[VMEM_SPEC] * 3 + [block],
        out_specs=block,
        input_output_aliases={3: 0},
        compiler_params=pltpu.CompilerParams(vmem_limit_bytes=16 << 20),
        name="tail",
    )(*args, part)


def body(
    covariance, latitude_offset, longitude_offset, upwind, courant,
    longitude_diffusion, latitude_diffusion,
):
    block = covariance[0]
    rows, width = block.shape
    row_count, col_count = lax.axis_size("row"), lax.axis_size("col")
    forward = lambda n: [(i, i + 1) for i in range(n - 1)]
    backward = lambda n: [(i + 1, i) for i in range(n - 1)]

    last = row_count - 1
    middle = row_count // 2
    chip_pairs = [(i, i ^ 1) for i in range(row_count)]
    cross_pairs = [((i + 1 ^ 1) - 1, i) for i in range(1, last)]
    middle_pairs = [(middle - 1, middle), (middle, middle - 1)]

    fields = [
        a.reshape(NLAT, NLON)
        for a in (
            latitude_offset, longitude_offset, upwind, courant,
            longitude_diffusion, latitude_diffusion,
        )
    ]
    lat_row = (lax.axis_index("row") * (rows // NLON)).astype(jnp.int32).reshape(1)
    lat_col = (lax.axis_index("col") * (width // NLON)).astype(jnp.int32).reshape(1)

    starts = (0, width - PAIR, PAIR, width - 2 * PAIR)
    chip = lax.ppermute(block, "row", chip_pairs)
    (own0,) = take_columns(block, [(0, PAIR)])
    own1, own2 = take_columns(block, [(width - PAIR, width), (PAIR, width - PAIR)])
    across0 = lax.ppermute(own0, "row", cross_pairs)
    ways = [pair for pair in cross_pairs if pair not in middle_pairs]
    across1 = lax.ppermute(own1, "row", ways + [(middle - 1, 0), (middle, last)])
    relay = lax.ppermute(across1, "row", [(0, middle), (last, middle - 1)])
    across2 = lax.ppermute(own2, "row", cross_pairs)
    row_bands = build_bands(lat_row, fields, rows // PAIR, True)
    across = ([across0], [across1, relay], [across2], [across2])
    offset = ([0], [0, 0], [0], [width - 3 * PAIR])
    half, side = [], []
    for k in range(4):
        sources = [block, chip] + across[k]
        begins = [starts[k]] * 2 + offset[k]
        half.append(apply_rows(lat_row, PAIR, sources, begins, row_bands))
        pairs = forward(col_count) if k % 2 else backward(col_count)
        side.append(lax.ppermute(half[k], "col", pairs))
    col_bands = build_bands(lat_col, fields, width // PAIR, False)
    parts = [side[1], half[0], half[2], half[3], half[1], side[0], side[2]]
    part = apply_cols(parts, col_bands, width)
    return apply_tail(side[3], col_bands, part)[None]


def solution(mesh):
    in_specs = (P(None, "row", "col"), P(), P(), P(), P(), P(), P())
    out_specs = P(None, "row", "col")
    return jax.shard_map(body, mesh=mesh, in_specs=in_specs, out_specs=out_specs, check_vma=False)
```

```python
import functools

import jax
import jax.numpy as jnp
from jax import lax
from jax.experimental import pallas as pl
from jax.experimental.pallas import tpu as pltpu
from jax.sharding import PartitionSpec as P


NLAT = 64
NLON = 128
HALO = 4
SPAN = 10 * NLON
PAIR = 2 * NLON


def split(x):
    high = x.astype(jnp.bfloat16)
    low = (x - high.astype(jnp.float32)).astype(jnp.bfloat16)
    return high, low


def dot3(a_high, a_low, b_high, b_low):
    dot = functools.partial(jnp.dot, preferred_element_type=jnp.float32)
    return dot(a_high, b_high) + (dot(a_high, b_low) + dot(a_low, b_high))


def band_kernel(
    transposed, place, lat_off, lon_off, upwind, courant, lon_diff, lat_diff,
    high, low, depart_lat, depart_lon, near_lat, near_lon, hot,
):
    shape = (NLAT, NLON)
    lat = lax.broadcasted_iota(jnp.int32, shape, 0)
    lon = lax.broadcasted_iota(jnp.int32, shape, 1)
    up = upwind[...]
    one = jnp.ones(shape, jnp.int32)
    zero = jnp.zeros(shape, jnp.int32)
    d_lat = jnp.clip(lat + lat_off[...], 0, NLAT - 1)
    d_lon = (lon + lon_off[...]) & (NLON - 1)
    depart_lat[...] = d_lat
    depart_lon[...] = d_lon
    near_lat[...] = jnp.clip(
        d_lat + jnp.where(up == 2, one, zero) - jnp.where(up == 3, one, zero), 0, NLAT - 1
    )
    near_lon[...] = (
        d_lon + jnp.where(up == 0, one, zero) - jnp.where(up == 1, one, zero)
    ) & (NLON - 1)

    sub = lax.broadcasted_iota(jnp.int32, (NLON, NLON), 0)
    first = place[0]
    pairs = high.shape[0]

    def put(pair, half, t, value):
        if transposed:
            value = value.T
        h, l = split(value)
        cells = pl.ds(t * NLON, NLON)
        cols = pl.ds(half * NLON, NLON)
        at = (pair, cols, cells) if transposed else (pair, cells, cols)
        high[at] = h
        low[at] = l

    def fill(pair, half):
        y = first + 2 * pair + half
        lx = lon_diff[pl.ds(y, 1), :]
        ly = lat_diff[pl.ds(y, 1), :]
        core = 1.0 - 2.0 * lx - 2.0 * ly
        none = jnp.zeros_like(lx)
        reach = ((0, 0), (0, 1), (-1, 0))
        rows = (y, jnp.minimum(y + 1, NLAT - 1), jnp.maximum(y - 1, 0))
        rows = [pl.ds(r, 1) for r in rows]
        for k, row in enumerate(rows):
            on = jnp.ones((NLON, NLON), jnp.float32)
            off = jnp.zeros((NLON, NLON), jnp.float32)
            hot[2 * k] = jnp.where(sub == depart_lon[row, :], on, off)
            hot[2 * k + 1] = jnp.where(sub == near_lon[row, :], on, off)
        for t in range(2 * HALO + 1):
            far = t - HALO
            in_lat = y + far
            value = None
            for k, row in enumerate(rows):
                w = courant[row, :]
                below, above = reach[k]
                scale = ly if k else jnp.ones_like(lx)
                terms = []
                if -2 + below <= far <= 2 + above:
                    keep = jnp.where(depart_lat[row, :] == in_lat, scale * (1.0 - w), none)
                    terms.append(keep * hot[2 * k])
                if -3 + below <= far <= 3 + above:
                    take = jnp.where(near_lat[row, :] == in_lat, scale * w, none)
                    terms.append(take * hot[2 * k + 1])
                if not terms:
                    continue
                total = sum(terms[1:], terms[0])
                if k == 0:
                    beside = pltpu.roll(total, 1, 1) + pltpu.roll(total, NLON - 1, 1)
                    total = core * total + lx * beside
                value = total if value is None else value + total
            put(pair, half, t + half, value)
        put(pair, half, 0 if half else 2 * HALO + 1, jnp.zeros((NLON, NLON), jnp.float32))

    def step(pair, carry):
        fill(pair, 0)
        fill(pair, 1)
        return carry

    lax.fori_loop(0, pairs, step, 0)


VMEM_SPEC = pl.BlockSpec(memory_space=pltpu.VMEM)


def held(x):
    return pltpu.with_memory_space_constraint(x, pltpu.VMEM)


def in_hbm(x):
    return pltpu.with_memory_space_constraint(x, pltpu.HBM)


def build_bands(place, fields, pairs, transposed):
    shape = (pairs, PAIR, SPAN) if transposed else (pairs, SPAN, PAIR)
    band = pltpu.VMEM(shape, jnp.bfloat16)
    return pl.pallas_call(
        functools.partial(band_kernel, transposed),
        out_shape=(band, band),
        in_specs=[pl.BlockSpec(memory_space=pltpu.SMEM)] + [VMEM_SPEC] * 6,
        out_specs=(VMEM_SPEC,) * 2,
        scratch_shapes=[pltpu.VMEM((NLAT, NLON), jnp.int32)] * 4
        + [pltpu.VMEM((6, NLON, NLON), jnp.float32)],
        compiler_params=pltpu.CompilerParams(vmem_limit_bytes=24 << 20),
        name="row_bands" if transposed else "col_bands",
    )(place, *fields)


def take_kernel(starts, source, *refs):
    outs, sems = refs[:-1], refs[-1]
    count = sems.shape[1]
    piece = source.shape[0] // count
    copies = []
    for i, (at, out) in enumerate(zip(starts, outs)):
        for j in range(count):
            rows = pl.ds(j * piece, piece)
            copies.append(
                pltpu.make_async_copy(
                    source.at[rows, pl.ds(at, out.shape[1])], out.at[rows], sems.at[i, j]
                )
            )
    for copy in copies:
        copy.start()
    for copy in copies:
        copy.wait()


def take_columns(source, ranges):
    rows = source.shape[0]
    starts = [start for start, _ in ranges]
    return pl.pallas_call(
        functools.partial(take_kernel, starts),
        out_shape=tuple(pltpu.VMEM((rows, stop - start), jnp.float32) for start, stop in ranges),
        in_specs=[pl.BlockSpec(memory_space=pltpu.HBM)],
        out_specs=(VMEM_SPEC,) * len(ranges),
        scratch_shapes=[pltpu.SemaphoreType.DMA((len(ranges), 4))],
        compiler_params=pltpu.CompilerParams(vmem_limit_bytes=8 << 20),
        name="take",
    )(in_hbm(source))


def rows_kernel(starts, place, *refs):
    *sources, band_high, band_low, out, high, low, landed, sems = refs
    rows, width = out.shape
    copies = [
        pltpu.make_async_copy(ref.at[:, pl.ds(start, width)], landed.at[i], sems.at[i])
        for i, (start, ref) in enumerate(zip(starts, sources))
    ]
    for copy in copies:
        copy.start()
    odd = (place[0] // HALO) & 1
    to_chip = pl.multiple_of((1 - odd) * 2 * rows, rows)
    to_cross = pl.multiple_of(odd * 2 * rows, rows)

    def put(value, at):
        h, l = split(value)
        high[pl.ds(at, rows), :] = h
        low[pl.ds(at, rows), :] = l

    copies[0].wait()
    put(landed[0], rows)
    copies[1].wait()
    put(landed[1], to_chip)
    for copy in copies[2:]:
        copy.wait()
    put(sum((landed[i] for i in range(3, len(copies))), landed[2]), to_cross)
    for pair in range(rows // PAIR):
        at = pair * PAIR
        out[at : at + PAIR, :] = dot3(
            band_high[pair], band_low[pair], high[at : at + SPAN, :], low[at : at + SPAN, :]
        )


def apply_rows(place, width, sources, starts, bands):
    rows = sources[0].shape[0]
    ext = pltpu.VMEM((3 * rows, width), jnp.bfloat16)
    hbm = [in_hbm(a) for a in sources]
    landed = pltpu.VMEM((len(hbm), rows, width), jnp.float32)
    return pl.pallas_call(
        functools.partial(rows_kernel, starts),
        out_shape=pltpu.VMEM((rows, width), jnp.float32),
        in_specs=[pl.BlockSpec(memory_space=pltpu.SMEM)]
        + [pl.BlockSpec(memory_space=pltpu.HBM)] * len(hbm)
        + [VMEM_SPEC] * 2,
        out_specs=VMEM_SPEC,
        scratch_shapes=[ext, ext, landed, pltpu.SemaphoreType.DMA((len(hbm),))],
        compiler_params=pltpu.CompilerParams(vmem_limit_bytes=16 << 20),
        name="rows",
    )(place, *hbm, *(held(a) for a in bands))


def cols_kernel(*refs):
    parts = refs[:-5]
    band_high, band_low, out, high, low = refs[-5:]
    at = 0
    for ref in parts:
        h, l = split(ref[...])
        high[:, at : at + ref.shape[1]] = h
        low[:, at : at + ref.shape[1]] = l
        at += ref.shape[1]
    for pair in range(out.shape[1] // PAIR):
        begin = (pair - 1) * PAIR
        skip = max(0, -begin)
        stop = min(at, begin + SPAN)
        ext = slice(begin + skip, stop)
        band = slice(skip, stop - begin)
        out[:, pair * PAIR : (pair + 1) * PAIR] = dot3(
            high[:, ext], low[:, ext], band_high[pair, band], band_low[pair, band]
        )


def apply_cols(parts, bands, width):
    rows = parts[0].shape[0]
    ext = pltpu.VMEM((rows, sum(p.shape[1] for p in parts)), jnp.bfloat16)
    args = [held(a) for a in (*parts, *bands)]
    return pl.pallas_call(
        cols_kernel,
        out_shape=jax.ShapeDtypeStruct((rows, width), jnp.float32),
        in_specs=[VMEM_SPEC] * len(args),
        out_specs=VMEM_SPEC,
        scratch_shapes=[ext, ext],
        compiler_params=pltpu.CompilerParams(vmem_limit_bytes=32 << 20),
        name="cols",
    )(*args)


def tail_kernel(pair, band_rows, side, band_high, band_low, part, out):
    h, l = split(side[...])
    out[...] = part[...] + dot3(h, l, band_high[pair, band_rows], band_low[pair, band_rows])


def apply_tail(side, bands, part, pair, band_rows):
    rows, width = part.shape
    block = pl.BlockSpec((rows, PAIR), lambda i: (0, pair))
    args = [held(a) for a in (side, *bands)]
    return pl.pallas_call(
        functools.partial(tail_kernel, pair, band_rows),
        grid=(1,),
        out_shape=jax.ShapeDtypeStruct((rows, width), jnp.float32),
        in_specs=[VMEM_SPEC] * 3 + [block],
        out_specs=block,
        input_output_aliases={3: 0},
        compiler_params=pltpu.CompilerParams(vmem_limit_bytes=16 << 20),
        name="tail",
    )(*args, part)


def body(
    covariance, latitude_offset, longitude_offset, upwind, courant,
    longitude_diffusion, latitude_diffusion,
):
    block = covariance[0]
    rows, width = block.shape
    row_count, col_count = lax.axis_size("row"), lax.axis_size("col")
    forward = lambda n: [(i, i + 1) for i in range(n - 1)]
    backward = lambda n: [(i + 1, i) for i in range(n - 1)]

    last = row_count - 1
    middle = row_count // 2
    chip_pairs = [(i, i ^ 1) for i in range(row_count)]
    cross_pairs = [((i + 1 ^ 1) - 1, i) for i in range(1, last)]
    middle_pairs = [(middle - 1, middle), (middle, middle - 1)]

    fields = [
        a.reshape(NLAT, NLON)
        for a in (
            latitude_offset, longitude_offset, upwind, courant,
            longitude_diffusion, latitude_diffusion,
        )
    ]
    lat_row = (lax.axis_index("row") * (rows // NLON)).astype(jnp.int32).reshape(1)
    lat_col = (lax.axis_index("col") * (width // NLON)).astype(jnp.int32).reshape(1)

    starts = (0, width - PAIR, PAIR, width - 2 * PAIR)
    chip = lax.ppermute(block, "row", chip_pairs)
    own0, own1 = take_columns(block, [(0, PAIR), (width - PAIR, width)])
    (own2,) = take_columns(block, [(PAIR, width - PAIR)])
    across0 = lax.ppermute(own0, "row", cross_pairs)
    ways = [pair for pair in cross_pairs if pair not in middle_pairs]
    across1 = lax.ppermute(own1, "row", ways)
    ends = lax.ppermute(own1, "row", [(middle - 1, 0), (middle, last)])
    relay = lax.ppermute(ends, "row", [(0, middle), (last, middle - 1)])
    across2 = lax.ppermute(own2, "row", cross_pairs)
    row_bands = build_bands(lat_row, fields, rows // PAIR, True)
    across = ([across0], [across1, relay], [across2], [across2])
    offset = ([0], [0, 0], [0], [width - 3 * PAIR])
    half, side = [], []
    for k in range(4):
        sources = [block, chip] + across[k]
        begins = [starts[k]] * 2 + offset[k]
        half.append(apply_rows(lat_row, PAIR, sources, begins, row_bands))
        pairs = forward(col_count) if k % 2 else backward(col_count)
        side.append(lax.ppermute(half[k], "col", pairs))
    col_bands = build_bands(lat_col, fields, width // PAIR, False)
    parts = [side[1], half[0], half[2], half[3], half[1], side[0]]
    part = apply_cols(parts, col_bands, width)
    pairs = width // PAIR
    part = apply_tail(side[2], col_bands, part, pairs - 1, slice(SPAN - PAIR, SPAN))
    return apply_tail(side[3], col_bands, part, 0, slice(0, PAIR))[None]


def solution(mesh):
    in_specs = (P(None, "row", "col"), P(), P(), P(), P(), P(), P())
    out_specs = P(None, "row", "col")
    return jax.shard_map(body, mesh=mesh, in_specs=in_specs, out_specs=out_specs, check_vma=False)
```

```python
import functools

import jax
import jax.numpy as jnp
from jax import lax
from jax.experimental import pallas as pl
from jax.experimental.pallas import tpu as pltpu
from jax.sharding import PartitionSpec as P


NLAT = 64
NLON = 128
HALO = 4
SPAN = 10 * NLON
PAIR = 2 * NLON


def split(x):
    high = x.astype(jnp.bfloat16)
    low = (x - high.astype(jnp.float32)).astype(jnp.bfloat16)
    return high, low


def dot3(a_high, a_low, b_high, b_low):
    dot = functools.partial(jnp.dot, preferred_element_type=jnp.float32)
    return dot(a_high, b_high) + (dot(a_high, b_low) + dot(a_low, b_high))


def band_kernel(
    transposed, place, lat_off, lon_off, upwind, courant, lon_diff, lat_diff,
    high, low, depart_lat, depart_lon, near_lat, near_lon, hot,
):
    shape = (NLAT, NLON)
    lat = lax.broadcasted_iota(jnp.int32, shape, 0)
    lon = lax.broadcasted_iota(jnp.int32, shape, 1)
    up = upwind[...]
    one = jnp.ones(shape, jnp.int32)
    zero = jnp.zeros(shape, jnp.int32)
    d_lat = jnp.clip(lat + lat_off[...], 0, NLAT - 1)
    d_lon = (lon + lon_off[...]) & (NLON - 1)
    depart_lat[...] = d_lat
    depart_lon[...] = d_lon
    near_lat[...] = jnp.clip(
        d_lat + jnp.where(up == 2, one, zero) - jnp.where(up == 3, one, zero), 0, NLAT - 1
    )
    near_lon[...] = (
        d_lon + jnp.where(up == 0, one, zero) - jnp.where(up == 1, one, zero)
    ) & (NLON - 1)

    sub = lax.broadcasted_iota(jnp.int32, (NLON, NLON), 0)
    first = place[0]
    pairs = high.shape[0]

    def put(pair, half, t, value):
        if transposed:
            value = value.T
        h, l = split(value)
        cells = pl.ds(t * NLON, NLON)
        cols = pl.ds(half * NLON, NLON)
        at = (pair, cols, cells) if transposed else (pair, cells, cols)
        high[at] = h
        low[at] = l

    def fill(pair, half):
        y = first + 2 * pair + half
        lx = lon_diff[pl.ds(y, 1), :]
        ly = lat_diff[pl.ds(y, 1), :]
        core = 1.0 - 2.0 * lx - 2.0 * ly
        none = jnp.zeros_like(lx)
        reach = ((0, 0), (0, 1), (-1, 0))
        rows = (y, jnp.minimum(y + 1, NLAT - 1), jnp.maximum(y - 1, 0))
        rows = [pl.ds(r, 1) for r in rows]
        for k, row in enumerate(rows):
            on = jnp.ones((NLON, NLON), jnp.float32)
            off = jnp.zeros((NLON, NLON), jnp.float32)
            hot[2 * k] = jnp.where(sub == depart_lon[row, :], on, off)
            hot[2 * k + 1] = jnp.where(sub == near_lon[row, :], on, off)
        for t in range(2 * HALO + 1):
            far = t - HALO
            in_lat = y + far
            value = None
            for k, row in enumerate(rows):
                w = courant[row, :]
                below, above = reach[k]
                scale = ly if k else jnp.ones_like(lx)
                terms = []
                if -2 + below <= far <= 2 + above:
                    keep = jnp.where(depart_lat[row, :] == in_lat, scale * (1.0 - w), none)
                    terms.append(keep * hot[2 * k])
                if -3 + below <= far <= 3 + above:
                    take = jnp.where(near_lat[row, :] == in_lat, scale * w, none)
                    terms.append(take * hot[2 * k + 1])
                if not terms:
                    continue
                total = sum(terms[1:], terms[0])
                if k == 0:
                    beside = pltpu.roll(total, 1, 1) + pltpu.roll(total, NLON - 1, 1)
                    total = core * total + lx * beside
                value = total if value is None else value + total
            put(pair, half, t + half, value)
        put(pair, half, 0 if half else 2 * HALO + 1, jnp.zeros((NLON, NLON), jnp.float32))

    def step(pair, carry):
        fill(pair, 0)
        fill(pair, 1)
        return carry

    lax.fori_loop(0, pairs, step, 0)


VMEM_SPEC = pl.BlockSpec(memory_space=pltpu.VMEM)


def held(x):
    return pltpu.with_memory_space_constraint(x, pltpu.VMEM)


def in_hbm(x):
    return pltpu.with_memory_space_constraint(x, pltpu.HBM)


def build_bands(place, fields, pairs, transposed):
    shape = (pairs, PAIR, SPAN) if transposed else (pairs, SPAN, PAIR)
    band = pltpu.VMEM(shape, jnp.bfloat16)
    return pl.pallas_call(
        functools.partial(band_kernel, transposed),
        out_shape=(band, band),
        in_specs=[pl.BlockSpec(memory_space=pltpu.SMEM)] + [VMEM_SPEC] * 6,
        out_specs=(VMEM_SPEC,) * 2,
        scratch_shapes=[pltpu.VMEM((NLAT, NLON), jnp.int32)] * 4
        + [pltpu.VMEM((6, NLON, NLON), jnp.float32)],
        compiler_params=pltpu.CompilerParams(vmem_limit_bytes=24 << 20),
        name="row_bands" if transposed else "col_bands",
    )(place, *fields)


def take_kernel(starts, source, *refs):
    outs, sems = refs[:-1], refs[-1]
    count = sems.shape[1]
    piece = source.shape[0] // count
    copies = []
    for i, (at, out) in enumerate(zip(starts, outs)):
        for j in range(count):
            rows = pl.ds(j * piece, piece)
            copies.append(
                pltpu.make_async_copy(
                    source.at[rows, pl.ds(at, out.shape[1])], out.at[rows], sems.at[i, j]
                )
            )
    for copy in copies:
        copy.start()
    for copy in copies:
        copy.wait()


def take_columns(source, ranges):
    rows = source.shape[0]
    starts = [start for start, _ in ranges]
    return pl.pallas_call(
        functools.partial(take_kernel, starts),
        out_shape=tuple(pltpu.VMEM((rows, stop - start), jnp.float32) for start, stop in ranges),
        in_specs=[pl.BlockSpec(memory_space=pltpu.HBM)],
        out_specs=(VMEM_SPEC,) * len(ranges),
        scratch_shapes=[pltpu.SemaphoreType.DMA((len(ranges), 4))],
        compiler_params=pltpu.CompilerParams(vmem_limit_bytes=8 << 20),
        name="take",
    )(in_hbm(source))


def rows_kernel(starts, place, *refs):
    *sources, band_high, band_low, out, high, low, landed, sems = refs
    rows, width = out.shape
    copies = [
        pltpu.make_async_copy(ref.at[:, pl.ds(start, width)], landed.at[i], sems.at[i])
        for i, (start, ref) in enumerate(zip(starts, sources))
    ]
    for copy in copies:
        copy.start()
    odd = (place[0] // HALO) & 1
    to_chip = pl.multiple_of((1 - odd) * 2 * rows, rows)
    to_cross = pl.multiple_of(odd * 2 * rows, rows)

    def put(value, at):
        h, l = split(value)
        high[pl.ds(at, rows), :] = h
        low[pl.ds(at, rows), :] = l

    copies[0].wait()
    put(landed[0], rows)
    copies[1].wait()
    put(landed[1], to_chip)
    for copy in copies[2:]:
        copy.wait()
    put(sum((landed[i] for i in range(3, len(copies))), landed[2]), to_cross)
    for pair in range(rows // PAIR):
        at = pair * PAIR
        out[at : at + PAIR, :] = dot3(
            band_high[pair], band_low[pair], high[at : at + SPAN, :], low[at : at + SPAN, :]
        )


def apply_rows(place, width, sources, starts, bands):
    rows = sources[0].shape[0]
    ext = pltpu.VMEM((3 * rows, width), jnp.bfloat16)
    hbm = [in_hbm(a) for a in sources]
    landed = pltpu.VMEM((len(hbm), rows, width), jnp.float32)
    return pl.pallas_call(
        functools.partial(rows_kernel, starts),
        out_shape=pltpu.VMEM((rows, width), jnp.float32),
        in_specs=[pl.BlockSpec(memory_space=pltpu.SMEM)]
        + [pl.BlockSpec(memory_space=pltpu.HBM)] * len(hbm)
        + [VMEM_SPEC] * 2,
        out_specs=VMEM_SPEC,
        scratch_shapes=[ext, ext, landed, pltpu.SemaphoreType.DMA((len(hbm),))],
        compiler_params=pltpu.CompilerParams(vmem_limit_bytes=16 << 20),
        name="rows",
    )(place, *hbm, *(held(a) for a in bands))


def cols_kernel(*refs):
    parts = refs[:-5]
    band_high, band_low, out, high, low = refs[-5:]
    at = 0
    for ref in parts:
        h, l = split(ref[...])
        high[:, at : at + ref.shape[1]] = h
        low[:, at : at + ref.shape[1]] = l
        at += ref.shape[1]
    for pair in range(out.shape[1] // PAIR):
        begin = (pair - 1) * PAIR
        skip = max(0, -begin)
        stop = min(at, begin + SPAN)
        ext = slice(begin + skip, stop)
        band = slice(skip, stop - begin)
        out[:, pair * PAIR : (pair + 1) * PAIR] = dot3(
            high[:, ext], low[:, ext], band_high[pair, band], band_low[pair, band]
        )


def apply_cols(parts, bands, width):
    rows = parts[0].shape[0]
    ext = pltpu.VMEM((rows, sum(p.shape[1] for p in parts)), jnp.bfloat16)
    args = [held(a) for a in (*parts, *bands)]
    return pl.pallas_call(
        cols_kernel,
        out_shape=jax.ShapeDtypeStruct((rows, width), jnp.float32),
        in_specs=[VMEM_SPEC] * len(args),
        out_specs=VMEM_SPEC,
        scratch_shapes=[ext, ext],
        compiler_params=pltpu.CompilerParams(vmem_limit_bytes=32 << 20),
        name="cols",
    )(*args)


def tail_kernel(pair, band_rows, side, band_high, band_low, part, out):
    h, l = split(side[...])
    out[...] = part[...] + dot3(h, l, band_high[pair, band_rows], band_low[pair, band_rows])


def apply_tail(side, bands, part, pair, band_rows):
    rows, width = part.shape
    block = pl.BlockSpec((rows, PAIR), lambda i: (0, pair))
    args = [held(a) for a in (side, *bands)]
    return pl.pallas_call(
        functools.partial(tail_kernel, pair, band_rows),
        grid=(1,),
        out_shape=jax.ShapeDtypeStruct((rows, width), jnp.float32),
        in_specs=[VMEM_SPEC] * 3 + [block],
        out_specs=block,
        input_output_aliases={3: 0},
        compiler_params=pltpu.CompilerParams(vmem_limit_bytes=16 << 20),
        name="tail",
    )(*args, part)


def body(
    covariance, latitude_offset, longitude_offset, upwind, courant,
    longitude_diffusion, latitude_diffusion,
):
    block = covariance[0]
    rows, width = block.shape
    row_count, col_count = lax.axis_size("row"), lax.axis_size("col")
    forward = lambda n: [(i, i + 1) for i in range(n - 1)]
    backward = lambda n: [(i + 1, i) for i in range(n - 1)]

    chip_pairs = [(i, i ^ 1) for i in range(row_count)]
    cross_pairs = [((i + 1 ^ 1) - 1, i) for i in range(1, row_count - 1)]

    fields = [
        a.reshape(NLAT, NLON)
        for a in (
            latitude_offset, longitude_offset, upwind, courant,
            longitude_diffusion, latitude_diffusion,
        )
    ]
    lat_row = (lax.axis_index("row") * (rows // NLON)).astype(jnp.int32).reshape(1)
    lat_col = (lax.axis_index("col") * (width // NLON)).astype(jnp.int32).reshape(1)

    starts = (0, width - PAIR, PAIR, width - 2 * PAIR)
    chip = lax.ppermute(block, "row", chip_pairs)
    (own0,) = take_columns(block, [(0, PAIR)])
    (own1,) = take_columns(block, [(PAIR, width)])
    across0 = lax.ppermute(own0, "row", cross_pairs)
    across1 = lax.ppermute(own1, "row", cross_pairs)
    row_bands = build_bands(lat_row, fields, rows // PAIR, True)
    half, side = [], []
    for k in range(4):
        sources = [block, chip, across1 if k else across0]
        begins = [starts[k], starts[k], starts[k] - PAIR if k else 0]
        half.append(apply_rows(lat_row, PAIR, sources, begins, row_bands))
        pairs = forward(col_count) if k % 2 else backward(col_count)
        side.append(lax.ppermute(half[k], "col", pairs))
    col_bands = build_bands(lat_col, fields, width // PAIR, False)
    parts = [side[1], half[0], half[2], half[3], half[1], side[0]]
    part = apply_cols(parts, col_bands, width)
    pairs = width // PAIR
    part = apply_tail(side[2], col_bands, part, pairs - 1, slice(SPAN - PAIR, SPAN))
    return apply_tail(side[3], col_bands, part, 0, slice(0, PAIR))[None]


def solution(mesh):
    in_specs = (P(None, "row", "col"), P(), P(), P(), P(), P(), P())
    out_specs = P(None, "row", "col")
    return jax.shard_map(body, mesh=mesh, in_specs=in_specs, out_specs=out_specs, check_vma=False)
```

```python
import functools

import jax
import jax.numpy as jnp
from jax import lax
from jax.experimental import pallas as pl
from jax.experimental.pallas import tpu as pltpu
from jax.sharding import PartitionSpec as P


NLAT = 64
NLON = 128
HALO = 4
SPAN = 10 * NLON
PAIR = 2 * NLON


def split(x):
    high = x.astype(jnp.bfloat16)
    low = (x - high.astype(jnp.float32)).astype(jnp.bfloat16)
    return high, low


def dot3(a_high, a_low, b_high, b_low):
    dot = functools.partial(jnp.dot, preferred_element_type=jnp.float32)
    return dot(a_high, b_high) + (dot(a_high, b_low) + dot(a_low, b_high))


def band_kernel(
    transposed, place, lat_off, lon_off, upwind, courant, lon_diff, lat_diff,
    high, low, depart_lat, depart_lon, near_lat, near_lon, hot,
):
    shape = (NLAT, NLON)
    lat = lax.broadcasted_iota(jnp.int32, shape, 0)
    lon = lax.broadcasted_iota(jnp.int32, shape, 1)
    up = upwind[...]
    one = jnp.ones(shape, jnp.int32)
    zero = jnp.zeros(shape, jnp.int32)
    d_lat = jnp.clip(lat + lat_off[...], 0, NLAT - 1)
    d_lon = (lon + lon_off[...]) & (NLON - 1)
    depart_lat[...] = d_lat
    depart_lon[...] = d_lon
    near_lat[...] = jnp.clip(
        d_lat + jnp.where(up == 2, one, zero) - jnp.where(up == 3, one, zero), 0, NLAT - 1
    )
    near_lon[...] = (
        d_lon + jnp.where(up == 0, one, zero) - jnp.where(up == 1, one, zero)
    ) & (NLON - 1)

    sub = lax.broadcasted_iota(jnp.int32, (NLON, NLON), 0)
    first = place[0]
    pairs = high.shape[0]

    def put(pair, half, t, value):
        if transposed:
            value = value.T
        h, l = split(value)
        cells = pl.ds(t * NLON, NLON)
        cols = pl.ds(half * NLON, NLON)
        at = (pair, cols, cells) if transposed else (pair, cells, cols)
        high[at] = h
        low[at] = l

    def fill(pair, half):
        y = first + 2 * pair + half
        lx = lon_diff[pl.ds(y, 1), :]
        ly = lat_diff[pl.ds(y, 1), :]
        core = 1.0 - 2.0 * lx - 2.0 * ly
        none = jnp.zeros_like(lx)
        reach = ((0, 0), (0, 1), (-1, 0))
        rows = (y, jnp.minimum(y + 1, NLAT - 1), jnp.maximum(y - 1, 0))
        rows = [pl.ds(r, 1) for r in rows]
        for k, row in enumerate(rows):
            on = jnp.ones((NLON, NLON), jnp.float32)
            off = jnp.zeros((NLON, NLON), jnp.float32)
            hot[2 * k] = jnp.where(sub == depart_lon[row, :], on, off)
            hot[2 * k + 1] = jnp.where(sub == near_lon[row, :], on, off)
        for t in range(2 * HALO + 1):
            far = t - HALO
            in_lat = y + far
            value = None
            for k, row in enumerate(rows):
                w = courant[row, :]
                below, above = reach[k]
                scale = ly if k else jnp.ones_like(lx)
                terms = []
                if -2 + below <= far <= 2 + above:
                    keep = jnp.where(depart_lat[row, :] == in_lat, scale * (1.0 - w), none)
                    terms.append(keep * hot[2 * k])
                if -3 + below <= far <= 3 + above:
                    take = jnp.where(near_lat[row, :] == in_lat, scale * w, none)
                    terms.append(take * hot[2 * k + 1])
                if not terms:
                    continue
                total = sum(terms[1:], terms[0])
                if k == 0:
                    beside = pltpu.roll(total, 1, 1) + pltpu.roll(total, NLON - 1, 1)
                    total = core * total + lx * beside
                value = total if value is None else value + total
            put(pair, half, t + half, value)
        put(pair, half, 0 if half else 2 * HALO + 1, jnp.zeros((NLON, NLON), jnp.float32))

    def step(pair, carry):
        fill(pair, 0)
        fill(pair, 1)
        return carry

    lax.fori_loop(0, pairs, step, 0)


VMEM_SPEC = pl.BlockSpec(memory_space=pltpu.VMEM)


def held(x):
    return pltpu.with_memory_space_constraint(x, pltpu.VMEM)


def in_hbm(x):
    return pltpu.with_memory_space_constraint(x, pltpu.HBM)


def build_bands(place, fields, pairs, transposed):
    shape = (pairs, PAIR, SPAN) if transposed else (pairs, SPAN, PAIR)
    band = pltpu.VMEM(shape, jnp.bfloat16)
    return pl.pallas_call(
        functools.partial(band_kernel, transposed),
        out_shape=(band, band),
        in_specs=[pl.BlockSpec(memory_space=pltpu.SMEM)] + [VMEM_SPEC] * 6,
        out_specs=(VMEM_SPEC,) * 2,
        scratch_shapes=[pltpu.VMEM((NLAT, NLON), jnp.int32)] * 4
        + [pltpu.VMEM((6, NLON, NLON), jnp.float32)],
        compiler_params=pltpu.CompilerParams(vmem_limit_bytes=24 << 20),
        name="row_bands" if transposed else "col_bands",
    )(place, *fields)


def take_kernel(starts, source, *refs):
    outs, sems = refs[:-1], refs[-1]
    count = sems.shape[1]
    piece = source.shape[0] // count
    copies = []
    for i, (at, out) in enumerate(zip(starts, outs)):
        for j in range(count):
            rows = pl.ds(j * piece, piece)
            copies.append(
                pltpu.make_async_copy(
                    source.at[rows, pl.ds(at, out.shape[1])], out.at[rows], sems.at[i, j]
                )
            )
    for copy in copies:
        copy.start()
    for copy in copies:
        copy.wait()


def take_columns(source, ranges):
    rows = source.shape[0]
    starts = [start for start, _ in ranges]
    return pl.pallas_call(
        functools.partial(take_kernel, starts),
        out_shape=tuple(pltpu.VMEM((rows, stop - start), jnp.float32) for start, stop in ranges),
        in_specs=[pl.BlockSpec(memory_space=pltpu.HBM)],
        out_specs=(VMEM_SPEC,) * len(ranges),
        scratch_shapes=[pltpu.SemaphoreType.DMA((len(ranges), 4))],
        compiler_params=pltpu.CompilerParams(vmem_limit_bytes=8 << 20),
        name="take",
    )(in_hbm(source))


def rows_kernel(starts, place, *refs):
    *sources, band_high, band_low, out, high, low, landed, sems = refs
    rows, width = out.shape
    copies = [
        pltpu.make_async_copy(ref.at[:, pl.ds(start, width)], landed.at[i], sems.at[i])
        for i, (start, ref) in enumerate(zip(starts, sources))
    ]
    for copy in copies:
        copy.start()
    odd = (place[0] // HALO) & 1
    to_chip = pl.multiple_of((1 - odd) * 2 * rows, rows)
    to_cross = pl.multiple_of(odd * 2 * rows, rows)

    def put(value, at):
        h, l = split(value)
        high[pl.ds(at, rows), :] = h
        low[pl.ds(at, rows), :] = l

    copies[0].wait()
    put(landed[0], rows)
    copies[1].wait()
    put(landed[1], to_chip)
    for copy in copies[2:]:
        copy.wait()
    put(sum((landed[i] for i in range(3, len(copies))), landed[2]), to_cross)
    for pair in range(rows // PAIR):
        at = pair * PAIR
        out[at : at + PAIR, :] = dot3(
            band_high[pair], band_low[pair], high[at : at + SPAN, :], low[at : at + SPAN, :]
        )


def apply_rows(place, width, sources, starts, bands):
    rows = sources[0].shape[0]
    ext = pltpu.VMEM((3 * rows, width), jnp.bfloat16)
    hbm = [in_hbm(a) for a in sources]
    landed = pltpu.VMEM((len(hbm), rows, width), jnp.float32)
    return pl.pallas_call(
        functools.partial(rows_kernel, starts),
        out_shape=pltpu.VMEM((rows, width), jnp.float32),
        in_specs=[pl.BlockSpec(memory_space=pltpu.SMEM)]
        + [pl.BlockSpec(memory_space=pltpu.HBM)] * len(hbm)
        + [VMEM_SPEC] * 2,
        out_specs=VMEM_SPEC,
        scratch_shapes=[ext, ext, landed, pltpu.SemaphoreType.DMA((len(hbm),))],
        compiler_params=pltpu.CompilerParams(vmem_limit_bytes=16 << 20),
        name="rows",
    )(place, *hbm, *(held(a) for a in bands))


def cols_kernel(*refs):
    parts = refs[:-5]
    band_high, band_low, out, high, low = refs[-5:]
    at = 0
    for ref in parts:
        h, l = split(ref[...])
        high[:, at : at + ref.shape[1]] = h
        low[:, at : at + ref.shape[1]] = l
        at += ref.shape[1]
    for pair in range(out.shape[1] // PAIR):
        begin = (pair - 1) * PAIR
        skip = max(0, -begin)
        stop = min(at, begin + SPAN)
        ext = slice(begin + skip, stop)
        band = slice(skip, stop - begin)
        out[:, pair * PAIR : (pair + 1) * PAIR] = dot3(
            high[:, ext], low[:, ext], band_high[pair, band], band_low[pair, band]
        )


def apply_cols(parts, bands, width):
    rows = parts[0].shape[0]
    ext = pltpu.VMEM((rows, sum(p.shape[1] for p in parts)), jnp.bfloat16)
    args = [held(a) for a in (*parts, *bands)]
    return pl.pallas_call(
        cols_kernel,
        out_shape=jax.ShapeDtypeStruct((rows, width), jnp.float32),
        in_specs=[VMEM_SPEC] * len(args),
        out_specs=VMEM_SPEC,
        scratch_shapes=[ext, ext],
        compiler_params=pltpu.CompilerParams(vmem_limit_bytes=32 << 20),
        name="cols",
    )(*args)


def tail_kernel(pair, band_rows, side, band_high, band_low, part, out):
    h, l = split(side[...])
    out[...] = part[...] + dot3(h, l, band_high[pair, band_rows], band_low[pair, band_rows])


def apply_tail(side, bands, part, pair, band_rows):
    rows, width = part.shape
    block = pl.BlockSpec((rows, PAIR), lambda i: (0, pair))
    args = [held(a) for a in (side, *bands)]
    return pl.pallas_call(
        functools.partial(tail_kernel, pair, band_rows),
        grid=(1,),
        out_shape=jax.ShapeDtypeStruct((rows, width), jnp.float32),
        in_specs=[VMEM_SPEC] * 3 + [block],
        out_specs=block,
        input_output_aliases={3: 0},
        compiler_params=pltpu.CompilerParams(vmem_limit_bytes=16 << 20),
        name="tail",
    )(*args, part)


def body(
    covariance, latitude_offset, longitude_offset, upwind, courant,
    longitude_diffusion, latitude_diffusion,
):
    block = covariance[0]
    rows, width = block.shape
    row_count, col_count = lax.axis_size("row"), lax.axis_size("col")
    forward = lambda n: [(i, i + 1) for i in range(n - 1)]
    backward = lambda n: [(i + 1, i) for i in range(n - 1)]

    chip_pairs = [(i, i ^ 1) for i in range(row_count)]
    cross_pairs = [((i + 1 ^ 1) - 1, i) for i in range(1, row_count - 1)]

    fields = [
        a.reshape(NLAT, NLON)
        for a in (
            latitude_offset, longitude_offset, upwind, courant,
            longitude_diffusion, latitude_diffusion,
        )
    ]
    lat_row = (lax.axis_index("row") * (rows // NLON)).astype(jnp.int32).reshape(1)
    lat_col = (lax.axis_index("col") * (width // NLON)).astype(jnp.int32).reshape(1)

    starts = (0, width - PAIR, PAIR, width - 2 * PAIR)
    chip = lax.ppermute(block, "row", chip_pairs)
    (own0,) = take_columns(block, [(0, PAIR)])
    own1, own2 = take_columns(block, [(width - PAIR, width), (PAIR, width - PAIR)])
    across0, across1, across2 = (
        lax.ppermute(x, "row", cross_pairs) for x in (own0, own1, own2)
    )
    across = (across0, across1, across2, across2)
    offset = (0, 0, 0, width - 3 * PAIR)
    row_bands = build_bands(lat_row, fields, rows // PAIR, True)
    half, side = [], []
    for k in range(4):
        sources = [block, chip, across[k]]
        begins = [starts[k], starts[k], offset[k]]
        half.append(apply_rows(lat_row, PAIR, sources, begins, row_bands))
        pairs = forward(col_count) if k % 2 else backward(col_count)
        side.append(lax.ppermute(half[k], "col", pairs))
    col_bands = build_bands(lat_col, fields, width // PAIR, False)
    parts = [side[1], half[0], half[2], half[3], half[1], side[0]]
    part = apply_cols(parts, col_bands, width)
    pairs = width // PAIR
    part = apply_tail(side[2], col_bands, part, pairs - 1, slice(SPAN - PAIR, SPAN))
    return apply_tail(side[3], col_bands, part, 0, slice(0, PAIR))[None]


def solution(mesh):
    in_specs = (P(None, "row", "col"), P(), P(), P(), P(), P(), P())
    out_specs = P(None, "row", "col")
    return jax.shard_map(body, mesh=mesh, in_specs=in_specs, out_specs=out_specs, check_vma=False)
```

```python
import functools

import jax
import jax.numpy as jnp
from jax import lax
from jax.experimental import pallas as pl
from jax.experimental.pallas import tpu as pltpu
from jax.sharding import PartitionSpec as P


NLAT = 64
NLON = 128
HALO = 4
SPAN = 10 * NLON
PAIR = 2 * NLON


def split(x):
    high = x.astype(jnp.bfloat16)
    low = (x - high.astype(jnp.float32)).astype(jnp.bfloat16)
    return high, low


def dot3(a_high, a_low, b_high, b_low):
    dot = functools.partial(jnp.dot, preferred_element_type=jnp.float32)
    return dot(a_high, b_high) + (dot(a_high, b_low) + dot(a_low, b_high))


def band_kernel(
    transposed, place, lat_off, lon_off, upwind, courant, lon_diff, lat_diff,
    high, low, depart_lat, depart_lon, near_lat, near_lon, hot,
):
    shape = (NLAT, NLON)
    lat = lax.broadcasted_iota(jnp.int32, shape, 0)
    lon = lax.broadcasted_iota(jnp.int32, shape, 1)
    up = upwind[...]
    one = jnp.ones(shape, jnp.int32)
    zero = jnp.zeros(shape, jnp.int32)
    d_lat = jnp.clip(lat + lat_off[...], 0, NLAT - 1)
    d_lon = (lon + lon_off[...]) & (NLON - 1)
    depart_lat[...] = d_lat
    depart_lon[...] = d_lon
    near_lat[...] = jnp.clip(
        d_lat + jnp.where(up == 2, one, zero) - jnp.where(up == 3, one, zero), 0, NLAT - 1
    )
    near_lon[...] = (
        d_lon + jnp.where(up == 0, one, zero) - jnp.where(up == 1, one, zero)
    ) & (NLON - 1)

    sub = lax.broadcasted_iota(jnp.int32, (NLON, NLON), 0)
    first = place[0]
    pairs = high.shape[0]

    def put(pair, half, t, value):
        if transposed:
            value = value.T
        h, l = split(value)
        cells = pl.ds(t * NLON, NLON)
        cols = pl.ds(half * NLON, NLON)
        at = (pair, cols, cells) if transposed else (pair, cells, cols)
        high[at] = h
        low[at] = l

    def fill(pair, half):
        y = first + 2 * pair + half
        lx = lon_diff[pl.ds(y, 1), :]
        ly = lat_diff[pl.ds(y, 1), :]
        core = 1.0 - 2.0 * lx - 2.0 * ly
        none = jnp.zeros_like(lx)
        reach = ((0, 0), (0, 1), (-1, 0))
        rows = (y, jnp.minimum(y + 1, NLAT - 1), jnp.maximum(y - 1, 0))
        rows = [pl.ds(r, 1) for r in rows]
        for k, row in enumerate(rows):
            on = jnp.ones((NLON, NLON), jnp.float32)
            off = jnp.zeros((NLON, NLON), jnp.float32)
            hot[2 * k] = jnp.where(sub == depart_lon[row, :], on, off)
            hot[2 * k + 1] = jnp.where(sub == near_lon[row, :], on, off)
        for t in range(2 * HALO + 1):
            far = t - HALO
            in_lat = y + far
            value = None
            for k, row in enumerate(rows):
                w = courant[row, :]
                below, above = reach[k]
                scale = ly if k else jnp.ones_like(lx)
                terms = []
                if -2 + below <= far <= 2 + above:
                    keep = jnp.where(depart_lat[row, :] == in_lat, scale * (1.0 - w), none)
                    terms.append(keep * hot[2 * k])
                if -3 + below <= far <= 3 + above:
                    take = jnp.where(near_lat[row, :] == in_lat, scale * w, none)
                    terms.append(take * hot[2 * k + 1])
                if not terms:
                    continue
                total = sum(terms[1:], terms[0])
                if k == 0:
                    beside = pltpu.roll(total, 1, 1) + pltpu.roll(total, NLON - 1, 1)
                    total = core * total + lx * beside
                value = total if value is None else value + total
            put(pair, half, t + half, value)
        put(pair, half, 0 if half else 2 * HALO + 1, jnp.zeros((NLON, NLON), jnp.float32))

    def step(pair, carry):
        fill(pair, 0)
        fill(pair, 1)
        return carry

    lax.fori_loop(0, pairs, step, 0)


VMEM_SPEC = pl.BlockSpec(memory_space=pltpu.VMEM)


def held(x):
    return pltpu.with_memory_space_constraint(x, pltpu.VMEM)


def in_hbm(x):
    return pltpu.with_memory_space_constraint(x, pltpu.HBM)


def build_bands(place, fields, pairs, transposed):
    shape = (pairs, PAIR, SPAN) if transposed else (pairs, SPAN, PAIR)
    band = pltpu.VMEM(shape, jnp.bfloat16)
    return pl.pallas_call(
        functools.partial(band_kernel, transposed),
        out_shape=(band, band),
        in_specs=[pl.BlockSpec(memory_space=pltpu.SMEM)] + [VMEM_SPEC] * 6,
        out_specs=(VMEM_SPEC,) * 2,
        scratch_shapes=[pltpu.VMEM((NLAT, NLON), jnp.int32)] * 4
        + [pltpu.VMEM((6, NLON, NLON), jnp.float32)],
        compiler_params=pltpu.CompilerParams(vmem_limit_bytes=24 << 20),
        name="row_bands" if transposed else "col_bands",
    )(place, *fields)


def take_kernel(starts, source, *refs):
    outs, sems = refs[:-1], refs[-1]
    count = sems.shape[1]
    piece = source.shape[0] // count
    copies = []
    for i, (at, out) in enumerate(zip(starts, outs)):
        for j in range(count):
            rows = pl.ds(j * piece, piece)
            copies.append(
                pltpu.make_async_copy(
                    source.at[rows, pl.ds(at, out.shape[1])], out.at[rows], sems.at[i, j]
                )
            )
    for copy in copies:
        copy.start()
    for copy in copies:
        copy.wait()


def take_columns(source, ranges):
    rows = source.shape[0]
    starts = [start for start, _ in ranges]
    return pl.pallas_call(
        functools.partial(take_kernel, starts),
        out_shape=tuple(pltpu.VMEM((rows, stop - start), jnp.float32) for start, stop in ranges),
        in_specs=[pl.BlockSpec(memory_space=pltpu.HBM)],
        out_specs=(VMEM_SPEC,) * len(ranges),
        scratch_shapes=[pltpu.SemaphoreType.DMA((len(ranges), 4))],
        compiler_params=pltpu.CompilerParams(vmem_limit_bytes=8 << 20),
        name="take",
    )(in_hbm(source))


def rows_kernel(starts, place, *refs):
    *sources, band_high, band_low, out, high, low, landed, sems = refs
    rows, width = out.shape
    copies = [
        pltpu.make_async_copy(ref.at[:, pl.ds(start, width)], landed.at[i], sems.at[i])
        for i, (start, ref) in enumerate(zip(starts, sources))
    ]
    for copy in copies:
        copy.start()
    odd = (place[0] // HALO) & 1
    to_chip = pl.multiple_of((1 - odd) * 2 * rows, rows)
    to_cross = pl.multiple_of(odd * 2 * rows, rows)

    def put(value, at):
        h, l = split(value)
        high[pl.ds(at, rows), :] = h
        low[pl.ds(at, rows), :] = l

    copies[0].wait()
    put(landed[0], rows)
    copies[1].wait()
    put(landed[1], to_chip)
    for copy in copies[2:]:
        copy.wait()
    put(sum((landed[i] for i in range(3, len(copies))), landed[2]), to_cross)
    for pair in range(rows // PAIR):
        at = pair * PAIR
        out[at : at + PAIR, :] = dot3(
            band_high[pair], band_low[pair], high[at : at + SPAN, :], low[at : at + SPAN, :]
        )


def apply_rows(place, width, sources, starts, bands):
    rows = sources[0].shape[0]
    ext = pltpu.VMEM((3 * rows, width), jnp.bfloat16)
    hbm = [in_hbm(a) for a in sources]
    landed = pltpu.VMEM((len(hbm), rows, width), jnp.float32)
    return pl.pallas_call(
        functools.partial(rows_kernel, starts),
        out_shape=pltpu.VMEM((rows, width), jnp.float32),
        in_specs=[pl.BlockSpec(memory_space=pltpu.SMEM)]
        + [pl.BlockSpec(memory_space=pltpu.HBM)] * len(hbm)
        + [VMEM_SPEC] * 2,
        out_specs=VMEM_SPEC,
        scratch_shapes=[ext, ext, landed, pltpu.SemaphoreType.DMA((len(hbm),))],
        compiler_params=pltpu.CompilerParams(vmem_limit_bytes=16 << 20),
        name="rows",
    )(place, *hbm, *(held(a) for a in bands))


def cols_kernel(*refs):
    parts = refs[:-5]
    band_high, band_low, out, high, low = refs[-5:]
    at = 0
    for ref in parts:
        h, l = split(ref[...])
        high[:, at : at + ref.shape[1]] = h
        low[:, at : at + ref.shape[1]] = l
        at += ref.shape[1]
    for pair in range(out.shape[1] // PAIR):
        begin = (pair - 1) * PAIR
        skip = max(0, -begin)
        stop = min(at, begin + SPAN)
        ext = slice(begin + skip, stop)
        band = slice(skip, stop - begin)
        out[:, pair * PAIR : (pair + 1) * PAIR] = dot3(
            high[:, ext], low[:, ext], band_high[pair, band], band_low[pair, band]
        )


def apply_cols(parts, bands, width):
    rows = parts[0].shape[0]
    ext = pltpu.VMEM((rows, sum(p.shape[1] for p in parts)), jnp.bfloat16)
    args = [held(a) for a in (*parts, *bands)]
    return pl.pallas_call(
        cols_kernel,
        out_shape=jax.ShapeDtypeStruct((rows, width), jnp.float32),
        in_specs=[VMEM_SPEC] * len(args),
        out_specs=VMEM_SPEC,
        scratch_shapes=[ext, ext],
        compiler_params=pltpu.CompilerParams(vmem_limit_bytes=32 << 20),
        name="cols",
    )(*args)


def tail_kernel(pair, band_rows, side, band_high, band_low, part, out):
    h, l = split(side[...])
    out[...] = part[...] + dot3(h, l, band_high[pair, band_rows], band_low[pair, band_rows])


def apply_tail(side, bands, part, pair, band_rows):
    rows, width = part.shape
    block = pl.BlockSpec((rows, PAIR), lambda i: (0, pair))
    args = [held(a) for a in (side, *bands)]
    return pl.pallas_call(
        functools.partial(tail_kernel, pair, band_rows),
        grid=(1,),
        out_shape=jax.ShapeDtypeStruct((rows, width), jnp.float32),
        in_specs=[VMEM_SPEC] * 3 + [block],
        out_specs=block,
        input_output_aliases={3: 0},
        compiler_params=pltpu.CompilerParams(vmem_limit_bytes=16 << 20),
        name="tail",
    )(*args, part)


def body(
    covariance, latitude_offset, longitude_offset, upwind, courant,
    longitude_diffusion, latitude_diffusion,
):
    block = covariance[0]
    rows, width = block.shape
    row_count, col_count = lax.axis_size("row"), lax.axis_size("col")
    forward = lambda n: [(i, i + 1) for i in range(n - 1)]
    backward = lambda n: [(i + 1, i) for i in range(n - 1)]

    chip_pairs = [(i, i ^ 1) for i in range(row_count)]
    cross_pairs = [((i + 1 ^ 1) - 1, i) for i in range(1, row_count - 1)]
    middle = row_count // 2
    middle_pairs = [(middle - 1, middle), (middle, middle - 1)]
    other_pairs = [pair for pair in cross_pairs if pair not in middle_pairs]

    fields = [
        a.reshape(NLAT, NLON)
        for a in (
            latitude_offset, longitude_offset, upwind, courant,
            longitude_diffusion, latitude_diffusion,
        )
    ]
    lat_row = (lax.axis_index("row") * (rows // NLON)).astype(jnp.int32).reshape(1)
    lat_col = (lax.axis_index("col") * (width // NLON)).astype(jnp.int32).reshape(1)

    starts = (0, width - PAIR, PAIR, width - 2 * PAIR)
    chip = lax.ppermute(block, "row", chip_pairs)
    (own0,) = take_columns(block, [(0, PAIR)])
    own1, own2 = take_columns(block, [(width - PAIR, width), (PAIR, width - PAIR)])
    across0 = lax.ppermute(own0, "row", cross_pairs)
    across1 = lax.ppermute(own1, "row", cross_pairs)
    across2 = [lax.ppermute(own2, "row", middle_pairs), lax.ppermute(own2, "row", other_pairs)]
    across = ([across0], [across1], across2, across2)
    offset = (0, 0, 0, width - 3 * PAIR)
    row_bands = build_bands(lat_row, fields, rows // PAIR, True)
    half, side = [], []
    for k in range(4):
        sources = [block, chip] + across[k]
        begins = [starts[k]] * 2 + [offset[k]] * len(across[k])
        half.append(apply_rows(lat_row, PAIR, sources, begins, row_bands))
        pairs = forward(col_count) if k % 2 else backward(col_count)
        side.append(lax.ppermute(half[k], "col", pairs))
    col_bands = build_bands(lat_col, fields, width // PAIR, False)
    parts = [side[1], half[0], half[2], half[3], half[1], side[0]]
    part = apply_cols(parts, col_bands, width)
    pairs = width // PAIR
    part = apply_tail(side[2], col_bands, part, pairs - 1, slice(SPAN - PAIR, SPAN))
    return apply_tail(side[3], col_bands, part, 0, slice(0, PAIR))[None]


def solution(mesh):
    in_specs = (P(None, "row", "col"), P(), P(), P(), P(), P(), P())
    out_specs = P(None, "row", "col")
    return jax.shard_map(body, mesh=mesh, in_specs=in_specs, out_specs=out_specs, check_vma=False)
```

```python
import functools

import jax
import jax.numpy as jnp
from jax import lax
from jax.experimental import pallas as pl
from jax.experimental.pallas import tpu as pltpu
from jax.sharding import PartitionSpec as P


NLAT = 64
NLON = 128
HALO = 4
SPAN = 10 * NLON
PAIR = 2 * NLON


def split(x):
    high = x.astype(jnp.bfloat16)
    low = (x - high.astype(jnp.float32)).astype(jnp.bfloat16)
    return high, low


def dot3(a_high, a_low, b_high, b_low):
    dot = functools.partial(jnp.dot, preferred_element_type=jnp.float32)
    return dot(a_high, b_high) + (dot(a_high, b_low) + dot(a_low, b_high))


def band_kernel(
    transposed, place, lat_off, lon_off, upwind, courant, lon_diff, lat_diff,
    high, low, depart_lat, depart_lon, near_lat, near_lon, hot,
):
    shape = (NLAT, NLON)
    lat = lax.broadcasted_iota(jnp.int32, shape, 0)
    lon = lax.broadcasted_iota(jnp.int32, shape, 1)
    up = upwind[...]
    one = jnp.ones(shape, jnp.int32)
    zero = jnp.zeros(shape, jnp.int32)
    d_lat = jnp.clip(lat + lat_off[...], 0, NLAT - 1)
    d_lon = (lon + lon_off[...]) & (NLON - 1)
    depart_lat[...] = d_lat
    depart_lon[...] = d_lon
    near_lat[...] = jnp.clip(
        d_lat + jnp.where(up == 2, one, zero) - jnp.where(up == 3, one, zero), 0, NLAT - 1
    )
    near_lon[...] = (
        d_lon + jnp.where(up == 0, one, zero) - jnp.where(up == 1, one, zero)
    ) & (NLON - 1)

    sub = lax.broadcasted_iota(jnp.int32, (NLON, NLON), 0)
    first = place[0]
    pairs = high.shape[0]

    def put(pair, half, t, value):
        if transposed:
            value = value.T
        h, l = split(value)
        cells = pl.ds(t * NLON, NLON)
        cols = pl.ds(half * NLON, NLON)
        at = (pair, cols, cells) if transposed else (pair, cells, cols)
        high[at] = h
        low[at] = l

    def fill(pair, half):
        y = first + 2 * pair + half
        lx = lon_diff[pl.ds(y, 1), :]
        ly = lat_diff[pl.ds(y, 1), :]
        core = 1.0 - 2.0 * lx - 2.0 * ly
        none = jnp.zeros_like(lx)
        reach = ((0, 0), (0, 1), (-1, 0))
        rows = (y, jnp.minimum(y + 1, NLAT - 1), jnp.maximum(y - 1, 0))
        rows = [pl.ds(r, 1) for r in rows]
        for k, row in enumerate(rows):
            on = jnp.ones((NLON, NLON), jnp.float32)
            off = jnp.zeros((NLON, NLON), jnp.float32)
            hot[2 * k] = jnp.where(sub == depart_lon[row, :], on, off)
            hot[2 * k + 1] = jnp.where(sub == near_lon[row, :], on, off)
        for t in range(2 * HALO + 1):
            far = t - HALO
            in_lat = y + far
            value = None
            for k, row in enumerate(rows):
                w = courant[row, :]
                below, above = reach[k]
                scale = ly if k else jnp.ones_like(lx)
                terms = []
                if -2 + below <= far <= 2 + above:
                    keep = jnp.where(depart_lat[row, :] == in_lat, scale * (1.0 - w), none)
                    terms.append(keep * hot[2 * k])
                if -3 + below <= far <= 3 + above:
                    take = jnp.where(near_lat[row, :] == in_lat, scale * w, none)
                    terms.append(take * hot[2 * k + 1])
                if not terms:
                    continue
                total = sum(terms[1:], terms[0])
                if k == 0:
                    beside = pltpu.roll(total, 1, 1) + pltpu.roll(total, NLON - 1, 1)
                    total = core * total + lx * beside
                value = total if value is None else value + total
            put(pair, half, t + half, value)
        put(pair, half, 0 if half else 2 * HALO + 1, jnp.zeros((NLON, NLON), jnp.float32))

    def step(pair, carry):
        fill(pair, 0)
        fill(pair, 1)
        return carry

    lax.fori_loop(0, pairs, step, 0)


VMEM_SPEC = pl.BlockSpec(memory_space=pltpu.VMEM)


def held(x):
    return pltpu.with_memory_space_constraint(x, pltpu.VMEM)


def in_hbm(x):
    return pltpu.with_memory_space_constraint(x, pltpu.HBM)


def build_bands(place, fields, pairs, transposed):
    shape = (pairs, PAIR, SPAN) if transposed else (pairs, SPAN, PAIR)
    band = pltpu.VMEM(shape, jnp.bfloat16)
    return pl.pallas_call(
        functools.partial(band_kernel, transposed),
        out_shape=(band, band),
        in_specs=[pl.BlockSpec(memory_space=pltpu.SMEM)] + [VMEM_SPEC] * 6,
        out_specs=(VMEM_SPEC,) * 2,
        scratch_shapes=[pltpu.VMEM((NLAT, NLON), jnp.int32)] * 4
        + [pltpu.VMEM((6, NLON, NLON), jnp.float32)],
        compiler_params=pltpu.CompilerParams(vmem_limit_bytes=24 << 20),
        name="row_bands" if transposed else "col_bands",
    )(place, *fields)


def take_kernel(starts, source, *refs):
    outs, sems = refs[:-1], refs[-1]
    count = sems.shape[1]
    piece = source.shape[0] // count
    copies = []
    for i, (at, out) in enumerate(zip(starts, outs)):
        for j in range(count):
            rows = pl.ds(j * piece, piece)
            copies.append(
                pltpu.make_async_copy(
                    source.at[rows, pl.ds(at, out.shape[1])], out.at[rows], sems.at[i, j]
                )
            )
    for copy in copies:
        copy.start()
    for copy in copies:
        copy.wait()


def take_columns(source, ranges):
    rows = source.shape[0]
    starts = [start for start, _ in ranges]
    return pl.pallas_call(
        functools.partial(take_kernel, starts),
        out_shape=tuple(pltpu.VMEM((rows, stop - start), jnp.float32) for start, stop in ranges),
        in_specs=[pl.BlockSpec(memory_space=pltpu.HBM)],
        out_specs=(VMEM_SPEC,) * len(ranges),
        scratch_shapes=[pltpu.SemaphoreType.DMA((len(ranges), 4))],
        compiler_params=pltpu.CompilerParams(vmem_limit_bytes=8 << 20),
        name="take",
    )(in_hbm(source))


def rows_kernel(starts, place, *refs):
    *sources, band_high, band_low, out, high, low, landed, sems = refs
    rows, width = out.shape
    copies = [
        pltpu.make_async_copy(ref.at[:, pl.ds(start, width)], landed.at[i], sems.at[i])
        for i, (start, ref) in enumerate(zip(starts, sources))
    ]
    for copy in copies:
        copy.start()
    odd = (place[0] // HALO) & 1
    to_chip = pl.multiple_of((1 - odd) * 2 * rows, rows)
    to_cross = pl.multiple_of(odd * 2 * rows, rows)

    def put(value, at):
        h, l = split(value)
        high[pl.ds(at, rows), :] = h
        low[pl.ds(at, rows), :] = l

    copies[0].wait()
    put(landed[0], rows)
    copies[1].wait()
    put(landed[1], to_chip)
    for copy in copies[2:]:
        copy.wait()
    put(sum((landed[i] for i in range(3, len(copies))), landed[2]), to_cross)
    for pair in range(rows // PAIR):
        at = pair * PAIR
        out[at : at + PAIR, :] = dot3(
            band_high[pair], band_low[pair], high[at : at + SPAN, :], low[at : at + SPAN, :]
        )


def apply_rows(place, width, sources, starts, bands):
    rows = sources[0].shape[0]
    ext = pltpu.VMEM((3 * rows, width), jnp.bfloat16)
    hbm = [in_hbm(a) for a in sources]
    landed = pltpu.VMEM((len(hbm), rows, width), jnp.float32)
    return pl.pallas_call(
        functools.partial(rows_kernel, starts),
        out_shape=pltpu.VMEM((rows, width), jnp.float32),
        in_specs=[pl.BlockSpec(memory_space=pltpu.SMEM)]
        + [pl.BlockSpec(memory_space=pltpu.HBM)] * len(hbm)
        + [VMEM_SPEC] * 2,
        out_specs=VMEM_SPEC,
        scratch_shapes=[ext, ext, landed, pltpu.SemaphoreType.DMA((len(hbm),))],
        compiler_params=pltpu.CompilerParams(vmem_limit_bytes=16 << 20),
        name="rows",
    )(place, *hbm, *(held(a) for a in bands))


def cols_kernel(*refs):
    parts = refs[:-5]
    band_high, band_low, out, high, low = refs[-5:]
    at = 0
    for ref in parts:
        h, l = split(ref[...])
        high[:, at : at + ref.shape[1]] = h
        low[:, at : at + ref.shape[1]] = l
        at += ref.shape[1]
    for pair in range(out.shape[1] // PAIR):
        begin = (pair - 1) * PAIR
        skip = max(0, -begin)
        stop = min(at, begin + SPAN)
        ext = slice(begin + skip, stop)
        band = slice(skip, stop - begin)
        out[:, pair * PAIR : (pair + 1) * PAIR] = dot3(
            high[:, ext], low[:, ext], band_high[pair, band], band_low[pair, band]
        )


def apply_cols(parts, bands, width):
    rows = parts[0].shape[0]
    ext = pltpu.VMEM((rows, sum(p.shape[1] for p in parts)), jnp.bfloat16)
    args = [held(a) for a in (*parts, *bands)]
    return pl.pallas_call(
        cols_kernel,
        out_shape=jax.ShapeDtypeStruct((rows, width), jnp.float32),
        in_specs=[VMEM_SPEC] * len(args),
        out_specs=VMEM_SPEC,
        scratch_shapes=[ext, ext],
        compiler_params=pltpu.CompilerParams(vmem_limit_bytes=32 << 20),
        name="cols",
    )(*args)


def tail_kernel(pair, band_rows, side, band_high, band_low, part, out):
    h, l = split(side[...])
    out[...] = part[...] + dot3(h, l, band_high[pair, band_rows], band_low[pair, band_rows])


def apply_tail(side, bands, part, pair, band_rows):
    rows, width = part.shape
    block = pl.BlockSpec((rows, PAIR), lambda i: (0, pair))
    args = [held(a) for a in (side, *bands)]
    return pl.pallas_call(
        functools.partial(tail_kernel, pair, band_rows),
        grid=(1,),
        out_shape=jax.ShapeDtypeStruct((rows, width), jnp.float32),
        in_specs=[VMEM_SPEC] * 3 + [block],
        out_specs=block,
        input_output_aliases={3: 0},
        compiler_params=pltpu.CompilerParams(vmem_limit_bytes=16 << 20),
        name="tail",
    )(*args, part)


def body(
    covariance, latitude_offset, longitude_offset, upwind, courant,
    longitude_diffusion, latitude_diffusion,
):
    block = covariance[0]
    rows, width = block.shape
    row_count, col_count = lax.axis_size("row"), lax.axis_size("col")
    forward = lambda n: [(i, i + 1) for i in range(n - 1)]
    backward = lambda n: [(i + 1, i) for i in range(n - 1)]

    chip_pairs = [(i, i ^ 1) for i in range(row_count)]
    cross_pairs = [((i + 1 ^ 1) - 1, i) for i in range(1, row_count - 1)]
    copy_pairs = [(source ^ 1, target) for source, target in cross_pairs]

    fields = [
        a.reshape(NLAT, NLON)
        for a in (
            latitude_offset, longitude_offset, upwind, courant,
            longitude_diffusion, latitude_diffusion,
        )
    ]
    lat_row = (lax.axis_index("row") * (rows // NLON)).astype(jnp.int32).reshape(1)
    lat_col = (lax.axis_index("col") * (width // NLON)).astype(jnp.int32).reshape(1)

    starts = (0, width - PAIR, PAIR, width - 2 * PAIR)
    chip = lax.ppermute(block, "row", chip_pairs)
    (own0,) = take_columns(block, [(0, PAIR)])
    (own1,) = take_columns(block, [(width - PAIR, width)])
    (copy2,) = take_columns(chip, [(PAIR, width - PAIR)])
    across0 = lax.ppermute(own0, "row", cross_pairs)
    across1 = lax.ppermute(own1, "row", cross_pairs)
    across2 = lax.ppermute(copy2, "row", copy_pairs)
    across = (across0, across1, across2, across2)
    offset = (0, 0, 0, width - 3 * PAIR)
    row_bands = build_bands(lat_row, fields, rows // PAIR, True)
    half, side = [], []
    for k in range(4):
        sources = [block, chip, across[k]]
        begins = [starts[k], starts[k], offset[k]]
        half.append(apply_rows(lat_row, PAIR, sources, begins, row_bands))
        pairs = forward(col_count) if k % 2 else backward(col_count)
        side.append(lax.ppermute(half[k], "col", pairs))
    col_bands = build_bands(lat_col, fields, width // PAIR, False)
    parts = [side[1], half[0], half[2], half[3], half[1], side[0]]
    part = apply_cols(parts, col_bands, width)
    pairs = width // PAIR
    part = apply_tail(side[2], col_bands, part, pairs - 1, slice(SPAN - PAIR, SPAN))
    return apply_tail(side[3], col_bands, part, 0, slice(0, PAIR))[None]


def solution(mesh):
    in_specs = (P(None, "row", "col"), P(), P(), P(), P(), P(), P())
    out_specs = P(None, "row", "col")
    return jax.shard_map(body, mesh=mesh, in_specs=in_specs, out_specs=out_specs, check_vma=False)
```

```python
import functools

import jax
import jax.numpy as jnp
from jax import lax
from jax.experimental import pallas as pl
from jax.experimental.pallas import tpu as pltpu
from jax.sharding import PartitionSpec as P


NLAT = 64
NLON = 128
HALO = 4
SPAN = 10 * NLON
PAIR = 2 * NLON


def split(x):
    high = x.astype(jnp.bfloat16)
    low = (x - high.astype(jnp.float32)).astype(jnp.bfloat16)
    return high, low


def dot3(a_high, a_low, b_high, b_low):
    dot = functools.partial(jnp.dot, preferred_element_type=jnp.float32)
    return dot(a_high, b_high) + (dot(a_high, b_low) + dot(a_low, b_high))


def band_kernel(
    transposed, place, lat_off, lon_off, upwind, courant, lon_diff, lat_diff,
    high, low, depart_lat, depart_lon, near_lat, near_lon, hot,
):
    shape = (NLAT, NLON)
    lat = lax.broadcasted_iota(jnp.int32, shape, 0)
    lon = lax.broadcasted_iota(jnp.int32, shape, 1)
    up = upwind[...]
    one = jnp.ones(shape, jnp.int32)
    zero = jnp.zeros(shape, jnp.int32)
    d_lat = jnp.clip(lat + lat_off[...], 0, NLAT - 1)
    d_lon = (lon + lon_off[...]) & (NLON - 1)
    depart_lat[...] = d_lat
    depart_lon[...] = d_lon
    near_lat[...] = jnp.clip(
        d_lat + jnp.where(up == 2, one, zero) - jnp.where(up == 3, one, zero), 0, NLAT - 1
    )
    near_lon[...] = (
        d_lon + jnp.where(up == 0, one, zero) - jnp.where(up == 1, one, zero)
    ) & (NLON - 1)

    sub = lax.broadcasted_iota(jnp.int32, (NLON, NLON), 0)
    first = place[0]
    pairs = high.shape[0]

    def put(pair, half, t, value):
        if transposed:
            value = value.T
        h, l = split(value)
        cells = pl.ds(t * NLON, NLON)
        cols = pl.ds(half * NLON, NLON)
        at = (pair, cols, cells) if transposed else (pair, cells, cols)
        high[at] = h
        low[at] = l

    def fill(pair, half):
        y = first + 2 * pair + half
        lx = lon_diff[pl.ds(y, 1), :]
        ly = lat_diff[pl.ds(y, 1), :]
        core = 1.0 - 2.0 * lx - 2.0 * ly
        none = jnp.zeros_like(lx)
        reach = ((0, 0), (0, 1), (-1, 0))
        rows = (y, jnp.minimum(y + 1, NLAT - 1), jnp.maximum(y - 1, 0))
        rows = [pl.ds(r, 1) for r in rows]
        for k, row in enumerate(rows):
            on = jnp.ones((NLON, NLON), jnp.float32)
            off = jnp.zeros((NLON, NLON), jnp.float32)
            hot[2 * k] = jnp.where(sub == depart_lon[row, :], on, off)
            hot[2 * k + 1] = jnp.where(sub == near_lon[row, :], on, off)
        for t in range(2 * HALO + 1):
            far = t - HALO
            in_lat = y + far
            value = None
            for k, row in enumerate(rows):
                w = courant[row, :]
                below, above = reach[k]
                scale = ly if k else jnp.ones_like(lx)
                terms = []
                if -2 + below <= far <= 2 + above:
                    keep = jnp.where(depart_lat[row, :] == in_lat, scale * (1.0 - w), none)
                    terms.append(keep * hot[2 * k])
                if -3 + below <= far <= 3 + above:
                    take = jnp.where(near_lat[row, :] == in_lat, scale * w, none)
                    terms.append(take * hot[2 * k + 1])
                if not terms:
                    continue
                total = sum(terms[1:], terms[0])
                if k == 0:
                    beside = pltpu.roll(total, 1, 1) + pltpu.roll(total, NLON - 1, 1)
                    total = core * total + lx * beside
                value = total if value is None else value + total
            put(pair, half, t + half, value)
        put(pair, half, 0 if half else 2 * HALO + 1, jnp.zeros((NLON, NLON), jnp.float32))

    def step(pair, carry):
        fill(pair, 0)
        fill(pair, 1)
        return carry

    lax.fori_loop(0, pairs, step, 0)


VMEM_SPEC = pl.BlockSpec(memory_space=pltpu.VMEM)


def held(x):
    return pltpu.with_memory_space_constraint(x, pltpu.VMEM)


def in_hbm(x):
    return pltpu.with_memory_space_constraint(x, pltpu.HBM)


def build_bands(place, fields, pairs, transposed):
    shape = (pairs, PAIR, SPAN) if transposed else (pairs, SPAN, PAIR)
    band = pltpu.VMEM(shape, jnp.bfloat16)
    return pl.pallas_call(
        functools.partial(band_kernel, transposed),
        out_shape=(band, band),
        in_specs=[pl.BlockSpec(memory_space=pltpu.SMEM)] + [VMEM_SPEC] * 6,
        out_specs=(VMEM_SPEC,) * 2,
        scratch_shapes=[pltpu.VMEM((NLAT, NLON), jnp.int32)] * 4
        + [pltpu.VMEM((6, NLON, NLON), jnp.float32)],
        compiler_params=pltpu.CompilerParams(vmem_limit_bytes=24 << 20),
        name="row_bands" if transposed else "col_bands",
    )(place, *fields)


def take_kernel(starts, source, *refs):
    outs, sems = refs[:-1], refs[-1]
    count = sems.shape[1]
    piece = source.shape[0] // count
    copies = []
    for i, (at, out) in enumerate(zip(starts, outs)):
        for j in range(count):
            rows = pl.ds(j * piece, piece)
            copies.append(
                pltpu.make_async_copy(
                    source.at[rows, pl.ds(at, out.shape[1])], out.at[rows], sems.at[i, j]
                )
            )
    for copy in copies:
        copy.start()
    for copy in copies:
        copy.wait()


def take_columns(source, space, ranges):
    rows = source.shape[0]
    starts = [start for start, _ in ranges]
    return pl.pallas_call(
        functools.partial(take_kernel, starts),
        out_shape=tuple(pltpu.VMEM((rows, stop - start), jnp.float32) for start, stop in ranges),
        in_specs=[pl.BlockSpec(memory_space=space)],
        out_specs=(VMEM_SPEC,) * len(ranges),
        scratch_shapes=[pltpu.SemaphoreType.DMA((len(ranges), 4))],
        compiler_params=pltpu.CompilerParams(vmem_limit_bytes=8 << 20),
        name="take",
    )(source)


def rows_kernel(starts, place, *refs):
    *sources, band_high, band_low, out, high, low, landed, sems = refs
    rows, width = out.shape
    copies = [
        pltpu.make_async_copy(ref.at[:, pl.ds(start, width)], landed.at[i], sems.at[i])
        for i, (start, ref) in enumerate(zip(starts, sources))
    ]
    for copy in copies:
        copy.start()
    odd = (place[0] // HALO) & 1
    to_chip = pl.multiple_of((1 - odd) * 2 * rows, rows)
    to_cross = pl.multiple_of(odd * 2 * rows, rows)

    def put(value, at):
        h, l = split(value)
        high[pl.ds(at, rows), :] = h
        low[pl.ds(at, rows), :] = l

    copies[0].wait()
    put(landed[0], rows)
    copies[1].wait()
    put(landed[1], to_chip)
    for copy in copies[2:]:
        copy.wait()
    put(sum((landed[i] for i in range(3, len(copies))), landed[2]), to_cross)
    for pair in range(rows // PAIR):
        at = pair * PAIR
        out[at : at + PAIR, :] = dot3(
            band_high[pair], band_low[pair], high[at : at + SPAN, :], low[at : at + SPAN, :]
        )


def apply_rows(place, width, sources, starts, bands):
    rows = sources[0].shape[0]
    ext = pltpu.VMEM((3 * rows, width), jnp.bfloat16)
    landed = pltpu.VMEM((len(sources), rows, width), jnp.float32)
    return pl.pallas_call(
        functools.partial(rows_kernel, starts),
        out_shape=pltpu.VMEM((rows, width), jnp.float32),
        in_specs=[pl.BlockSpec(memory_space=pltpu.SMEM)]
        + [pl.BlockSpec(memory_space=pltpu.HBM)]
        + [pl.BlockSpec(memory_space=pl.ANY)] * (len(sources) - 1)
        + [VMEM_SPEC] * 2,
        out_specs=VMEM_SPEC,
        scratch_shapes=[ext, ext, landed, pltpu.SemaphoreType.DMA((len(sources),))],
        compiler_params=pltpu.CompilerParams(vmem_limit_bytes=16 << 20),
        name="rows",
    )(place, in_hbm(sources[0]), *sources[1:], *(held(a) for a in bands))


def cols_kernel(*refs):
    parts = refs[:-5]
    band_high, band_low, out, high, low = refs[-5:]
    at = 0
    for ref in parts:
        h, l = split(ref[...])
        high[:, at : at + ref.shape[1]] = h
        low[:, at : at + ref.shape[1]] = l
        at += ref.shape[1]
    for pair in range(out.shape[1] // PAIR):
        begin = (pair - 1) * PAIR
        skip = max(0, -begin)
        stop = min(at, begin + SPAN)
        ext = slice(begin + skip, stop)
        band = slice(skip, stop - begin)
        out[:, pair * PAIR : (pair + 1) * PAIR] = dot3(
            high[:, ext], low[:, ext], band_high[pair, band], band_low[pair, band]
        )


def apply_cols(parts, bands, width):
    rows = parts[0].shape[0]
    ext = pltpu.VMEM((rows, sum(p.shape[1] for p in parts)), jnp.bfloat16)
    args = [held(a) for a in (*parts, *bands)]
    return pl.pallas_call(
        cols_kernel,
        out_shape=jax.ShapeDtypeStruct((rows, width), jnp.float32),
        in_specs=[VMEM_SPEC] * len(args),
        out_specs=VMEM_SPEC,
        scratch_shapes=[ext, ext],
        compiler_params=pltpu.CompilerParams(vmem_limit_bytes=32 << 20),
        name="cols",
    )(*args)


def tail_kernel(west, east, band_high, band_low, part, out):
    last = band_high.shape[0] - 1

    def add(ref, pair, rows):
        h, l = split(ref[...])
        out[...] = part[...] + dot3(h, l, band_high[pair, rows], band_low[pair, rows])

    @pl.when(pl.program_id(0) == 0)
    def _():
        add(east, last, slice(SPAN - east.shape[1], SPAN))

    @pl.when(pl.program_id(0) == 1)
    def _():
        add(west, 0, slice(0, west.shape[1]))


def apply_tail(west, east, bands, part):
    rows, width = part.shape
    block = pl.BlockSpec((rows, PAIR), lambda i: (0, (1 - i) * (width // PAIR - 1)))
    args = [held(a) for a in (west, east, *bands)]
    return pl.pallas_call(
        tail_kernel,
        grid=(2,),
        out_shape=jax.ShapeDtypeStruct((rows, width), jnp.float32),
        in_specs=[VMEM_SPEC] * 4 + [block],
        out_specs=block,
        input_output_aliases={4: 0},
        compiler_params=pltpu.CompilerParams(vmem_limit_bytes=16 << 20),
        name="tail",
    )(*args, part)


def body(
    covariance, latitude_offset, longitude_offset, upwind, courant,
    longitude_diffusion, latitude_diffusion,
):
    block = covariance[0]
    rows, width = block.shape
    row_count, col_count = lax.axis_size("row"), lax.axis_size("col")
    forward = lambda n: [(i, i + 1) for i in range(n - 1)]
    backward = lambda n: [(i + 1, i) for i in range(n - 1)]

    chip_pairs = [(i, i ^ 1) for i in range(row_count)]
    cross_pairs = [((i + 1 ^ 1) - 1, i) for i in range(1, row_count - 1)]
    copy_pairs = [(source ^ 1, target) for source, target in cross_pairs]

    fields = [
        a.reshape(NLAT, NLON)
        for a in (
            latitude_offset, longitude_offset, upwind, courant,
            longitude_diffusion, latitude_diffusion,
        )
    ]
    lat_row = (lax.axis_index("row") * (rows // NLON)).astype(jnp.int32).reshape(1)
    lat_col = (lax.axis_index("col") * (width // NLON)).astype(jnp.int32).reshape(1)

    starts = (0, width - PAIR, PAIR, width - 2 * PAIR)
    chip = lax.ppermute(block, "row", chip_pairs)
    (own0,) = take_columns(in_hbm(block), pltpu.HBM, [(0, PAIR)])
    (own1,) = take_columns(in_hbm(block), pltpu.HBM, [(width - PAIR, width)])
    (copy2,) = take_columns(chip, pl.ANY, [(PAIR, width - PAIR)])
    across0 = lax.ppermute(own0, "row", cross_pairs)
    across1 = lax.ppermute(own1, "row", cross_pairs)
    across2 = lax.ppermute(copy2, "row", copy_pairs)
    across = (across0, across1, across2, across2)
    offset = (0, 0, 0, width - 3 * PAIR)
    row_bands = build_bands(lat_row, fields, rows // PAIR, True)
    half, side = [], []
    for k in range(4):
        sources = [block, chip, across[k]]
        begins = [starts[k], starts[k], offset[k]]
        half.append(apply_rows(lat_row, PAIR, sources, begins, row_bands))
        pairs = forward(col_count) if k % 2 else backward(col_count)
        side.append(lax.ppermute(half[k], "col", pairs))
    col_bands = build_bands(lat_col, fields, width // PAIR, False)
    parts = [side[1], half[0], half[2], half[3], half[1], side[0]]
    part = apply_cols(parts, col_bands, width)
    return apply_tail(side[3], side[2], col_bands, part)[None]


def solution(mesh):
    in_specs = (P(None, "row", "col"), P(), P(), P(), P(), P(), P())
    out_specs = P(None, "row", "col")
    return jax.shard_map(body, mesh=mesh, in_specs=in_specs, out_specs=out_specs, check_vma=False)
```

```python
import functools

import jax
import jax.numpy as jnp
from jax import lax
from jax.experimental import pallas as pl
from jax.experimental.pallas import tpu as pltpu
from jax.sharding import PartitionSpec as P


NLAT = 64
NLON = 128
HALO = 4
SPAN = 10 * NLON
PAIR = 2 * NLON


def split(x):
    high = x.astype(jnp.bfloat16)
    low = (x - high.astype(jnp.float32)).astype(jnp.bfloat16)
    return high, low


def dot3(a_high, a_low, b_high, b_low):
    dot = functools.partial(jnp.dot, preferred_element_type=jnp.float32)
    return dot(a_high, b_high) + (dot(a_high, b_low) + dot(a_low, b_high))


def band_kernel(
    transposed, place, lat_off, lon_off, upwind, courant, lon_diff, lat_diff,
    high, low, depart_lat, depart_lon, near_lat, near_lon, hot,
):
    shape = (NLAT, NLON)
    lat = lax.broadcasted_iota(jnp.int32, shape, 0)
    lon = lax.broadcasted_iota(jnp.int32, shape, 1)
    up = upwind[...]
    one = jnp.ones(shape, jnp.int32)
    zero = jnp.zeros(shape, jnp.int32)
    d_lat = jnp.clip(lat + lat_off[...], 0, NLAT - 1)
    d_lon = (lon + lon_off[...]) & (NLON - 1)
    depart_lat[...] = d_lat
    depart_lon[...] = d_lon
    near_lat[...] = jnp.clip(
        d_lat + jnp.where(up == 2, one, zero) - jnp.where(up == 3, one, zero), 0, NLAT - 1
    )
    near_lon[...] = (
        d_lon + jnp.where(up == 0, one, zero) - jnp.where(up == 1, one, zero)
    ) & (NLON - 1)

    sub = lax.broadcasted_iota(jnp.int32, (NLON, NLON), 0)
    first = place[0]
    pairs = high.shape[0]

    def put(pair, half, t, value):
        if transposed:
            value = value.T
        h, l = split(value)
        cells = pl.ds(t * NLON, NLON)
        cols = pl.ds(half * NLON, NLON)
        at = (pair, cols, cells) if transposed else (pair, cells, cols)
        high[at] = h
        low[at] = l

    def fill(pair, half):
        y = first + 2 * pair + half
        lx = lon_diff[pl.ds(y, 1), :]
        ly = lat_diff[pl.ds(y, 1), :]
        core = 1.0 - 2.0 * lx - 2.0 * ly
        none = jnp.zeros_like(lx)
        reach = ((0, 0), (0, 1), (-1, 0))
        rows = (y, jnp.minimum(y + 1, NLAT - 1), jnp.maximum(y - 1, 0))
        rows = [pl.ds(r, 1) for r in rows]
        for k, row in enumerate(rows):
            on = jnp.ones((NLON, NLON), jnp.float32)
            off = jnp.zeros((NLON, NLON), jnp.float32)
            hot[2 * k] = jnp.where(sub == depart_lon[row, :], on, off)
            hot[2 * k + 1] = jnp.where(sub == near_lon[row, :], on, off)
        for t in range(2 * HALO + 1):
            far = t - HALO
            in_lat = y + far
            value = None
            for k, row in enumerate(rows):
                w = courant[row, :]
                below, above = reach[k]
                scale = ly if k else jnp.ones_like(lx)
                terms = []
                if -2 + below <= far <= 2 + above:
                    keep = jnp.where(depart_lat[row, :] == in_lat, scale * (1.0 - w), none)
                    terms.append(keep * hot[2 * k])
                if -3 + below <= far <= 3 + above:
                    take = jnp.where(near_lat[row, :] == in_lat, scale * w, none)
                    terms.append(take * hot[2 * k + 1])
                if not terms:
                    continue
                total = sum(terms[1:], terms[0])
                if k == 0:
                    beside = pltpu.roll(total, 1, 1) + pltpu.roll(total, NLON - 1, 1)
                    total = core * total + lx * beside
                value = total if value is None else value + total
            put(pair, half, t + half, value)
        put(pair, half, 0 if half else 2 * HALO + 1, jnp.zeros((NLON, NLON), jnp.float32))

    def step(pair, carry):
        fill(pair, 0)
        fill(pair, 1)
        return carry

    lax.fori_loop(0, pairs, step, 0)


VMEM_SPEC = pl.BlockSpec(memory_space=pltpu.VMEM)


def held(x):
    return pltpu.with_memory_space_constraint(x, pltpu.VMEM)


def in_hbm(x):
    return pltpu.with_memory_space_constraint(x, pltpu.HBM)


def build_bands(place, fields, pairs, transposed):
    shape = (pairs, PAIR, SPAN) if transposed else (pairs, SPAN, PAIR)
    band = pltpu.VMEM(shape, jnp.bfloat16)
    return pl.pallas_call(
        functools.partial(band_kernel, transposed),
        out_shape=(band, band),
        in_specs=[pl.BlockSpec(memory_space=pltpu.SMEM)] + [VMEM_SPEC] * 6,
        out_specs=(VMEM_SPEC,) * 2,
        scratch_shapes=[pltpu.VMEM((NLAT, NLON), jnp.int32)] * 4
        + [pltpu.VMEM((6, NLON, NLON), jnp.float32)],
        compiler_params=pltpu.CompilerParams(vmem_limit_bytes=24 << 20),
        name="row_bands" if transposed else "col_bands",
    )(place, *fields)


def take_kernel(starts, source, *refs):
    outs, sems = refs[:-1], refs[-1]
    count = sems.shape[1]
    piece = source.shape[0] // count
    copies = []
    for i, (at, out) in enumerate(zip(starts, outs)):
        for j in range(count):
            rows = pl.ds(j * piece, piece)
            copies.append(
                pltpu.make_async_copy(
                    source.at[rows, pl.ds(at, out.shape[1])], out.at[rows], sems.at[i, j]
                )
            )
    for copy in copies:
        copy.start()
    for copy in copies:
        copy.wait()


def take_columns(source, space, ranges):
    rows = source.shape[0]
    starts = [start for start, _ in ranges]
    return pl.pallas_call(
        functools.partial(take_kernel, starts),
        out_shape=tuple(pltpu.VMEM((rows, stop - start), jnp.float32) for start, stop in ranges),
        in_specs=[pl.BlockSpec(memory_space=space)],
        out_specs=(VMEM_SPEC,) * len(ranges),
        scratch_shapes=[pltpu.SemaphoreType.DMA((len(ranges), 4))],
        compiler_params=pltpu.CompilerParams(vmem_limit_bytes=8 << 20),
        name="take",
    )(source)


def rows_kernel(starts, place, *refs):
    *sources, band_high, band_low, out, high, low, landed, sems = refs
    rows, width = out.shape
    copies = [
        pltpu.make_async_copy(ref.at[:, pl.ds(start, width)], landed.at[i], sems.at[i])
        for i, (start, ref) in enumerate(zip(starts, sources))
    ]
    for copy in copies:
        copy.start()
    odd = (place[0] // HALO) & 1
    to_chip = pl.multiple_of((1 - odd) * 2 * rows, rows)
    to_cross = pl.multiple_of(odd * 2 * rows, rows)

    def put(value, at):
        h, l = split(value)
        high[pl.ds(at, rows), :] = h
        low[pl.ds(at, rows), :] = l

    copies[0].wait()
    put(landed[0], rows)
    copies[1].wait()
    put(landed[1], to_chip)
    for copy in copies[2:]:
        copy.wait()
    put(sum((landed[i] for i in range(3, len(copies))), landed[2]), to_cross)
    for pair in range(rows // PAIR):
        at = pair * PAIR
        out[at : at + PAIR, :] = dot3(
            band_high[pair], band_low[pair], high[at : at + SPAN, :], low[at : at + SPAN, :]
        )


def apply_rows(place, width, sources, starts, bands):
    rows = sources[0].shape[0]
    ext = pltpu.VMEM((3 * rows, width), jnp.bfloat16)
    landed = pltpu.VMEM((len(sources), rows, width), jnp.float32)
    return pl.pallas_call(
        functools.partial(rows_kernel, starts),
        out_shape=pltpu.VMEM((rows, width), jnp.float32),
        in_specs=[pl.BlockSpec(memory_space=pltpu.SMEM)]
        + [pl.BlockSpec(memory_space=pltpu.HBM)]
        + [pl.BlockSpec(memory_space=pl.ANY)] * (len(sources) - 1)
        + [VMEM_SPEC] * 2,
        out_specs=VMEM_SPEC,
        scratch_shapes=[ext, ext, landed, pltpu.SemaphoreType.DMA((len(sources),))],
        compiler_params=pltpu.CompilerParams(vmem_limit_bytes=16 << 20),
        name="rows",
    )(place, in_hbm(sources[0]), *sources[1:], *(held(a) for a in bands))


def cols_kernel(*refs):
    parts = refs[:-5]
    band_high, band_low, out, high, low = refs[-5:]
    at = 0
    for ref in parts:
        h, l = split(ref[...])
        high[:, at : at + ref.shape[1]] = h
        low[:, at : at + ref.shape[1]] = l
        at += ref.shape[1]
    for pair in range(out.shape[1] // PAIR):
        begin = (pair - 1) * PAIR
        skip = max(0, -begin)
        stop = min(at, begin + SPAN)
        ext = slice(begin + skip, stop)
        band = slice(skip, stop - begin)
        out[:, pair * PAIR : (pair + 1) * PAIR] = dot3(
            high[:, ext], low[:, ext], band_high[pair, band], band_low[pair, band]
        )


def apply_cols(parts, bands, width):
    rows = parts[0].shape[0]
    ext = pltpu.VMEM((rows, sum(p.shape[1] for p in parts)), jnp.bfloat16)
    args = [held(a) for a in (*parts, *bands)]
    return pl.pallas_call(
        cols_kernel,
        out_shape=jax.ShapeDtypeStruct((rows, width), jnp.float32),
        in_specs=[VMEM_SPEC] * len(args),
        out_specs=VMEM_SPEC,
        scratch_shapes=[ext, ext],
        compiler_params=pltpu.CompilerParams(vmem_limit_bytes=32 << 20),
        name="cols",
    )(*args)


def tail_kernel(west, east, band_high, band_low, part, out):
    last = band_high.shape[0] - 1

    def add(ref, pair, rows):
        h, l = split(ref[...])
        out[...] = part[...] + dot3(h, l, band_high[pair, rows], band_low[pair, rows])

    @pl.when(pl.program_id(0) == 0)
    def _():
        add(east, last, slice(SPAN - east.shape[1], SPAN))

    @pl.when(pl.program_id(0) == 1)
    def _():
        add(west, 0, slice(0, west.shape[1]))


def apply_tail(west, east, bands, part):
    rows, width = part.shape
    block = pl.BlockSpec((rows, PAIR), lambda i: (0, (1 - i) * (width // PAIR - 1)))
    args = [held(a) for a in (west, east, *bands)]
    return pl.pallas_call(
        tail_kernel,
        grid=(2,),
        out_shape=jax.ShapeDtypeStruct((rows, width), jnp.float32),
        in_specs=[VMEM_SPEC] * 4 + [block],
        out_specs=block,
        input_output_aliases={4: 0},
        compiler_params=pltpu.CompilerParams(vmem_limit_bytes=16 << 20),
        name="tail",
    )(*args, part)


def body(
    covariance, latitude_offset, longitude_offset, upwind, courant,
    longitude_diffusion, latitude_diffusion,
):
    block = covariance[0]
    rows, width = block.shape
    row_count, col_count = lax.axis_size("row"), lax.axis_size("col")
    forward = lambda n: [(i, i + 1) for i in range(n - 1)]
    backward = lambda n: [(i + 1, i) for i in range(n - 1)]

    chip_pairs = [(i, i ^ 1) for i in range(row_count)]
    cross_pairs = [((i + 1 ^ 1) - 1, i) for i in range(1, row_count - 1)]
    middle = row_count // 2
    last = row_count - 1
    middle_pairs = [(middle - 1, middle), (middle, middle - 1)]
    other_pairs = [pair for pair in cross_pairs if pair not in middle_pairs]
    copy_pairs = [(source ^ 1, target) for source, target in cross_pairs]

    fields = [
        a.reshape(NLAT, NLON)
        for a in (
            latitude_offset, longitude_offset, upwind, courant,
            longitude_diffusion, latitude_diffusion,
        )
    ]
    lat_row = (lax.axis_index("row") * (rows // NLON)).astype(jnp.int32).reshape(1)
    lat_col = (lax.axis_index("col") * (width // NLON)).astype(jnp.int32).reshape(1)

    starts = (0, width - PAIR, PAIR, width - 2 * PAIR)
    chip = lax.ppermute(block, "row", chip_pairs)
    own0, own1 = take_columns(in_hbm(block), pltpu.HBM, [(0, PAIR), (width - PAIR, width)])
    (copy2,) = take_columns(chip, pl.ANY, [(PAIR, width - PAIR)])
    across0 = lax.ppermute(own0, "row", cross_pairs)
    ends = lax.ppermute(own1, "row", [(middle - 1, 0), (middle, last)])
    relay = lax.ppermute(ends, "row", [(0, middle), (last, middle - 1)])
    across1 = lax.ppermute(own1, "row", other_pairs)
    across2 = lax.ppermute(copy2, "row", copy_pairs)
    across = ([across0], [across1, relay], [across2], [across2])
    offset = (0, 0, 0, width - 3 * PAIR)
    row_bands = build_bands(lat_row, fields, rows // PAIR, True)
    half, side = [], []
    for k in range(4):
        sources = [block, chip] + across[k]
        begins = [starts[k]] * 2 + [offset[k]] * len(across[k])
        half.append(apply_rows(lat_row, PAIR, sources, begins, row_bands))
        pairs = forward(col_count) if k % 2 else backward(col_count)
        side.append(lax.ppermute(half[k], "col", pairs))
    col_bands = build_bands(lat_col, fields, width // PAIR, False)
    parts = [side[1], half[0], half[2], half[3], half[1], side[0]]
    part = apply_cols(parts, col_bands, width)
    return apply_tail(side[3], side[2], col_bands, part)[None]


def solution(mesh):
    in_specs = (P(None, "row", "col"), P(), P(), P(), P(), P(), P())
    out_specs = P(None, "row", "col")
    return jax.shard_map(body, mesh=mesh, in_specs=in_specs, out_specs=out_specs, check_vma=False)
```

```python
import functools

import jax
import jax.numpy as jnp
from jax import lax
from jax.experimental import pallas as pl
from jax.experimental.pallas import tpu as pltpu
from jax.sharding import PartitionSpec as P


NLAT = 64
NLON = 128
HALO = 4
SPAN = 10 * NLON
PAIR = 2 * NLON


def split(x):
    high = x.astype(jnp.bfloat16)
    low = (x - high.astype(jnp.float32)).astype(jnp.bfloat16)
    return high, low


def dot3(a_high, a_low, b_high, b_low):
    dot = functools.partial(jnp.dot, preferred_element_type=jnp.float32)
    return dot(a_high, b_high) + (dot(a_high, b_low) + dot(a_low, b_high))


def band_kernel(
    transposed, place, lat_off, lon_off, upwind, courant, lon_diff, lat_diff,
    high, low, depart_lat, depart_lon, near_lat, near_lon, hot,
):
    shape = (NLAT, NLON)
    lat = lax.broadcasted_iota(jnp.int32, shape, 0)
    lon = lax.broadcasted_iota(jnp.int32, shape, 1)
    up = upwind[...]
    one = jnp.ones(shape, jnp.int32)
    zero = jnp.zeros(shape, jnp.int32)
    d_lat = jnp.clip(lat + lat_off[...], 0, NLAT - 1)
    d_lon = (lon + lon_off[...]) & (NLON - 1)
    depart_lat[...] = d_lat
    depart_lon[...] = d_lon
    near_lat[...] = jnp.clip(
        d_lat + jnp.where(up == 2, one, zero) - jnp.where(up == 3, one, zero), 0, NLAT - 1
    )
    near_lon[...] = (
        d_lon + jnp.where(up == 0, one, zero) - jnp.where(up == 1, one, zero)
    ) & (NLON - 1)

    sub = lax.broadcasted_iota(jnp.int32, (NLON, NLON), 0)
    first = place[0]
    pairs = high.shape[0]

    def put(pair, half, t, value):
        if transposed:
            value = value.T
        h, l = split(value)
        cells = pl.ds(t * NLON, NLON)
        cols = pl.ds(half * NLON, NLON)
        at = (pair, cols, cells) if transposed else (pair, cells, cols)
        high[at] = h
        low[at] = l

    def fill(pair, half):
        y = first + 2 * pair + half
        lx = lon_diff[pl.ds(y, 1), :]
        ly = lat_diff[pl.ds(y, 1), :]
        core = 1.0 - 2.0 * lx - 2.0 * ly
        none = jnp.zeros_like(lx)
        reach = ((0, 0), (0, 1), (-1, 0))
        rows = (y, jnp.minimum(y + 1, NLAT - 1), jnp.maximum(y - 1, 0))
        rows = [pl.ds(r, 1) for r in rows]
        for k, row in enumerate(rows):
            on = jnp.ones((NLON, NLON), jnp.float32)
            off = jnp.zeros((NLON, NLON), jnp.float32)
            hot[2 * k] = jnp.where(sub == depart_lon[row, :], on, off)
            hot[2 * k + 1] = jnp.where(sub == near_lon[row, :], on, off)
        for t in range(2 * HALO + 1):
            far = t - HALO
            in_lat = y + far
            value = None
            for k, row in enumerate(rows):
                w = courant[row, :]
                below, above = reach[k]
                scale = ly if k else jnp.ones_like(lx)
                terms = []
                if -2 + below <= far <= 2 + above:
                    keep = jnp.where(depart_lat[row, :] == in_lat, scale * (1.0 - w), none)
                    terms.append(keep * hot[2 * k])
                if -3 + below <= far <= 3 + above:
                    take = jnp.where(near_lat[row, :] == in_lat, scale * w, none)
                    terms.append(take * hot[2 * k + 1])
                if not terms:
                    continue
                total = sum(terms[1:], terms[0])
                if k == 0:
                    beside = pltpu.roll(total, 1, 1) + pltpu.roll(total, NLON - 1, 1)
                    total = core * total + lx * beside
                value = total if value is None else value + total
            put(pair, half, t + half, value)
        put(pair, half, 0 if half else 2 * HALO + 1, jnp.zeros((NLON, NLON), jnp.float32))

    def step(pair, carry):
        fill(pair, 0)
        fill(pair, 1)
        return carry

    lax.fori_loop(0, pairs, step, 0)


VMEM_SPEC = pl.BlockSpec(memory_space=pltpu.VMEM)


def held(x):
    return pltpu.with_memory_space_constraint(x, pltpu.VMEM)


def in_hbm(x):
    return pltpu.with_memory_space_constraint(x, pltpu.HBM)


def build_bands(place, fields, pairs, transposed):
    shape = (pairs, PAIR, SPAN) if transposed else (pairs, SPAN, PAIR)
    band = pltpu.VMEM(shape, jnp.bfloat16)
    return pl.pallas_call(
        functools.partial(band_kernel, transposed),
        out_shape=(band, band),
        in_specs=[pl.BlockSpec(memory_space=pltpu.SMEM)] + [VMEM_SPEC] * 6,
        out_specs=(VMEM_SPEC,) * 2,
        scratch_shapes=[pltpu.VMEM((NLAT, NLON), jnp.int32)] * 4
        + [pltpu.VMEM((6, NLON, NLON), jnp.float32)],
        compiler_params=pltpu.CompilerParams(vmem_limit_bytes=24 << 20),
        name="row_bands" if transposed else "col_bands",
    )(place, *fields)


def take_kernel(starts, source, *refs):
    outs, sems = refs[:-1], refs[-1]
    count = sems.shape[1]
    piece = source.shape[0] // count
    copies = []
    for i, (at, out) in enumerate(zip(starts, outs)):
        for j in range(count):
            rows = pl.ds(j * piece, piece)
            copies.append(
                pltpu.make_async_copy(
                    source.at[rows, pl.ds(at, out.shape[1])], out.at[rows], sems.at[i, j]
                )
            )
    for copy in copies:
        copy.start()
    for copy in copies:
        copy.wait()


def take_columns(source, space, ranges):
    rows = source.shape[0]
    starts = [start for start, _ in ranges]
    return pl.pallas_call(
        functools.partial(take_kernel, starts),
        out_shape=tuple(pltpu.VMEM((rows, stop - start), jnp.float32) for start, stop in ranges),
        in_specs=[pl.BlockSpec(memory_space=space)],
        out_specs=(VMEM_SPEC,) * len(ranges),
        scratch_shapes=[pltpu.SemaphoreType.DMA((len(ranges), 4))],
        compiler_params=pltpu.CompilerParams(vmem_limit_bytes=8 << 20),
        name="take",
    )(source)


def rows_kernel(starts, place, *refs):
    *sources, band_high, band_low, out, high, low, landed, sems = refs
    rows, width = out.shape
    copies = [
        pltpu.make_async_copy(ref.at[:, pl.ds(start, width)], landed.at[i], sems.at[i])
        for i, (start, ref) in enumerate(zip(starts, sources))
    ]
    for copy in copies:
        copy.start()
    odd = (place[0] // HALO) & 1
    to_chip = pl.multiple_of((1 - odd) * 2 * rows, rows)
    to_cross = pl.multiple_of(odd * 2 * rows, rows)

    def put(value, at):
        h, l = split(value)
        high[pl.ds(at, rows), :] = h
        low[pl.ds(at, rows), :] = l

    copies[0].wait()
    put(landed[0], rows)
    copies[1].wait()
    put(landed[1], to_chip)
    for copy in copies[2:]:
        copy.wait()
    put(sum((landed[i] for i in range(3, len(copies))), landed[2]), to_cross)
    for pair in range(rows // PAIR):
        at = pair * PAIR
        out[at : at + PAIR, :] = dot3(
            band_high[pair], band_low[pair], high[at : at + SPAN, :], low[at : at + SPAN, :]
        )


def apply_rows(place, width, sources, starts, bands):
    rows = sources[0].shape[0]
    ext = pltpu.VMEM((3 * rows, width), jnp.bfloat16)
    landed = pltpu.VMEM((len(sources), rows, width), jnp.float32)
    return pl.pallas_call(
        functools.partial(rows_kernel, starts),
        out_shape=pltpu.VMEM((rows, width), jnp.float32),
        in_specs=[pl.BlockSpec(memory_space=pltpu.SMEM)]
        + [pl.BlockSpec(memory_space=pltpu.HBM)]
        + [pl.BlockSpec(memory_space=pl.ANY)] * (len(sources) - 1)
        + [VMEM_SPEC] * 2,
        out_specs=VMEM_SPEC,
        scratch_shapes=[ext, ext, landed, pltpu.SemaphoreType.DMA((len(sources),))],
        compiler_params=pltpu.CompilerParams(vmem_limit_bytes=16 << 20),
        name="rows",
    )(place, in_hbm(sources[0]), *sources[1:], *(held(a) for a in bands))


def cols_kernel(*refs):
    parts = refs[:-5]
    band_high, band_low, out, high, low = refs[-5:]
    at = 0
    for ref in parts:
        h, l = split(ref[...])
        high[:, at : at + ref.shape[1]] = h
        low[:, at : at + ref.shape[1]] = l
        at += ref.shape[1]
    for pair in range(out.shape[1] // PAIR):
        begin = (pair - 1) * PAIR
        skip = max(0, -begin)
        stop = min(at, begin + SPAN)
        ext = slice(begin + skip, stop)
        band = slice(skip, stop - begin)
        out[:, pair * PAIR : (pair + 1) * PAIR] = dot3(
            high[:, ext], low[:, ext], band_high[pair, band], band_low[pair, band]
        )


def apply_cols(parts, bands, width):
    rows = parts[0].shape[0]
    ext = pltpu.VMEM((rows, sum(p.shape[1] for p in parts)), jnp.bfloat16)
    args = [held(a) for a in (*parts, *bands)]
    return pl.pallas_call(
        cols_kernel,
        out_shape=jax.ShapeDtypeStruct((rows, width), jnp.float32),
        in_specs=[VMEM_SPEC] * len(args),
        out_specs=VMEM_SPEC,
        scratch_shapes=[ext, ext],
        compiler_params=pltpu.CompilerParams(vmem_limit_bytes=32 << 20),
        name="cols",
    )(*args)


def tail_kernel(west, east, band_high, band_low, part, out):
    last = band_high.shape[0] - 1

    def add(ref, pair, rows):
        h, l = split(ref[...])
        out[...] = part[...] + dot3(h, l, band_high[pair, rows], band_low[pair, rows])

    @pl.when(pl.program_id(0) == 0)
    def _():
        add(east, last, slice(SPAN - east.shape[1], SPAN))

    @pl.when(pl.program_id(0) == 1)
    def _():
        add(west, 0, slice(0, west.shape[1]))


def apply_tail(west, east, bands, part):
    rows, width = part.shape
    block = pl.BlockSpec((rows, PAIR), lambda i: (0, (1 - i) * (width // PAIR - 1)))
    args = [held(a) for a in (west, east, *bands)]
    return pl.pallas_call(
        tail_kernel,
        grid=(2,),
        out_shape=jax.ShapeDtypeStruct((rows, width), jnp.float32),
        in_specs=[VMEM_SPEC] * 4 + [block],
        out_specs=block,
        input_output_aliases={4: 0},
        compiler_params=pltpu.CompilerParams(vmem_limit_bytes=16 << 20),
        name="tail",
    )(*args, part)


def body(
    covariance, latitude_offset, longitude_offset, upwind, courant,
    longitude_diffusion, latitude_diffusion,
):
    block = covariance[0]
    rows, width = block.shape
    row_count, col_count = lax.axis_size("row"), lax.axis_size("col")
    forward = lambda n: [(i, i + 1) for i in range(n - 1)]
    backward = lambda n: [(i + 1, i) for i in range(n - 1)]

    def shift(x, axis, pairs):
        return lax.ppermute(x, axis, pairs)

    chip_pairs = [(i, i ^ 1) for i in range(row_count)]
    cross_pairs = [((i + 1 ^ 1) - 1, i) for i in range(1, row_count - 1)]
    middle = row_count // 2
    last = row_count - 1
    middle_pairs = [(middle - 1, middle), (middle, middle - 1)]
    other_pairs = [pair for pair in cross_pairs if pair not in middle_pairs]
    copy_pairs = [(source ^ 1, target) for source, target in cross_pairs]

    fields = [
        a.reshape(NLAT, NLON)
        for a in (
            latitude_offset, longitude_offset, upwind, courant,
            longitude_diffusion, latitude_diffusion,
        )
    ]
    lat_row = (lax.axis_index("row") * (rows // NLON)).astype(jnp.int32).reshape(1)
    lat_col = (lax.axis_index("col") * (width // NLON)).astype(jnp.int32).reshape(1)

    starts = (0, width - PAIR, PAIR, width - 2 * PAIR)
    chip = shift(block, "row", chip_pairs)
    (own0,) = take_columns(in_hbm(block), pltpu.HBM, [(0, PAIR)])
    (own1,) = take_columns(in_hbm(block), pltpu.HBM, [(width - PAIR, width)])
    (copy2,) = take_columns(chip, pl.ANY, [(PAIR, width - PAIR)])
    across0 = shift(own0, "row", cross_pairs)
    ends = shift(own1, "row", [(middle - 1, 0), (middle, last)])
    relay = shift(ends, "row", [(0, middle), (last, middle - 1)])
    across1 = shift(own1, "row", other_pairs)
    mid = shift(copy2, "row", [p for p in copy_pairs if p[1] in (middle - 1, middle)])
    across2 = shift(copy2, "row", [p for p in copy_pairs if p[1] not in (middle - 1, middle)])
    across = ([across0], [across1, relay], [mid, across2], [mid, across2])
    offset = (0, 0, 0, width - 3 * PAIR)
    row_bands = build_bands(lat_row, fields, rows // PAIR, True)
    half, side = [], []
    for k in range(4):
        sources = [block, chip] + across[k]
        begins = [starts[k]] * 2 + [offset[k]] * len(across[k])
        half.append(apply_rows(lat_row, PAIR, sources, begins, row_bands))
        pairs = forward(col_count) if k % 2 else backward(col_count)
        side.append(shift(half[k], "col", pairs))
    col_bands = build_bands(lat_col, fields, width // PAIR, False)
    parts = [side[1], half[0], half[2], half[3], half[1], side[0]]
    part = apply_cols(parts, col_bands, width)
    return apply_tail(side[3], side[2], col_bands, part)[None]


def solution(mesh):
    in_specs = (P(None, "row", "col"), P(), P(), P(), P(), P(), P())
    out_specs = P(None, "row", "col")
    return jax.shard_map(body, mesh=mesh, in_specs=in_specs, out_specs=out_specs, check_vma=False)
```

```python
import functools

import jax
import jax.numpy as jnp
from jax import lax
from jax.experimental import pallas as pl
from jax.experimental.pallas import tpu as pltpu
from jax.sharding import PartitionSpec as P


NLAT = 64
NLON = 128
HALO = 4
SPAN = 10 * NLON
PAIR = 2 * NLON


def split(x):
    high = x.astype(jnp.bfloat16)
    low = (x - high.astype(jnp.float32)).astype(jnp.bfloat16)
    return high, low


def dot3(a_high, a_low, b_high, b_low):
    dot = functools.partial(jnp.dot, preferred_element_type=jnp.float32)
    return dot(a_high, b_high) + (dot(a_high, b_low) + dot(a_low, b_high))


def band_kernel(
    transposed, place, lat_off, lon_off, upwind, courant, lon_diff, lat_diff,
    high, low, depart_lat, depart_lon, near_lat, near_lon, hot,
):
    shape = (NLAT, NLON)
    lat = lax.broadcasted_iota(jnp.int32, shape, 0)
    lon = lax.broadcasted_iota(jnp.int32, shape, 1)
    up = upwind[...]
    one = jnp.ones(shape, jnp.int32)
    zero = jnp.zeros(shape, jnp.int32)
    d_lat = jnp.clip(lat + lat_off[...], 0, NLAT - 1)
    d_lon = (lon + lon_off[...]) & (NLON - 1)
    depart_lat[...] = d_lat
    depart_lon[...] = d_lon
    near_lat[...] = jnp.clip(
        d_lat + jnp.where(up == 2, one, zero) - jnp.where(up == 3, one, zero), 0, NLAT - 1
    )
    near_lon[...] = (
        d_lon + jnp.where(up == 0, one, zero) - jnp.where(up == 1, one, zero)
    ) & (NLON - 1)

    sub = lax.broadcasted_iota(jnp.int32, (NLON, NLON), 0)
    first = place[0]
    pairs = high.shape[0]

    def put(pair, half, t, value):
        if transposed:
            value = value.T
        h, l = split(value)
        cells = pl.ds(t * NLON, NLON)
        cols = pl.ds(half * NLON, NLON)
        at = (pair, cols, cells) if transposed else (pair, cells, cols)
        high[at] = h
        low[at] = l

    def fill(pair, half):
        y = first + 2 * pair + half
        lx = lon_diff[pl.ds(y, 1), :]
        ly = lat_diff[pl.ds(y, 1), :]
        core = 1.0 - 2.0 * lx - 2.0 * ly
        none = jnp.zeros_like(lx)
        reach = ((0, 0), (0, 1), (-1, 0))
        rows = (y, jnp.minimum(y + 1, NLAT - 1), jnp.maximum(y - 1, 0))
        rows = [pl.ds(r, 1) for r in rows]
        for k, row in enumerate(rows):
            on = jnp.ones((NLON, NLON), jnp.float32)
            off = jnp.zeros((NLON, NLON), jnp.float32)
            hot[2 * k] = jnp.where(sub == depart_lon[row, :], on, off)
            hot[2 * k + 1] = jnp.where(sub == near_lon[row, :], on, off)
        for t in range(2 * HALO + 1):
            far = t - HALO
            in_lat = y + far
            value = None
            for k, row in enumerate(rows):
                w = courant[row, :]
                below, above = reach[k]
                scale = ly if k else jnp.ones_like(lx)
                terms = []
                if -2 + below <= far <= 2 + above:
                    keep = jnp.where(depart_lat[row, :] == in_lat, scale * (1.0 - w), none)
                    terms.append(keep * hot[2 * k])
                if -3 + below <= far <= 3 + above:
                    take = jnp.where(near_lat[row, :] == in_lat, scale * w, none)
                    terms.append(take * hot[2 * k + 1])
                if not terms:
                    continue
                total = sum(terms[1:], terms[0])
                if k == 0:
                    beside = pltpu.roll(total, 1, 1) + pltpu.roll(total, NLON - 1, 1)
                    total = core * total + lx * beside
                value = total if value is None else value + total
            put(pair, half, t + half, value)
        put(pair, half, 0 if half else 2 * HALO + 1, jnp.zeros((NLON, NLON), jnp.float32))

    def step(pair, carry):
        fill(pair, 0)
        fill(pair, 1)
        return carry

    lax.fori_loop(0, pairs, step, 0)


VMEM_SPEC = pl.BlockSpec(memory_space=pltpu.VMEM)


def held(x):
    return pltpu.with_memory_space_constraint(x, pltpu.VMEM)


def in_hbm(x):
    return pltpu.with_memory_space_constraint(x, pltpu.HBM)


def build_bands(place, fields, pairs, transposed):
    shape = (pairs, PAIR, SPAN) if transposed else (pairs, SPAN, PAIR)
    band = pltpu.VMEM(shape, jnp.bfloat16)
    return pl.pallas_call(
        functools.partial(band_kernel, transposed),
        out_shape=(band, band),
        in_specs=[pl.BlockSpec(memory_space=pltpu.SMEM)] + [VMEM_SPEC] * 6,
        out_specs=(VMEM_SPEC,) * 2,
        scratch_shapes=[pltpu.VMEM((NLAT, NLON), jnp.int32)] * 4
        + [pltpu.VMEM((6, NLON, NLON), jnp.float32)],
        compiler_params=pltpu.CompilerParams(vmem_limit_bytes=24 << 20),
        name="row_bands" if transposed else "col_bands",
    )(place, *fields)


def take_kernel(starts, source, *refs):
    outs, sems = refs[:-1], refs[-1]
    count = sems.shape[1]
    piece = source.shape[0] // count
    copies = []
    for i, (at, out) in enumerate(zip(starts, outs)):
        for j in range(count):
            rows = pl.ds(j * piece, piece)
            copies.append(
                pltpu.make_async_copy(
                    source.at[rows, pl.ds(at, out.shape[1])], out.at[rows], sems.at[i, j]
                )
            )
    for copy in copies:
        copy.start()
    for copy in copies:
        copy.wait()


def take_columns(source, space, ranges):
    rows = source.shape[0]
    starts = [start for start, _ in ranges]
    return pl.pallas_call(
        functools.partial(take_kernel, starts),
        out_shape=tuple(pltpu.VMEM((rows, stop - start), jnp.float32) for start, stop in ranges),
        in_specs=[pl.BlockSpec(memory_space=space)],
        out_specs=(VMEM_SPEC,) * len(ranges),
        scratch_shapes=[pltpu.SemaphoreType.DMA((len(ranges), 4))],
        compiler_params=pltpu.CompilerParams(vmem_limit_bytes=8 << 20),
        name="take",
    )(source)


def rows_kernel(starts, place, *refs):
    *sources, band_high, band_low, out, high, low, landed, sems = refs
    rows, width = out.shape
    copies = [
        pltpu.make_async_copy(ref.at[:, pl.ds(start, width)], landed.at[i], sems.at[i])
        for i, (start, ref) in enumerate(zip(starts, sources))
    ]
    for copy in copies:
        copy.start()
    odd = (place[0] // HALO) & 1
    to_chip = pl.multiple_of((1 - odd) * 2 * rows, rows)
    to_cross = pl.multiple_of(odd * 2 * rows, rows)

    def put(value, at):
        h, l = split(value)
        high[pl.ds(at, rows), :] = h
        low[pl.ds(at, rows), :] = l

    copies[0].wait()
    put(landed[0], rows)
    copies[1].wait()
    put(landed[1], to_chip)
    for copy in copies[2:]:
        copy.wait()
    put(sum((landed[i] for i in range(3, len(copies))), landed[2]), to_cross)
    for pair in range(rows // PAIR):
        at = pair * PAIR
        out[at : at + PAIR, :] = dot3(
            band_high[pair], band_low[pair], high[at : at + SPAN, :], low[at : at + SPAN, :]
        )


def apply_rows(place, width, sources, starts, bands):
    rows = sources[0].shape[0]
    ext = pltpu.VMEM((3 * rows, width), jnp.bfloat16)
    landed = pltpu.VMEM((len(sources), rows, width), jnp.float32)
    return pl.pallas_call(
        functools.partial(rows_kernel, starts),
        out_shape=pltpu.VMEM((rows, width), jnp.float32),
        in_specs=[pl.BlockSpec(memory_space=pltpu.SMEM)]
        + [pl.BlockSpec(memory_space=pltpu.HBM)]
        + [pl.BlockSpec(memory_space=pl.ANY)] * (len(sources) - 1)
        + [VMEM_SPEC] * 2,
        out_specs=VMEM_SPEC,
        scratch_shapes=[ext, ext, landed, pltpu.SemaphoreType.DMA((len(sources),))],
        compiler_params=pltpu.CompilerParams(vmem_limit_bytes=16 << 20),
        name="rows",
    )(place, in_hbm(sources[0]), *sources[1:], *(held(a) for a in bands))


def cols_kernel(*refs):
    parts = refs[:-5]
    band_high, band_low, out, high, low = refs[-5:]
    at = 0
    for ref in parts:
        h, l = split(ref[...])
        high[:, at : at + ref.shape[1]] = h
        low[:, at : at + ref.shape[1]] = l
        at += ref.shape[1]
    for pair in range(out.shape[1] // PAIR):
        begin = (pair - 1) * PAIR
        skip = max(0, -begin)
        stop = min(at, begin + SPAN)
        ext = slice(begin + skip, stop)
        band = slice(skip, stop - begin)
        out[:, pair * PAIR : (pair + 1) * PAIR] = dot3(
            high[:, ext], low[:, ext], band_high[pair, band], band_low[pair, band]
        )


def apply_cols(parts, bands, width):
    rows = parts[0].shape[0]
    ext = pltpu.VMEM((rows, sum(p.shape[1] for p in parts)), jnp.bfloat16)
    args = [held(a) for a in (*parts, *bands)]
    return pl.pallas_call(
        cols_kernel,
        out_shape=jax.ShapeDtypeStruct((rows, width), jnp.float32),
        in_specs=[VMEM_SPEC] * len(args),
        out_specs=VMEM_SPEC,
        scratch_shapes=[ext, ext],
        compiler_params=pltpu.CompilerParams(vmem_limit_bytes=32 << 20),
        name="cols",
    )(*args)


def tail_kernel(west, east, band_high, band_low, part, out):
    last = band_high.shape[0] - 1

    def add(ref, pair, rows):
        h, l = split(ref[...])
        out[...] = part[...] + dot3(h, l, band_high[pair, rows], band_low[pair, rows])

    @pl.when(pl.program_id(0) == 0)
    def _():
        add(east, last, slice(SPAN - east.shape[1], SPAN))

    @pl.when(pl.program_id(0) == 1)
    def _():
        add(west, 0, slice(0, west.shape[1]))


def apply_tail(west, east, bands, part):
    rows, width = part.shape
    block = pl.BlockSpec((rows, PAIR), lambda i: (0, (1 - i) * (width // PAIR - 1)))
    args = [held(a) for a in (west, east, *bands)]
    return pl.pallas_call(
        tail_kernel,
        grid=(2,),
        out_shape=jax.ShapeDtypeStruct((rows, width), jnp.float32),
        in_specs=[VMEM_SPEC] * 4 + [block],
        out_specs=block,
        input_output_aliases={4: 0},
        compiler_params=pltpu.CompilerParams(vmem_limit_bytes=16 << 20),
        name="tail",
    )(*args, part)


def body(
    covariance, latitude_offset, longitude_offset, upwind, courant,
    longitude_diffusion, latitude_diffusion,
):
    block = covariance[0]
    rows, width = block.shape
    row_count, col_count = lax.axis_size("row"), lax.axis_size("col")
    forward = lambda n: [(i, i + 1) for i in range(n - 1)]
    backward = lambda n: [(i + 1, i) for i in range(n - 1)]

    chip_pairs = [(i, i ^ 1) for i in range(row_count)]
    cross_pairs = [((i + 1 ^ 1) - 1, i) for i in range(1, row_count - 1)]
    middle = row_count // 2
    last = row_count - 1
    middle_pairs = [(middle - 1, middle), (middle, middle - 1)]
    other_pairs = [pair for pair in cross_pairs if pair not in middle_pairs]
    copy_pairs = [(source ^ 1, target) for source, target in cross_pairs]

    fields = [
        a.reshape(NLAT, NLON)
        for a in (
            latitude_offset, longitude_offset, upwind, courant,
            longitude_diffusion, latitude_diffusion,
        )
    ]
    lat_row = (lax.axis_index("row") * (rows // NLON)).astype(jnp.int32).reshape(1)
    lat_col = (lax.axis_index("col") * (width // NLON)).astype(jnp.int32).reshape(1)

    starts = (0, width - PAIR, PAIR, width - 2 * PAIR)
    chip = lax.ppermute(block, "row", chip_pairs)
    (own0,) = take_columns(in_hbm(block), pltpu.HBM, [(0, PAIR)])
    own1, own3 = take_columns(
        in_hbm(block), pltpu.HBM,
        [(width - PAIR, width), (width - 2 * PAIR, width - PAIR)],
    )
    (copy2,) = take_columns(chip, pl.ANY, [(PAIR, 2 * PAIR)])
    across0 = lax.ppermute(own0, "row", cross_pairs)
    across1 = lax.ppermute(own1, "row", cross_pairs)
    across2 = lax.ppermute(copy2, "row", copy_pairs)
    across3 = lax.ppermute(own3, "row", other_pairs + [(middle - 1, 0), (middle, last)])
    relay = lax.ppermute(across3, "row", [(0, middle), (last, middle - 1)])
    across = ([across0], [across1], [across2], [across3, relay])
    row_bands = build_bands(lat_row, fields, rows // PAIR, True)
    half, side = [], []
    for k in range(4):
        sources = [block, chip] + across[k]
        begins = [starts[k]] * 2 + [0] * len(across[k])
        half.append(apply_rows(lat_row, PAIR, sources, begins, row_bands))
        pairs = forward(col_count) if k % 2 else backward(col_count)
        side.append(lax.ppermute(half[k], "col", pairs))
    col_bands = build_bands(lat_col, fields, width // PAIR, False)
    parts = [side[1], half[0], half[2], half[3], half[1], side[0]]
    part = apply_cols(parts, col_bands, width)
    return apply_tail(side[3], side[2], col_bands, part)[None]


def solution(mesh):
    in_specs = (P(None, "row", "col"), P(), P(), P(), P(), P(), P())
    out_specs = P(None, "row", "col")
    return jax.shard_map(body, mesh=mesh, in_specs=in_specs, out_specs=out_specs, check_vma=False)
```

```python
import functools

import jax
import jax.numpy as jnp
from jax import lax
from jax.experimental import pallas as pl
from jax.experimental.pallas import tpu as pltpu
from jax.sharding import PartitionSpec as P


NLAT = 64
NLON = 128
HALO = 4
SPAN = 10 * NLON
PAIR = 2 * NLON


def split(x):
    high = x.astype(jnp.bfloat16)
    low = (x - high.astype(jnp.float32)).astype(jnp.bfloat16)
    return high, low


def dot3(a_high, a_low, b_high, b_low):
    dot = functools.partial(jnp.dot, preferred_element_type=jnp.float32)
    return dot(a_high, b_high) + (dot(a_high, b_low) + dot(a_low, b_high))


def band_kernel(
    transposed, place, lat_off, lon_off, upwind, courant, lon_diff, lat_diff,
    high, low, depart_lat, depart_lon, near_lat, near_lon, hot,
):
    shape = (NLAT, NLON)
    lat = lax.broadcasted_iota(jnp.int32, shape, 0)
    lon = lax.broadcasted_iota(jnp.int32, shape, 1)
    up = upwind[...]
    one = jnp.ones(shape, jnp.int32)
    zero = jnp.zeros(shape, jnp.int32)
    d_lat = jnp.clip(lat + lat_off[...], 0, NLAT - 1)
    d_lon = (lon + lon_off[...]) & (NLON - 1)
    depart_lat[...] = d_lat
    depart_lon[...] = d_lon
    near_lat[...] = jnp.clip(
        d_lat + jnp.where(up == 2, one, zero) - jnp.where(up == 3, one, zero), 0, NLAT - 1
    )
    near_lon[...] = (
        d_lon + jnp.where(up == 0, one, zero) - jnp.where(up == 1, one, zero)
    ) & (NLON - 1)

    sub = lax.broadcasted_iota(jnp.int32, (NLON, NLON), 0)
    first = place[0]
    pairs = high.shape[0]

    def put(pair, half, t, value):
        if transposed:
            value = value.T
        h, l = split(value)
        cells = pl.ds(t * NLON, NLON)
        cols = pl.ds(half * NLON, NLON)
        at = (pair, cols, cells) if transposed else (pair, cells, cols)
        high[at] = h
        low[at] = l

    def fill(pair, half):
        y = first + 2 * pair + half
        lx = lon_diff[pl.ds(y, 1), :]
        ly = lat_diff[pl.ds(y, 1), :]
        core = 1.0 - 2.0 * lx - 2.0 * ly
        none = jnp.zeros_like(lx)
        reach = ((0, 0), (0, 1), (-1, 0))
        rows = (y, jnp.minimum(y + 1, NLAT - 1), jnp.maximum(y - 1, 0))
        rows = [pl.ds(r, 1) for r in rows]
        for k, row in enumerate(rows):
            on = jnp.ones((NLON, NLON), jnp.float32)
            off = jnp.zeros((NLON, NLON), jnp.float32)
            hot[2 * k] = jnp.where(sub == depart_lon[row, :], on, off)
            hot[2 * k + 1] = jnp.where(sub == near_lon[row, :], on, off)
        for t in range(2 * HALO + 1):
            far = t - HALO
            in_lat = y + far
            value = None
            for k, row in enumerate(rows):
                w = courant[row, :]
                below, above = reach[k]
                scale = ly if k else jnp.ones_like(lx)
                terms = []
                if -2 + below <= far <= 2 + above:
                    keep = jnp.where(depart_lat[row, :] == in_lat, scale * (1.0 - w), none)
                    terms.append(keep * hot[2 * k])
                if -3 + below <= far <= 3 + above:
                    take = jnp.where(near_lat[row, :] == in_lat, scale * w, none)
                    terms.append(take * hot[2 * k + 1])
                if not terms:
                    continue
                total = sum(terms[1:], terms[0])
                if k == 0:
                    beside = pltpu.roll(total, 1, 1) + pltpu.roll(total, NLON - 1, 1)
                    total = core * total + lx * beside
                value = total if value is None else value + total
            put(pair, half, t + half, value)
        put(pair, half, 0 if half else 2 * HALO + 1, jnp.zeros((NLON, NLON), jnp.float32))

    def step(pair, carry):
        fill(pair, 0)
        fill(pair, 1)
        return carry

    lax.fori_loop(0, pairs, step, 0)


VMEM_SPEC = pl.BlockSpec(memory_space=pltpu.VMEM)


def held(x):
    return pltpu.with_memory_space_constraint(x, pltpu.VMEM)


def in_hbm(x):
    return pltpu.with_memory_space_constraint(x, pltpu.HBM)


def build_bands(place, fields, pairs, transposed):
    shape = (pairs, PAIR, SPAN) if transposed else (pairs, SPAN, PAIR)
    band = pltpu.VMEM(shape, jnp.bfloat16)
    return pl.pallas_call(
        functools.partial(band_kernel, transposed),
        out_shape=(band, band),
        in_specs=[pl.BlockSpec(memory_space=pltpu.SMEM)] + [VMEM_SPEC] * 6,
        out_specs=(VMEM_SPEC,) * 2,
        scratch_shapes=[pltpu.VMEM((NLAT, NLON), jnp.int32)] * 4
        + [pltpu.VMEM((6, NLON, NLON), jnp.float32)],
        compiler_params=pltpu.CompilerParams(vmem_limit_bytes=24 << 20),
        name="row_bands" if transposed else "col_bands",
    )(place, *fields)


def take_kernel(starts, source, *refs):
    count = len(starts)
    outs, landed, sems = refs[:count], refs[count:-1], refs[-1]
    pieces = sems.shape[2]
    size = source.shape[0] // pieces
    moves = []
    for i, (at, out) in enumerate(zip(starts, outs)):
        for j in range(pieces):
            rows = pl.ds(j * size, size)
            here = landed[i].at[rows]
            moves.append(
                (
                    pltpu.make_async_copy(
                        source.at[rows, pl.ds(at, out.shape[1])], here, sems.at[0, i, j]
                    ),
                    pltpu.make_async_copy(here, out.at[rows], sems.at[1, i, j]),
                )
            )
    for arrive, _ in moves:
        arrive.start()
    for arrive, leave in moves:
        arrive.wait()
        leave.start()
    for _, leave in moves:
        leave.wait()


def take_columns(source, space, ranges):
    rows = source.shape[0]
    starts = [start for start, _ in ranges]
    shapes = [(rows, stop - start) for start, stop in ranges]
    hbm = pl.BlockSpec(memory_space=pltpu.HBM)
    return pl.pallas_call(
        functools.partial(take_kernel, starts),
        out_shape=tuple(jax.ShapeDtypeStruct(shape, jnp.float32) for shape in shapes),
        in_specs=[pl.BlockSpec(memory_space=space)],
        out_specs=(hbm,) * len(ranges),
        scratch_shapes=[pltpu.VMEM(shape, jnp.float32) for shape in shapes]
        + [pltpu.SemaphoreType.DMA((2, len(ranges), 4))],
        compiler_params=pltpu.CompilerParams(vmem_limit_bytes=8 << 20),
        name="take",
    )(source)


def rows_kernel(starts, place, *refs):
    *sources, band_high, band_low, out, high, low, landed, sems = refs
    rows, width = out.shape
    copies = [
        pltpu.make_async_copy(ref.at[:, pl.ds(start, width)], landed.at[i], sems.at[i])
        for i, (start, ref) in enumerate(zip(starts, sources))
    ]
    for copy in copies:
        copy.start()
    odd = (place[0] // HALO) & 1
    to_chip = pl.multiple_of((1 - odd) * 2 * rows, rows)
    to_cross = pl.multiple_of(odd * 2 * rows, rows)

    def put(value, at):
        h, l = split(value)
        high[pl.ds(at, rows), :] = h
        low[pl.ds(at, rows), :] = l

    copies[0].wait()
    put(landed[0], rows)
    copies[1].wait()
    put(landed[1], to_chip)
    for copy in copies[2:]:
        copy.wait()
    put(sum((landed[i] for i in range(3, len(copies))), landed[2]), to_cross)
    for pair in range(rows // PAIR):
        at = pair * PAIR
        out[at : at + PAIR, :] = dot3(
            band_high[pair], band_low[pair], high[at : at + SPAN, :], low[at : at + SPAN, :]
        )


def apply_rows(place, width, sources, starts, bands):
    rows = sources[0].shape[0]
    ext = pltpu.VMEM((3 * rows, width), jnp.bfloat16)
    landed = pltpu.VMEM((len(sources), rows, width), jnp.float32)
    return pl.pallas_call(
        functools.partial(rows_kernel, starts),
        out_shape=pltpu.VMEM((rows, width), jnp.float32),
        in_specs=[pl.BlockSpec(memory_space=pltpu.SMEM)]
        + [pl.BlockSpec(memory_space=pltpu.HBM)]
        + [pl.BlockSpec(memory_space=pl.ANY)] * (len(sources) - 1)
        + [VMEM_SPEC] * 2,
        out_specs=VMEM_SPEC,
        scratch_shapes=[ext, ext, landed, pltpu.SemaphoreType.DMA((len(sources),))],
        compiler_params=pltpu.CompilerParams(vmem_limit_bytes=16 << 20),
        name="rows",
    )(place, in_hbm(sources[0]), *sources[1:], *(held(a) for a in bands))


def cols_kernel(*refs):
    parts = refs[:-5]
    band_high, band_low, out, high, low = refs[-5:]
    at = 0
    for ref in parts:
        h, l = split(ref[...])
        high[:, at : at + ref.shape[1]] = h
        low[:, at : at + ref.shape[1]] = l
        at += ref.shape[1]
    for pair in range(out.shape[1] // PAIR):
        begin = (pair - 1) * PAIR
        skip = max(0, -begin)
        stop = min(at, begin + SPAN)
        ext = slice(begin + skip, stop)
        band = slice(skip, stop - begin)
        out[:, pair * PAIR : (pair + 1) * PAIR] = dot3(
            high[:, ext], low[:, ext], band_high[pair, band], band_low[pair, band]
        )


def apply_cols(parts, bands, width):
    rows = parts[0].shape[0]
    ext = pltpu.VMEM((rows, sum(p.shape[1] for p in parts)), jnp.bfloat16)
    args = [held(a) for a in (*parts, *bands)]
    return pl.pallas_call(
        cols_kernel,
        out_shape=jax.ShapeDtypeStruct((rows, width), jnp.float32),
        in_specs=[VMEM_SPEC] * len(args),
        out_specs=VMEM_SPEC,
        scratch_shapes=[ext, ext],
        compiler_params=pltpu.CompilerParams(vmem_limit_bytes=32 << 20),
        name="cols",
    )(*args)


def tail_kernel(west, east, band_high, band_low, part, out):
    last = band_high.shape[0] - 1
    tile = out.shape[0]
    here = pl.ds(pl.multiple_of(pl.program_id(1) * tile, tile), tile)

    def add(ref, pair, rows):
        h, l = split(ref[here, :])
        out[...] = part[...] + dot3(h, l, band_high[pair, rows], band_low[pair, rows])

    @pl.when(pl.program_id(0) == 0)
    def _():
        add(east, last, slice(SPAN - east.shape[1], SPAN))

    @pl.when(pl.program_id(0) == 1)
    def _():
        add(west, 0, slice(0, west.shape[1]))


def apply_tail(west, east, bands, part):
    rows, width = part.shape
    tile = rows // 2
    block = pl.BlockSpec((tile, PAIR), lambda i, j: (j, (1 - i) * (width // PAIR - 1)))
    args = [held(a) for a in (west, east, *bands)]
    return pl.pallas_call(
        tail_kernel,
        grid=(2, rows // tile),
        out_shape=jax.ShapeDtypeStruct((rows, width), jnp.float32),
        in_specs=[VMEM_SPEC] * 4 + [block],
        out_specs=block,
        input_output_aliases={4: 0},
        compiler_params=pltpu.CompilerParams(vmem_limit_bytes=16 << 20),
        name="tail",
    )(*args, part)


def body(
    covariance, latitude_offset, longitude_offset, upwind, courant,
    longitude_diffusion, latitude_diffusion,
):
    block = covariance[0]
    rows, width = block.shape
    row_count, col_count = lax.axis_size("row"), lax.axis_size("col")
    forward = lambda n: [(i, i + 1) for i in range(n - 1)]
    backward = lambda n: [(i + 1, i) for i in range(n - 1)]

    chip_pairs = [(i, i ^ 1) for i in range(row_count)]
    cross_pairs = [((i + 1 ^ 1) - 1, i) for i in range(1, row_count - 1)]
    middle = row_count // 2
    last = row_count - 1
    middle_pairs = [(middle - 1, middle), (middle, middle - 1)]
    other_pairs = [pair for pair in cross_pairs if pair not in middle_pairs]
    copy_pairs = [(source ^ 1, target) for source, target in cross_pairs]

    fields = [
        a.reshape(NLAT, NLON)
        for a in (
            latitude_offset, longitude_offset, upwind, courant,
            longitude_diffusion, latitude_diffusion,
        )
    ]
    lat_row = (lax.axis_index("row") * (rows // NLON)).astype(jnp.int32).reshape(1)
    lat_col = (lax.axis_index("col") * (width // NLON)).astype(jnp.int32).reshape(1)

    starts = (0, width - PAIR, PAIR, width - 2 * PAIR)
    chip = lax.ppermute(block, "row", chip_pairs)
    own0, own1 = take_columns(in_hbm(block), pltpu.HBM, [(0, PAIR), (width - PAIR, width)])
    (copy2,) = take_columns(chip, pl.ANY, [(PAIR, width - PAIR)])
    across0 = lax.ppermute(own0, "row", cross_pairs)
    ends = lax.ppermute(own1, "row", [(middle - 1, 0), (middle, last)])
    relay = lax.ppermute(ends, "row", [(0, middle), (last, middle - 1)])
    across1 = lax.ppermute(own1, "row", other_pairs)
    across2 = lax.ppermute(copy2, "row", copy_pairs)
    across = ([across0], [across1, relay], [across2], [across2])
    offset = (0, 0, 0, width - 3 * PAIR)
    row_bands = build_bands(lat_row, fields, rows // PAIR, True)
    half, side = [], []
    for k in range(4):
        sources = [block, chip] + across[k]
        begins = [starts[k]] * 2 + [offset[k]] * len(across[k])
        half.append(apply_rows(lat_row, PAIR, sources, begins, row_bands))
        pairs = forward(col_count) if k % 2 else backward(col_count)
        side.append(lax.ppermute(half[k], "col", pairs))
    col_bands = build_bands(lat_col, fields, width // PAIR, False)
    parts = [side[1], half[0], half[2], half[3], half[1], side[0]]
    part = apply_cols(parts, col_bands, width)
    return apply_tail(side[3], side[2], col_bands, part)[None]


def solution(mesh):
    in_specs = (P(None, "row", "col"), P(), P(), P(), P(), P(), P())
    out_specs = P(None, "row", "col")
    return jax.shard_map(body, mesh=mesh, in_specs=in_specs, out_specs=out_specs, check_vma=False)
```

```python
import functools

import jax
import jax.numpy as jnp
from jax import lax
from jax.experimental import pallas as pl
from jax.experimental.pallas import tpu as pltpu
from jax.sharding import PartitionSpec as P


NLAT = 64
NLON = 128
HALO = 4
SPAN = 10 * NLON
PAIR = 2 * NLON


def split(x):
    high = x.astype(jnp.bfloat16)
    low = (x - high.astype(jnp.float32)).astype(jnp.bfloat16)
    return high, low


def dot3(a_high, a_low, b_high, b_low):
    dot = functools.partial(jnp.dot, preferred_element_type=jnp.float32)
    return dot(a_high, b_high) + (dot(a_high, b_low) + dot(a_low, b_high))


def band_kernel(
    transposed, place, lat_off, lon_off, upwind, courant, lon_diff, lat_diff,
    high, low, depart_lat, depart_lon, near_lat, near_lon, hot,
):
    shape = (NLAT, NLON)
    lat = lax.broadcasted_iota(jnp.int32, shape, 0)
    lon = lax.broadcasted_iota(jnp.int32, shape, 1)
    up = upwind[...]
    one = jnp.ones(shape, jnp.int32)
    zero = jnp.zeros(shape, jnp.int32)
    d_lat = jnp.clip(lat + lat_off[...], 0, NLAT - 1)
    d_lon = (lon + lon_off[...]) & (NLON - 1)
    depart_lat[...] = d_lat
    depart_lon[...] = d_lon
    near_lat[...] = jnp.clip(
        d_lat + jnp.where(up == 2, one, zero) - jnp.where(up == 3, one, zero), 0, NLAT - 1
    )
    near_lon[...] = (
        d_lon + jnp.where(up == 0, one, zero) - jnp.where(up == 1, one, zero)
    ) & (NLON - 1)

    sub = lax.broadcasted_iota(jnp.int32, (NLON, NLON), 0)
    first = place[0]
    pairs = high.shape[0]

    def put(pair, half, t, value):
        if transposed:
            value = value.T
        h, l = split(value)
        cells = pl.ds(t * NLON, NLON)
        cols = pl.ds(half * NLON, NLON)
        at = (pair, cols, cells) if transposed else (pair, cells, cols)
        high[at] = h
        low[at] = l

    def fill(pair, half):
        y = first + 2 * pair + half
        lx = lon_diff[pl.ds(y, 1), :]
        ly = lat_diff[pl.ds(y, 1), :]
        core = 1.0 - 2.0 * lx - 2.0 * ly
        none = jnp.zeros_like(lx)
        reach = ((0, 0), (0, 1), (-1, 0))
        rows = (y, jnp.minimum(y + 1, NLAT - 1), jnp.maximum(y - 1, 0))
        rows = [pl.ds(r, 1) for r in rows]
        for k, row in enumerate(rows):
            on = jnp.ones((NLON, NLON), jnp.float32)
            off = jnp.zeros((NLON, NLON), jnp.float32)
            hot[2 * k] = jnp.where(sub == depart_lon[row, :], on, off)
            hot[2 * k + 1] = jnp.where(sub == near_lon[row, :], on, off)
        for t in range(2 * HALO + 1):
            far = t - HALO
            in_lat = y + far
            value = None
            for k, row in enumerate(rows):
                w = courant[row, :]
                below, above = reach[k]
                scale = ly if k else jnp.ones_like(lx)
                terms = []
                if -2 + below <= far <= 2 + above:
                    keep = jnp.where(depart_lat[row, :] == in_lat, scale * (1.0 - w), none)
                    terms.append(keep * hot[2 * k])
                if -3 + below <= far <= 3 + above:
                    take = jnp.where(near_lat[row, :] == in_lat, scale * w, none)
                    terms.append(take * hot[2 * k + 1])
                if not terms:
                    continue
                total = sum(terms[1:], terms[0])
                if k == 0:
                    beside = pltpu.roll(total, 1, 1) + pltpu.roll(total, NLON - 1, 1)
                    total = core * total + lx * beside
                value = total if value is None else value + total
            put(pair, half, t + half, value)
        put(pair, half, 0 if half else 2 * HALO + 1, jnp.zeros((NLON, NLON), jnp.float32))

    def step(pair, carry):
        fill(pair, 0)
        fill(pair, 1)
        return carry

    lax.fori_loop(0, pairs, step, 0)


VMEM_SPEC = pl.BlockSpec(memory_space=pltpu.VMEM)


def held(x):
    return pltpu.with_memory_space_constraint(x, pltpu.VMEM)


def in_hbm(x):
    return pltpu.with_memory_space_constraint(x, pltpu.HBM)


def build_bands(place, fields, pairs, transposed):
    shape = (pairs, PAIR, SPAN) if transposed else (pairs, SPAN, PAIR)
    band = pltpu.VMEM(shape, jnp.bfloat16)
    return pl.pallas_call(
        functools.partial(band_kernel, transposed),
        out_shape=(band, band),
        in_specs=[pl.BlockSpec(memory_space=pltpu.SMEM)] + [VMEM_SPEC] * 6,
        out_specs=(VMEM_SPEC,) * 2,
        scratch_shapes=[pltpu.VMEM((NLAT, NLON), jnp.int32)] * 4
        + [pltpu.VMEM((6, NLON, NLON), jnp.float32)],
        compiler_params=pltpu.CompilerParams(vmem_limit_bytes=24 << 20),
        name="row_bands" if transposed else "col_bands",
    )(place, *fields)


def take_kernel(starts, source, *refs):
    count = len(starts)
    outs, landed, sems = refs[:count], refs[count:-1], refs[-1]
    pieces = sems.shape[2]
    size = source.shape[0] // pieces
    moves = []
    for i, (at, out) in enumerate(zip(starts, outs)):
        for j in range(pieces):
            rows = pl.ds(j * size, size)
            here = landed[i].at[rows]
            moves.append(
                (
                    pltpu.make_async_copy(
                        source.at[rows, pl.ds(at, out.shape[1])], here, sems.at[0, i, j]
                    ),
                    pltpu.make_async_copy(here, out.at[rows], sems.at[1, i, j]),
                )
            )
    for arrive, _ in moves:
        arrive.start()
    for arrive, leave in moves:
        arrive.wait()
        leave.start()
    for _, leave in moves:
        leave.wait()


def take_columns(source, ranges):
    rows = source.shape[0]
    starts = [start for start, _ in ranges]
    shapes = [(rows, stop - start) for start, stop in ranges]
    hbm = pl.BlockSpec(memory_space=pltpu.HBM)
    return pl.pallas_call(
        functools.partial(take_kernel, starts),
        out_shape=tuple(jax.ShapeDtypeStruct(shape, jnp.float32) for shape in shapes),
        in_specs=[hbm],
        out_specs=(hbm,) * len(ranges),
        scratch_shapes=[pltpu.VMEM(shape, jnp.float32) for shape in shapes]
        + [pltpu.SemaphoreType.DMA((2, len(ranges), 4))],
        compiler_params=pltpu.CompilerParams(vmem_limit_bytes=8 << 20),
        name="take",
    )(in_hbm(source))


def rows_kernel(starts, place, *refs):
    *sources, band_high, band_low, out, high, low, landed, sems = refs
    rows, width = out.shape
    copies = [
        pltpu.make_async_copy(ref.at[:, pl.ds(start, width)], landed.at[i], sems.at[i])
        for i, (start, ref) in enumerate(zip(starts, sources))
    ]
    for copy in copies:
        copy.start()
    odd = (place[0] // HALO) & 1
    to_chip = pl.multiple_of((1 - odd) * 2 * rows, rows)
    to_cross = pl.multiple_of(odd * 2 * rows, rows)

    def put(value, at):
        h, l = split(value)
        high[pl.ds(at, rows), :] = h
        low[pl.ds(at, rows), :] = l

    copies[0].wait()
    put(landed[0], rows)
    copies[1].wait()
    put(landed[1], to_chip)
    for copy in copies[2:]:
        copy.wait()
    put(sum((landed[i] for i in range(3, len(copies))), landed[2]), to_cross)
    for pair in range(rows // PAIR):
        at = pair * PAIR
        out[at : at + PAIR, :] = dot3(
            band_high[pair], band_low[pair], high[at : at + SPAN, :], low[at : at + SPAN, :]
        )


def apply_rows(place, width, sources, starts, bands):
    rows = sources[0].shape[0]
    ext = pltpu.VMEM((3 * rows, width), jnp.bfloat16)
    landed = pltpu.VMEM((len(sources), rows, width), jnp.float32)
    return pl.pallas_call(
        functools.partial(rows_kernel, starts),
        out_shape=pltpu.VMEM((rows, width), jnp.float32),
        in_specs=[pl.BlockSpec(memory_space=pltpu.SMEM)]
        + [pl.BlockSpec(memory_space=pltpu.HBM)] * len(sources)
        + [VMEM_SPEC] * 2,
        out_specs=VMEM_SPEC,
        scratch_shapes=[ext, ext, landed, pltpu.SemaphoreType.DMA((len(sources),))],
        compiler_params=pltpu.CompilerParams(vmem_limit_bytes=16 << 20),
        name="rows",
    )(place, *(in_hbm(a) for a in sources), *(held(a) for a in bands))


def cols_kernel(*refs):
    parts = refs[:-5]
    band_high, band_low, out, high, low = refs[-5:]
    at = 0
    for ref in parts:
        h, l = split(ref[...])
        high[:, at : at + ref.shape[1]] = h
        low[:, at : at + ref.shape[1]] = l
        at += ref.shape[1]
    for pair in range(out.shape[1] // PAIR):
        begin = (pair - 1) * PAIR
        skip = max(0, -begin)
        stop = min(at, begin + SPAN)
        ext = slice(begin + skip, stop)
        band = slice(skip, stop - begin)
        out[:, pair * PAIR : (pair + 1) * PAIR] = dot3(
            high[:, ext], low[:, ext], band_high[pair, band], band_low[pair, band]
        )


def apply_cols(parts, bands, width):
    rows = parts[0].shape[0]
    ext = pltpu.VMEM((rows, sum(p.shape[1] for p in parts)), jnp.bfloat16)
    args = [held(a) for a in (*parts, *bands)]
    return pl.pallas_call(
        cols_kernel,
        out_shape=jax.ShapeDtypeStruct((rows, width), jnp.float32),
        in_specs=[VMEM_SPEC] * len(args),
        out_specs=VMEM_SPEC,
        scratch_shapes=[ext, ext],
        compiler_params=pltpu.CompilerParams(vmem_limit_bytes=32 << 20),
        name="cols",
    )(*args)


def tail_kernel(west, east, band_high, band_low, part, out):
    last = band_high.shape[0] - 1

    def add(ref, pair, rows):
        h, l = split(ref[...])
        out[...] = part[...] + dot3(h, l, band_high[pair, rows], band_low[pair, rows])

    @pl.when(pl.program_id(0) == 0)
    def _():
        add(east, last, slice(SPAN - east.shape[1], SPAN))

    @pl.when(pl.program_id(0) == 1)
    def _():
        add(west, 0, slice(0, west.shape[1]))


def apply_tail(west, east, bands, part):
    rows, width = part.shape
    block = pl.BlockSpec((rows, PAIR), lambda i: (0, (1 - i) * (width // PAIR - 1)))
    args = [held(a) for a in (west, east, *bands)]
    return pl.pallas_call(
        tail_kernel,
        grid=(2,),
        out_shape=jax.ShapeDtypeStruct((rows, width), jnp.float32),
        in_specs=[VMEM_SPEC] * 4 + [block],
        out_specs=block,
        input_output_aliases={4: 0},
        compiler_params=pltpu.CompilerParams(vmem_limit_bytes=16 << 20),
        name="tail",
    )(*args, part)


def body(
    covariance, latitude_offset, longitude_offset, upwind, courant,
    longitude_diffusion, latitude_diffusion,
):
    block = covariance[0]
    rows, width = block.shape
    row_count, col_count = lax.axis_size("row"), lax.axis_size("col")
    forward = lambda n: [(i, i + 1) for i in range(n - 1)]
    backward = lambda n: [(i + 1, i) for i in range(n - 1)]

    chip_pairs = [(i, i ^ 1) for i in range(row_count)]
    cross_pairs = [((i + 1 ^ 1) - 1, i) for i in range(1, row_count - 1)]
    middle = row_count // 2
    last = row_count - 1
    middle_pairs = [(middle - 1, middle), (middle, middle - 1)]
    other_pairs = [pair for pair in cross_pairs if pair not in middle_pairs]
    copy_pairs = [(source ^ 1, target) for source, target in cross_pairs]

    fields = [
        a.reshape(NLAT, NLON)
        for a in (
            latitude_offset, longitude_offset, upwind, courant,
            longitude_diffusion, latitude_diffusion,
        )
    ]
    lat_row = (lax.axis_index("row") * (rows // NLON)).astype(jnp.int32).reshape(1)
    lat_col = (lax.axis_index("col") * (width // NLON)).astype(jnp.int32).reshape(1)

    starts = (0, width - PAIR, PAIR, width - 2 * PAIR)
    chip = lax.ppermute(block, "row", chip_pairs)
    own0, own1, own2 = take_columns(
        block, [(0, PAIR), (PAIR, 2 * PAIR), (2 * PAIR, width)]
    )
    copy2 = lax.ppermute(own2, "row", chip_pairs)
    across0 = lax.ppermute(own0, "row", cross_pairs)
    ends = lax.ppermute(own1, "row", [(middle - 1, 0), (middle, last)])
    relay = lax.ppermute(ends, "row", [(0, middle), (last, middle - 1)])
    across1 = lax.ppermute(own1, "row", other_pairs)
    across2 = lax.ppermute(copy2, "row", copy_pairs)
    across = ([across0], [across2], [across1, relay], [across2])
    offset = (0, width - 3 * PAIR, 0, width - 4 * PAIR)
    row_bands = build_bands(lat_row, fields, rows // PAIR, True)
    half, side = [], []
    for k in range(4):
        sources = [block, chip] + across[k]
        begins = [starts[k]] * 2 + [offset[k]] * len(across[k])
        half.append(apply_rows(lat_row, PAIR, sources, begins, row_bands))
        pairs = forward(col_count) if k % 2 else backward(col_count)
        side.append(lax.ppermute(half[k], "col", pairs))
    col_bands = build_bands(lat_col, fields, width // PAIR, False)
    parts = [side[1], half[0], half[2], half[3], half[1], side[0]]
    part = apply_cols(parts, col_bands, width)
    return apply_tail(side[3], side[2], col_bands, part)[None]


def solution(mesh):
    in_specs = (P(None, "row", "col"), P(), P(), P(), P(), P(), P())
    out_specs = P(None, "row", "col")
    return jax.shard_map(
        body, mesh=mesh, in_specs=in_specs, out_specs=out_specs, check_vma=False
    )
```

```python
import functools

import jax
import jax.numpy as jnp
from jax import lax
from jax.experimental import pallas as pl
from jax.experimental.pallas import tpu as pltpu
from jax.sharding import PartitionSpec as P


NLAT = 64
NLON = 128
HALO = 4
SPAN = 10 * NLON
PAIR = 2 * NLON


def split(x):
    high = x.astype(jnp.bfloat16)
    low = (x - high.astype(jnp.float32)).astype(jnp.bfloat16)
    return high, low


def dot3(a_high, a_low, b_high, b_low):
    dot = functools.partial(jnp.dot, preferred_element_type=jnp.float32)
    return dot(a_high, b_high) + (dot(a_high, b_low) + dot(a_low, b_high))


def band_kernel(
    transposed, place, lat_off, lon_off, upwind, courant, lon_diff, lat_diff,
    high, low, depart_lat, depart_lon, near_lat, near_lon, hot,
):
    shape = (NLAT, NLON)
    lat = lax.broadcasted_iota(jnp.int32, shape, 0)
    lon = lax.broadcasted_iota(jnp.int32, shape, 1)
    up = upwind[...]
    one = jnp.ones(shape, jnp.int32)
    zero = jnp.zeros(shape, jnp.int32)
    d_lat = jnp.clip(lat + lat_off[...], 0, NLAT - 1)
    d_lon = (lon + lon_off[...]) & (NLON - 1)
    depart_lat[...] = d_lat
    depart_lon[...] = d_lon
    near_lat[...] = jnp.clip(
        d_lat + jnp.where(up == 2, one, zero) - jnp.where(up == 3, one, zero), 0, NLAT - 1
    )
    near_lon[...] = (
        d_lon + jnp.where(up == 0, one, zero) - jnp.where(up == 1, one, zero)
    ) & (NLON - 1)

    sub = lax.broadcasted_iota(jnp.int32, (NLON, NLON), 0)
    first = place[0]
    pairs = high.shape[0]

    def put(pair, half, t, value):
        if transposed:
            value = value.T
        h, l = split(value)
        cells = pl.ds(t * NLON, NLON)
        cols = pl.ds(half * NLON, NLON)
        at = (pair, cols, cells) if transposed else (pair, cells, cols)
        high[at] = h
        low[at] = l

    def fill(pair, half):
        y = first + 2 * pair + half
        lx = lon_diff[pl.ds(y, 1), :]
        ly = lat_diff[pl.ds(y, 1), :]
        core = 1.0 - 2.0 * lx - 2.0 * ly
        none = jnp.zeros_like(lx)
        reach = ((0, 0), (0, 1), (-1, 0))
        rows = (y, jnp.minimum(y + 1, NLAT - 1), jnp.maximum(y - 1, 0))
        rows = [pl.ds(r, 1) for r in rows]
        for k, row in enumerate(rows):
            on = jnp.ones((NLON, NLON), jnp.float32)
            off = jnp.zeros((NLON, NLON), jnp.float32)
            hot[2 * k] = jnp.where(sub == depart_lon[row, :], on, off)
            hot[2 * k + 1] = jnp.where(sub == near_lon[row, :], on, off)
        for t in range(2 * HALO + 1):
            far = t - HALO
            in_lat = y + far
            value = None
            for k, row in enumerate(rows):
                w = courant[row, :]
                below, above = reach[k]
                scale = ly if k else jnp.ones_like(lx)
                terms = []
                if -2 + below <= far <= 2 + above:
                    keep = jnp.where(depart_lat[row, :] == in_lat, scale * (1.0 - w), none)
                    terms.append(keep * hot[2 * k])
                if -3 + below <= far <= 3 + above:
                    take = jnp.where(near_lat[row, :] == in_lat, scale * w, none)
                    terms.append(take * hot[2 * k + 1])
                if not terms:
                    continue
                total = sum(terms[1:], terms[0])
                if k == 0:
                    beside = pltpu.roll(total, 1, 1) + pltpu.roll(total, NLON - 1, 1)
                    total = core * total + lx * beside
                value = total if value is None else value + total
            put(pair, half, t + half, value)
        put(pair, half, 0 if half else 2 * HALO + 1, jnp.zeros((NLON, NLON), jnp.float32))

    def step(pair, carry):
        fill(pair, 0)
        fill(pair, 1)
        return carry

    lax.fori_loop(0, pairs, step, 0)


VMEM_SPEC = pl.BlockSpec(memory_space=pltpu.VMEM)


def held(x):
    return pltpu.with_memory_space_constraint(x, pltpu.VMEM)


def in_hbm(x):
    return pltpu.with_memory_space_constraint(x, pltpu.HBM)


def build_bands(place, fields, pairs, transposed):
    shape = (pairs, PAIR, SPAN) if transposed else (pairs, SPAN, PAIR)
    band = pltpu.VMEM(shape, jnp.bfloat16)
    return pl.pallas_call(
        functools.partial(band_kernel, transposed),
        out_shape=(band, band),
        in_specs=[pl.BlockSpec(memory_space=pltpu.SMEM)] + [VMEM_SPEC] * 6,
        out_specs=(VMEM_SPEC,) * 2,
        scratch_shapes=[pltpu.VMEM((NLAT, NLON), jnp.int32)] * 4
        + [pltpu.VMEM((6, NLON, NLON), jnp.float32)],
        compiler_params=pltpu.CompilerParams(vmem_limit_bytes=24 << 20),
        name="row_bands" if transposed else "col_bands",
    )(place, *fields)


def take_kernel(starts, source, *refs):
    count = len(starts)
    outs, landed, sems = refs[:count], refs[count:-1], refs[-1]
    pieces = sems.shape[2]
    size = source.shape[0] // pieces
    moves = []
    for i, (at, out) in enumerate(zip(starts, outs)):
        for j in range(pieces):
            rows = pl.ds(j * size, size)
            here = landed[i].at[rows]
            moves.append(
                (
                    pltpu.make_async_copy(
                        source.at[rows, pl.ds(at, out.shape[1])], here, sems.at[0, i, j]
                    ),
                    pltpu.make_async_copy(here, out.at[rows], sems.at[1, i, j]),
                )
            )
    for arrive, _ in moves:
        arrive.start()
    for arrive, leave in moves:
        arrive.wait()
        leave.start()
    for _, leave in moves:
        leave.wait()


def take_columns(source, ranges):
    rows = source.shape[0]
    starts = [start for start, _ in ranges]
    shapes = [(rows, stop - start) for start, stop in ranges]
    hbm = pl.BlockSpec(memory_space=pltpu.HBM)
    return pl.pallas_call(
        functools.partial(take_kernel, starts),
        out_shape=tuple(jax.ShapeDtypeStruct(shape, jnp.float32) for shape in shapes),
        in_specs=[hbm],
        out_specs=(hbm,) * len(ranges),
        scratch_shapes=[pltpu.VMEM(shape, jnp.float32) for shape in shapes]
        + [pltpu.SemaphoreType.DMA((2, len(ranges), 4))],
        compiler_params=pltpu.CompilerParams(vmem_limit_bytes=8 << 20),
        name="take",
    )(in_hbm(source))


def rows_kernel(starts, place, *refs):
    *sources, band_high, band_low, out, high, low, landed, sems = refs
    rows, width = out.shape
    copies = [
        pltpu.make_async_copy(ref.at[:, pl.ds(start, width)], landed.at[i], sems.at[i])
        for i, (start, ref) in enumerate(zip(starts, sources))
    ]
    for copy in copies:
        copy.start()
    odd = (place[0] // HALO) & 1
    to_chip = pl.multiple_of((1 - odd) * 2 * rows, rows)
    to_cross = pl.multiple_of(odd * 2 * rows, rows)

    def put(value, at):
        h, l = split(value)
        high[pl.ds(at, rows), :] = h
        low[pl.ds(at, rows), :] = l

    copies[0].wait()
    put(landed[0], rows)
    copies[1].wait()
    put(landed[1], to_chip)
    for copy in copies[2:]:
        copy.wait()
    put(sum((landed[i] for i in range(3, len(copies))), landed[2]), to_cross)
    for pair in range(rows // PAIR):
        at = pair * PAIR
        out[at : at + PAIR, :] = dot3(
            band_high[pair], band_low[pair], high[at : at + SPAN, :], low[at : at + SPAN, :]
        )


def apply_rows(place, width, sources, starts, bands):
    rows = sources[0].shape[0]
    ext = pltpu.VMEM((3 * rows, width), jnp.bfloat16)
    landed = pltpu.VMEM((len(sources), rows, width), jnp.float32)
    return pl.pallas_call(
        functools.partial(rows_kernel, starts),
        out_shape=pltpu.VMEM((rows, width), jnp.float32),
        in_specs=[pl.BlockSpec(memory_space=pltpu.SMEM)]
        + [pl.BlockSpec(memory_space=pltpu.HBM)] * len(sources)
        + [VMEM_SPEC] * 2,
        out_specs=VMEM_SPEC,
        scratch_shapes=[ext, ext, landed, pltpu.SemaphoreType.DMA((len(sources),))],
        compiler_params=pltpu.CompilerParams(vmem_limit_bytes=16 << 20),
        name="rows",
    )(place, *(in_hbm(a) for a in sources), *(held(a) for a in bands))


def cols_kernel(*refs):
    parts = refs[:-5]
    band_high, band_low, out, high, low = refs[-5:]
    at = 0
    for ref in parts:
        h, l = split(ref[...])
        high[:, at : at + ref.shape[1]] = h
        low[:, at : at + ref.shape[1]] = l
        at += ref.shape[1]
    for pair in range(out.shape[1] // PAIR):
        begin = (pair - 1) * PAIR
        skip = max(0, -begin)
        stop = min(at, begin + SPAN)
        ext = slice(begin + skip, stop)
        band = slice(skip, stop - begin)
        out[:, pair * PAIR : (pair + 1) * PAIR] = dot3(
            high[:, ext], low[:, ext], band_high[pair, band], band_low[pair, band]
        )


def apply_cols(parts, bands, width):
    rows = parts[0].shape[0]
    ext = pltpu.VMEM((rows, sum(p.shape[1] for p in parts)), jnp.bfloat16)
    args = [held(a) for a in (*parts, *bands)]
    return pl.pallas_call(
        cols_kernel,
        out_shape=jax.ShapeDtypeStruct((rows, width), jnp.float32),
        in_specs=[VMEM_SPEC] * len(args),
        out_specs=VMEM_SPEC,
        scratch_shapes=[ext, ext],
        compiler_params=pltpu.CompilerParams(vmem_limit_bytes=32 << 20),
        name="cols",
    )(*args)


def tail_kernel(west, east, band_high, band_low, part, out, landed, sems):
    last = band_high.shape[0] - 1
    jobs = ((east, last, slice(SPAN - east.shape[1], SPAN)), (west, 0, slice(0, west.shape[1])))
    here = [pl.ds(pair * PAIR, PAIR) for _, pair, _ in jobs]
    arrive = [
        pltpu.make_async_copy(part.at[:, cols], landed.at[i], sems.at[0, i])
        for i, cols in enumerate(here)
    ]
    leave = [
        pltpu.make_async_copy(landed.at[i], out.at[:, cols], sems.at[1, i])
        for i, cols in enumerate(here)
    ]
    for copy in arrive:
        copy.start()
    for i, (side, pair, rows) in enumerate(jobs):
        h, l = split(side[...])
        value = dot3(h, l, band_high[pair, rows], band_low[pair, rows])
        arrive[i].wait()
        landed[i] = landed[i] + value
        leave[i].start()
    for copy in leave:
        copy.wait()


def apply_tail(west, east, bands, part):
    rows, width = part.shape
    args = [held(a) for a in (west, east, *bands)]
    hbm = pl.BlockSpec(memory_space=pltpu.HBM)
    return pl.pallas_call(
        tail_kernel,
        out_shape=jax.ShapeDtypeStruct((rows, width), jnp.float32),
        in_specs=[VMEM_SPEC] * 4 + [hbm],
        out_specs=hbm,
        scratch_shapes=[
            pltpu.VMEM((2, rows, PAIR), jnp.float32), pltpu.SemaphoreType.DMA((2, 2)),
        ],
        input_output_aliases={4: 0},
        compiler_params=pltpu.CompilerParams(vmem_limit_bytes=16 << 20),
        name="tail",
    )(*args, in_hbm(part))


def body(
    covariance, latitude_offset, longitude_offset, upwind, courant,
    longitude_diffusion, latitude_diffusion,
):
    block = covariance[0]
    rows, width = block.shape
    row_count, col_count = lax.axis_size("row"), lax.axis_size("col")
    forward = lambda n: [(i, i + 1) for i in range(n - 1)]
    backward = lambda n: [(i + 1, i) for i in range(n - 1)]

    chip_pairs = [(i, i ^ 1) for i in range(row_count)]
    cross_pairs = [((i + 1 ^ 1) - 1, i) for i in range(1, row_count - 1)]
    middle = row_count // 2
    last = row_count - 1
    middle_pairs = [(middle - 1, middle), (middle, middle - 1)]
    other_pairs = [pair for pair in cross_pairs if pair not in middle_pairs]
    copy_pairs = [(source ^ 1, target) for source, target in cross_pairs]

    fields = [
        a.reshape(NLAT, NLON)
        for a in (
            latitude_offset, longitude_offset, upwind, courant,
            longitude_diffusion, latitude_diffusion,
        )
    ]
    lat_row = (lax.axis_index("row") * (rows // NLON)).astype(jnp.int32).reshape(1)
    lat_col = (lax.axis_index("col") * (width // NLON)).astype(jnp.int32).reshape(1)

    starts = (0, width - PAIR, PAIR, width - 2 * PAIR)
    chip = lax.ppermute(block, "row", chip_pairs)
    own0, own1, own2 = take_columns(block, [(0, PAIR), (PAIR, 2 * PAIR), (2 * PAIR, width)])
    copy2 = lax.ppermute(own2, "row", chip_pairs)
    across0 = lax.ppermute(own0, "row", cross_pairs)
    ends = lax.ppermute(own1, "row", [(middle - 1, 0), (middle, last)])
    relay = lax.ppermute(ends, "row", [(0, middle), (last, middle - 1)])
    across1 = lax.ppermute(own1, "row", other_pairs)
    across2 = lax.ppermute(copy2, "row", copy_pairs)
    across = ([across0], [across2], [across1, relay], [across2])
    offset = (0, width - 3 * PAIR, 0, width - 4 * PAIR)
    row_bands = build_bands(lat_row, fields, rows // PAIR, True)
    half, side = [], []
    for k in range(4):
        sources = [block, chip] + across[k]
        begins = [starts[k]] * 2 + [offset[k]] * len(across[k])
        half.append(apply_rows(lat_row, PAIR, sources, begins, row_bands))
        pairs = forward(col_count) if k % 2 else backward(col_count)
        side.append(lax.ppermute(half[k], "col", pairs))
    col_bands = build_bands(lat_col, fields, width // PAIR, False)
    parts = [side[1], half[0], half[2], half[3], half[1], side[0]]
    part = apply_cols(parts, col_bands, width)
    return apply_tail(side[3], side[2], col_bands, part)[None]


def solution(mesh):
    in_specs = (P(None, "row", "col"), P(), P(), P(), P(), P(), P())
    out_specs = P(None, "row", "col")
    return jax.shard_map(body, mesh=mesh, in_specs=in_specs, out_specs=out_specs, check_vma=False)
```

```python
import functools

import jax
import jax.numpy as jnp
from jax import lax
from jax.experimental import pallas as pl
from jax.experimental.pallas import tpu as pltpu
from jax.sharding import PartitionSpec as P


NLAT = 64
NLON = 128
HALO = 4
SPAN = 10 * NLON
PAIR = 2 * NLON


def split(x):
    high = x.astype(jnp.bfloat16)
    low = (x - high.astype(jnp.float32)).astype(jnp.bfloat16)
    return high, low


def dot3(a_high, a_low, b_high, b_low):
    dot = functools.partial(jnp.dot, preferred_element_type=jnp.float32)
    return dot(a_high, b_high) + (dot(a_high, b_low) + dot(a_low, b_high))


def band_kernel(
    transposed, place, lat_off, lon_off, upwind, courant, lon_diff, lat_diff,
    high, low, depart_lat, depart_lon, near_lat, near_lon, hot,
):
    shape = (NLAT, NLON)
    lat = lax.broadcasted_iota(jnp.int32, shape, 0)
    lon = lax.broadcasted_iota(jnp.int32, shape, 1)
    up = upwind[...]
    one = jnp.ones(shape, jnp.int32)
    zero = jnp.zeros(shape, jnp.int32)
    d_lat = jnp.clip(lat + lat_off[...], 0, NLAT - 1)
    d_lon = (lon + lon_off[...]) & (NLON - 1)
    depart_lat[...] = d_lat
    depart_lon[...] = d_lon
    near_lat[...] = jnp.clip(
        d_lat + jnp.where(up == 2, one, zero) - jnp.where(up == 3, one, zero), 0, NLAT - 1
    )
    near_lon[...] = (
        d_lon + jnp.where(up == 0, one, zero) - jnp.where(up == 1, one, zero)
    ) & (NLON - 1)

    sub = lax.broadcasted_iota(jnp.int32, (NLON, NLON), 0)
    first = place[0]
    pairs = high.shape[0]

    def put(pair, half, t, value):
        if transposed:
            value = value.T
        h, l = split(value)
        cells = pl.ds(t * NLON, NLON)
        cols = pl.ds(half * NLON, NLON)
        at = (pair, cols, cells) if transposed else (pair, cells, cols)
        high[at] = h
        low[at] = l

    def fill(pair, half):
        y = first + 2 * pair + half
        lx = lon_diff[pl.ds(y, 1), :]
        ly = lat_diff[pl.ds(y, 1), :]
        core = 1.0 - 2.0 * lx - 2.0 * ly
        none = jnp.zeros_like(lx)
        reach = ((0, 0), (0, 1), (-1, 0))
        rows = (y, jnp.minimum(y + 1, NLAT - 1), jnp.maximum(y - 1, 0))
        rows = [pl.ds(r, 1) for r in rows]
        for k, row in enumerate(rows):
            on = jnp.ones((NLON, NLON), jnp.float32)
            off = jnp.zeros((NLON, NLON), jnp.float32)
            hot[2 * k] = jnp.where(sub == depart_lon[row, :], on, off)
            hot[2 * k + 1] = jnp.where(sub == near_lon[row, :], on, off)
        for t in range(2 * HALO + 1):
            far = t - HALO
            in_lat = y + far
            value = None
            for k, row in enumerate(rows):
                w = courant[row, :]
                below, above = reach[k]
                scale = ly if k else jnp.ones_like(lx)
                terms = []
                if -2 + below <= far <= 2 + above:
                    keep = jnp.where(depart_lat[row, :] == in_lat, scale * (1.0 - w), none)
                    terms.append(keep * hot[2 * k])
                if -3 + below <= far <= 3 + above:
                    take = jnp.where(near_lat[row, :] == in_lat, scale * w, none)
                    terms.append(take * hot[2 * k + 1])
                if not terms:
                    continue
                total = sum(terms[1:], terms[0])
                if k == 0:
                    beside = pltpu.roll(total, 1, 1) + pltpu.roll(total, NLON - 1, 1)
                    total = core * total + lx * beside
                value = total if value is None else value + total
            put(pair, half, t + half, value)
        put(pair, half, 0 if half else 2 * HALO + 1, jnp.zeros((NLON, NLON), jnp.float32))

    def step(pair, carry):
        fill(pair, 0)
        fill(pair, 1)
        return carry

    lax.fori_loop(0, pairs, step, 0)


VMEM_SPEC = pl.BlockSpec(memory_space=pltpu.VMEM)


def held(x):
    return pltpu.with_memory_space_constraint(x, pltpu.VMEM)


def in_hbm(x):
    return pltpu.with_memory_space_constraint(x, pltpu.HBM)


def build_bands(place, fields, pairs, transposed):
    shape = (pairs, PAIR, SPAN) if transposed else (pairs, SPAN, PAIR)
    band = pltpu.VMEM(shape, jnp.bfloat16)
    return pl.pallas_call(
        functools.partial(band_kernel, transposed),
        out_shape=(band, band),
        in_specs=[pl.BlockSpec(memory_space=pltpu.SMEM)] + [VMEM_SPEC] * 6,
        out_specs=(VMEM_SPEC,) * 2,
        scratch_shapes=[pltpu.VMEM((NLAT, NLON), jnp.int32)] * 4
        + [pltpu.VMEM((6, NLON, NLON), jnp.float32)],
        compiler_params=pltpu.CompilerParams(vmem_limit_bytes=24 << 20),
        name="row_bands" if transposed else "col_bands",
    )(place, *fields)


def take_kernel(starts, source, *refs):
    count = len(starts)
    outs, landed, sems = refs[:count], refs[count:-1], refs[-1]
    pieces = sems.shape[2]
    size = source.shape[0] // pieces
    moves = []
    for i, (at, out) in enumerate(zip(starts, outs)):
        for j in range(pieces):
            rows = pl.ds(j * size, size)
            here = landed[i].at[rows]
            moves.append(
                (
                    pltpu.make_async_copy(
                        source.at[rows, pl.ds(at, out.shape[1])], here, sems.at[0, i, j]
                    ),
                    pltpu.make_async_copy(here, out.at[rows], sems.at[1, i, j]),
                )
            )
    for arrive, _ in moves:
        arrive.start()
    for arrive, leave in moves:
        arrive.wait()
        leave.start()
    for _, leave in moves:
        leave.wait()


def take_columns(source, ranges):
    rows = source.shape[0]
    starts = [start for start, _ in ranges]
    shapes = [(rows, stop - start) for start, stop in ranges]
    hbm = pl.BlockSpec(memory_space=pltpu.HBM)
    return pl.pallas_call(
        functools.partial(take_kernel, starts),
        out_shape=tuple(jax.ShapeDtypeStruct(shape, jnp.float32) for shape in shapes),
        in_specs=[hbm],
        out_specs=(hbm,) * len(ranges),
        scratch_shapes=[pltpu.VMEM(shape, jnp.float32) for shape in shapes]
        + [pltpu.SemaphoreType.DMA((2, len(ranges), 4))],
        compiler_params=pltpu.CompilerParams(vmem_limit_bytes=8 << 20),
        name="take",
    )(in_hbm(source))


def rows_kernel(starts, place, *refs):
    *sources, band_high, band_low, out, high, low, landed, sems = refs
    rows, width = out.shape
    copies = [
        pltpu.make_async_copy(ref.at[:, pl.ds(start, width)], landed.at[i], sems.at[i])
        for i, (start, ref) in enumerate(zip(starts, sources))
    ]
    for copy in copies:
        copy.start()
    odd = (place[0] // HALO) & 1
    to_chip = pl.multiple_of((1 - odd) * 2 * rows, rows)
    to_cross = pl.multiple_of(odd * 2 * rows, rows)

    def put(value, at):
        h, l = split(value)
        high[pl.ds(at, rows), :] = h
        low[pl.ds(at, rows), :] = l

    copies[0].wait()
    put(landed[0], rows)
    copies[1].wait()
    put(landed[1], to_chip)
    for copy in copies[2:]:
        copy.wait()
    put(sum((landed[i] for i in range(3, len(copies))), landed[2]), to_cross)
    for pair in range(rows // PAIR):
        at = pair * PAIR
        out[at : at + PAIR, :] = dot3(
            band_high[pair], band_low[pair], high[at : at + SPAN, :], low[at : at + SPAN, :]
        )


def apply_rows(place, width, sources, starts, bands):
    rows = sources[0].shape[0]
    ext = pltpu.VMEM((3 * rows, width), jnp.bfloat16)
    landed = pltpu.VMEM((len(sources), rows, width), jnp.float32)
    return pl.pallas_call(
        functools.partial(rows_kernel, starts),
        out_shape=pltpu.VMEM((rows, width), jnp.float32),
        in_specs=[pl.BlockSpec(memory_space=pltpu.SMEM)]
        + [pl.BlockSpec(memory_space=pltpu.HBM)] * len(sources)
        + [VMEM_SPEC] * 2,
        out_specs=VMEM_SPEC,
        scratch_shapes=[ext, ext, landed, pltpu.SemaphoreType.DMA((len(sources),))],
        compiler_params=pltpu.CompilerParams(vmem_limit_bytes=16 << 20),
        name="rows",
    )(place, *(in_hbm(a) for a in sources), *(held(a) for a in bands))


def cols_kernel(*refs):
    parts = refs[:-5]
    band_high, band_low, out, high, low = refs[-5:]
    at = 0
    for ref in parts:
        h, l = split(ref[...])
        high[:, at : at + ref.shape[1]] = h
        low[:, at : at + ref.shape[1]] = l
        at += ref.shape[1]
    for pair in range(out.shape[1] // PAIR):
        begin = (pair - 2) * PAIR
        skip = max(0, -begin)
        stop = min(at, begin + SPAN)
        ext = slice(begin + skip, stop)
        band = slice(skip, stop - begin)
        out[:, pair * PAIR : (pair + 1) * PAIR] = dot3(
            high[:, ext], low[:, ext], band_high[pair, band], band_low[pair, band]
        )


def apply_cols(parts, bands, width):
    rows = parts[0].shape[0]
    ext = pltpu.VMEM((rows, sum(p.shape[1] for p in parts)), jnp.bfloat16)
    args = [held(a) for a in (*parts, *bands)]
    return pl.pallas_call(
        cols_kernel,
        out_shape=jax.ShapeDtypeStruct((rows, width), jnp.float32),
        in_specs=[VMEM_SPEC] * len(args),
        out_specs=VMEM_SPEC,
        scratch_shapes=[ext, ext],
        compiler_params=pltpu.CompilerParams(vmem_limit_bytes=32 << 20),
        name="cols",
    )(*args)


def tail_kernel(jobs, *refs):
    *sides, band_high, band_low, part, out, landed, sems = refs
    here = [pl.ds(pair * PAIR, PAIR) for _, pair, _ in jobs]
    arrive = [
        pltpu.make_async_copy(part.at[:, cols], landed.at[i], sems.at[0, i])
        for i, cols in enumerate(here)
    ]
    leave = [
        pltpu.make_async_copy(landed.at[i], out.at[:, cols], sems.at[1, i])
        for i, cols in enumerate(here)
    ]
    for copy in arrive:
        copy.start()
    pieces = [split(side[...]) for side in sides]
    for i, (side, pair, at) in enumerate(jobs):
        rows = slice(at, at + PAIR)
        value = dot3(*pieces[side], band_high[pair, rows], band_low[pair, rows])
        arrive[i].wait()
        landed[i] = landed[i] + value
        leave[i].start()
    for copy in leave:
        copy.wait()


def apply_tail(sides, bands, part, jobs):
    rows, width = part.shape
    args = [held(a) for a in (*sides, *bands)]
    hbm = pl.BlockSpec(memory_space=pltpu.HBM)
    return pl.pallas_call(
        functools.partial(tail_kernel, jobs),
        out_shape=jax.ShapeDtypeStruct((rows, width), jnp.float32),
        in_specs=[VMEM_SPEC] * len(args) + [hbm],
        out_specs=hbm,
        scratch_shapes=[
            pltpu.VMEM((len(jobs), rows, PAIR), jnp.float32),
            pltpu.SemaphoreType.DMA((2, len(jobs))),
        ],
        input_output_aliases={len(args): 0},
        compiler_params=pltpu.CompilerParams(vmem_limit_bytes=16 << 20),
        name="tail",
    )(*args, in_hbm(part))


def body(
    covariance, latitude_offset, longitude_offset, upwind, courant,
    longitude_diffusion, latitude_diffusion,
):
    block = covariance[0]
    rows, width = block.shape
    row_count, col_count = lax.axis_size("row"), lax.axis_size("col")
    forward = lambda n: [(i, i + 1) for i in range(n - 1)]
    backward = lambda n: [(i + 1, i) for i in range(n - 1)]

    chip_pairs = [(i, i ^ 1) for i in range(row_count)]
    cross_pairs = [((i + 1 ^ 1) - 1, i) for i in range(1, row_count - 1)]
    middle = row_count // 2
    last = row_count - 1
    middle_pairs = [(middle - 1, middle), (middle, middle - 1)]
    other_pairs = [pair for pair in cross_pairs if pair not in middle_pairs]
    copy_pairs = [(source ^ 1, target) for source, target in cross_pairs]

    fields = [
        a.reshape(NLAT, NLON)
        for a in (
            latitude_offset, longitude_offset, upwind, courant,
            longitude_diffusion, latitude_diffusion,
        )
    ]
    lat_row = (lax.axis_index("row") * (rows // NLON)).astype(jnp.int32).reshape(1)
    lat_col = (lax.axis_index("col") * (width // NLON)).astype(jnp.int32).reshape(1)

    starts = (0, width - PAIR, PAIR, width - 2 * PAIR)
    chip = lax.ppermute(block, "row", chip_pairs)
    own0, own1, own2 = take_columns(
        block, [(0, PAIR), (PAIR, 2 * PAIR), (2 * PAIR, width)]
    )
    copy2 = lax.ppermute(own2, "row", chip_pairs)
    across0 = lax.ppermute(own0, "row", cross_pairs)
    ends = lax.ppermute(own1, "row", [(middle - 1, 0), (middle, last)])
    relay = lax.ppermute(ends, "row", [(0, middle), (last, middle - 1)])
    across1 = lax.ppermute(own1, "row", other_pairs)
    across2 = lax.ppermute(copy2, "row", copy_pairs)
    across = ([across0], [across2], [across1, relay], [across2])
    offset = (0, width - 3 * PAIR, 0, width - 4 * PAIR)
    row_bands = build_bands(lat_row, fields, rows // PAIR, True)
    half, side = [], []
    for k in range(4):
        sources = [block, chip] + across[k]
        begins = [starts[k]] * 2 + [offset[k]] * len(across[k])
        half.append(apply_rows(lat_row, PAIR, sources, begins, row_bands))
        pairs = forward(col_count) if k % 2 else backward(col_count)
        side.append(lax.ppermute(half[k], "col", pairs))
    col_bands = build_bands(lat_col, fields, width // PAIR, False)
    parts = [half[0], half[2], half[3], half[1]]
    part = apply_cols(parts, col_bands, width)
    end = width // PAIR - 1
    first = [(0, end - 1, SPAN - PAIR), (0, end, SPAN - 2 * PAIR), (1, 0, PAIR), (1, 1, 0)]
    second = [(0, end, SPAN - PAIR), (1, 0, 0)]
    part = apply_tail(side[:2], col_bands, part, first)
    return apply_tail(side[2:], col_bands, part, second)[None]


def solution(mesh):
    in_specs = (P(None, "row", "col"), P(), P(), P(), P(), P(), P())
    out_specs = P(None, "row", "col")
    return jax.shard_map(
        body, mesh=mesh, in_specs=in_specs, out_specs=out_specs, check_vma=False
    )
```

```python
import functools

import jax
import jax.numpy as jnp
from jax import lax
from jax.experimental import pallas as pl
from jax.experimental.pallas import tpu as pltpu
from jax.sharding import PartitionSpec as P


NLAT = 64
NLON = 128
HALO = 4
SPAN = 10 * NLON
PAIR = 2 * NLON


def split(x):
    high = x.astype(jnp.bfloat16)
    low = (x - high.astype(jnp.float32)).astype(jnp.bfloat16)
    return high, low


def dot3(a_high, a_low, b_high, b_low):
    dot = functools.partial(jnp.dot, preferred_element_type=jnp.float32)
    return dot(a_high, b_high) + (dot(a_high, b_low) + dot(a_low, b_high))


def band_kernel(
    transposed, place, lat_off, lon_off, upwind, courant, lon_diff, lat_diff,
    high, low, depart_lat, depart_lon, near_lat, near_lon, hot,
):
    shape = (NLAT, NLON)
    lat = lax.broadcasted_iota(jnp.int32, shape, 0)
    lon = lax.broadcasted_iota(jnp.int32, shape, 1)
    up = upwind[...]
    one = jnp.ones(shape, jnp.int32)
    zero = jnp.zeros(shape, jnp.int32)
    d_lat = jnp.clip(lat + lat_off[...], 0, NLAT - 1)
    d_lon = (lon + lon_off[...]) & (NLON - 1)
    depart_lat[...] = d_lat
    depart_lon[...] = d_lon
    near_lat[...] = jnp.clip(
        d_lat + jnp.where(up == 2, one, zero) - jnp.where(up == 3, one, zero), 0, NLAT - 1
    )
    near_lon[...] = (
        d_lon + jnp.where(up == 0, one, zero) - jnp.where(up == 1, one, zero)
    ) & (NLON - 1)

    sub = lax.broadcasted_iota(jnp.int32, (NLON, NLON), 0)
    first = place[0]
    pairs = high.shape[0]

    def put(pair, half, t, value):
        if transposed:
            value = value.T
        h, l = split(value)
        cells = pl.ds(t * NLON, NLON)
        cols = pl.ds(half * NLON, NLON)
        at = (pair, cols, cells) if transposed else (pair, cells, cols)
        high[at] = h
        low[at] = l

    def fill(pair, half):
        y = first + 2 * pair + half
        lx = lon_diff[pl.ds(y, 1), :]
        ly = lat_diff[pl.ds(y, 1), :]
        core = 1.0 - 2.0 * lx - 2.0 * ly
        none = jnp.zeros_like(lx)
        reach = ((0, 0), (0, 1), (-1, 0))
        rows = (y, jnp.minimum(y + 1, NLAT - 1), jnp.maximum(y - 1, 0))
        rows = [pl.ds(r, 1) for r in rows]
        for k, row in enumerate(rows):
            on = jnp.ones((NLON, NLON), jnp.float32)
            off = jnp.zeros((NLON, NLON), jnp.float32)
            hot[2 * k] = jnp.where(sub == depart_lon[row, :], on, off)
            hot[2 * k + 1] = jnp.where(sub == near_lon[row, :], on, off)
        for t in range(2 * HALO + 1):
            far = t - HALO
            in_lat = y + far
            value = None
            for k, row in enumerate(rows):
                w = courant[row, :]
                below, above = reach[k]
                scale = ly if k else jnp.ones_like(lx)
                terms = []
                if -2 + below <= far <= 2 + above:
                    keep = jnp.where(depart_lat[row, :] == in_lat, scale * (1.0 - w), none)
                    terms.append(keep * hot[2 * k])
                if -3 + below <= far <= 3 + above:
                    take = jnp.where(near_lat[row, :] == in_lat, scale * w, none)
                    terms.append(take * hot[2 * k + 1])
                if not terms:
                    continue
                total = sum(terms[1:], terms[0])
                if k == 0:
                    beside = pltpu.roll(total, 1, 1) + pltpu.roll(total, NLON - 1, 1)
                    total = core * total + lx * beside
                value = total if value is None else value + total
            put(pair, half, t + half, value)
        put(pair, half, 0 if half else 2 * HALO + 1, jnp.zeros((NLON, NLON), jnp.float32))

    def step(pair, carry):
        fill(pair, 0)
        fill(pair, 1)
        return carry

    lax.fori_loop(0, pairs, step, 0)


VMEM_SPEC = pl.BlockSpec(memory_space=pltpu.VMEM)


def held(x):
    return pltpu.with_memory_space_constraint(x, pltpu.VMEM)


def in_hbm(x):
    return pltpu.with_memory_space_constraint(x, pltpu.HBM)


def build_bands(place, fields, pairs, transposed):
    shape = (pairs, PAIR, SPAN) if transposed else (pairs, SPAN, PAIR)
    band = pltpu.VMEM(shape, jnp.bfloat16)
    return pl.pallas_call(
        functools.partial(band_kernel, transposed),
        out_shape=(band, band),
        in_specs=[pl.BlockSpec(memory_space=pltpu.SMEM)] + [VMEM_SPEC] * 6,
        out_specs=(VMEM_SPEC,) * 2,
        scratch_shapes=[pltpu.VMEM((NLAT, NLON), jnp.int32)] * 4
        + [pltpu.VMEM((6, NLON, NLON), jnp.float32)],
        compiler_params=pltpu.CompilerParams(vmem_limit_bytes=24 << 20),
        name="row_bands" if transposed else "col_bands",
    )(place, *fields)


def take_kernel(starts, source, *refs):
    count = len(starts)
    outs, landed, sems = refs[:count], refs[count:-1], refs[-1]
    pieces = sems.shape[2]
    size = source.shape[0] // pieces
    moves = []
    for i, (at, out) in enumerate(zip(starts, outs)):
        for j in range(pieces):
            rows = pl.ds(j * size, size)
            here = landed[i].at[rows]
            moves.append(
                (
                    pltpu.make_async_copy(
                        source.at[rows, pl.ds(at, out.shape[1])], here, sems.at[0, i, j]
                    ),
                    pltpu.make_async_copy(here, out.at[rows], sems.at[1, i, j]),
                )
            )
    for arrive, _ in moves:
        arrive.start()
    for arrive, leave in moves:
        arrive.wait()
        leave.start()
    for _, leave in moves:
        leave.wait()


def take_columns(source, space, ranges):
    rows = source.shape[0]
    starts = [start for start, _ in ranges]
    shapes = [(rows, stop - start) for start, stop in ranges]
    hbm = pl.BlockSpec(memory_space=pltpu.HBM)
    return pl.pallas_call(
        functools.partial(take_kernel, starts),
        out_shape=tuple(jax.ShapeDtypeStruct(shape, jnp.float32) for shape in shapes),
        in_specs=[pl.BlockSpec(memory_space=space)],
        out_specs=(hbm,) * len(ranges),
        scratch_shapes=[pltpu.VMEM(shape, jnp.float32) for shape in shapes]
        + [pltpu.SemaphoreType.DMA((2, len(ranges), 4))],
        compiler_params=pltpu.CompilerParams(vmem_limit_bytes=8 << 20),
        name="take",
    )(source)


def rows_kernel(starts, place, *refs):
    *sources, band_high, band_low, out, high, low, landed, sems = refs
    rows, width = out.shape
    copies = [
        pltpu.make_async_copy(ref.at[:, pl.ds(start, width)], landed.at[i], sems.at[i])
        for i, (start, ref) in enumerate(zip(starts, sources))
    ]
    for copy in copies:
        copy.start()
    odd = (place[0] // HALO) & 1
    to_chip = pl.multiple_of((1 - odd) * 2 * rows, rows)
    to_cross = pl.multiple_of(odd * 2 * rows, rows)

    def put(value, at):
        h, l = split(value)
        high[pl.ds(at, rows), :] = h
        low[pl.ds(at, rows), :] = l

    copies[0].wait()
    put(landed[0], rows)
    copies[1].wait()
    put(landed[1], to_chip)
    for copy in copies[2:]:
        copy.wait()
    put(sum((landed[i] for i in range(3, len(copies))), landed[2]), to_cross)
    for pair in range(rows // PAIR):
        at = pair * PAIR
        out[at : at + PAIR, :] = dot3(
            band_high[pair], band_low[pair], high[at : at + SPAN, :], low[at : at + SPAN, :]
        )


def apply_rows(place, width, sources, starts, bands):
    rows = sources[0].shape[0]
    ext = pltpu.VMEM((3 * rows, width), jnp.bfloat16)
    landed = pltpu.VMEM((len(sources), rows, width), jnp.float32)
    return pl.pallas_call(
        functools.partial(rows_kernel, starts),
        out_shape=pltpu.VMEM((rows, width), jnp.float32),
        in_specs=[pl.BlockSpec(memory_space=pltpu.SMEM)]
        + [pl.BlockSpec(memory_space=pltpu.HBM)]
        + [pl.BlockSpec(memory_space=pl.ANY)] * (len(sources) - 1)
        + [VMEM_SPEC] * 2,
        out_specs=VMEM_SPEC,
        scratch_shapes=[ext, ext, landed, pltpu.SemaphoreType.DMA((len(sources),))],
        compiler_params=pltpu.CompilerParams(vmem_limit_bytes=16 << 20),
        name="rows",
    )(place, in_hbm(sources[0]), *sources[1:], *(held(a) for a in bands))


def cols_kernel(*refs):
    parts = refs[:-5]
    band_high, band_low, out, high, low = refs[-5:]
    at = 0
    for ref in parts:
        h, l = split(ref[...])
        high[:, at : at + ref.shape[1]] = h
        low[:, at : at + ref.shape[1]] = l
        at += ref.shape[1]
    for pair in range(out.shape[1] // PAIR):
        begin = (pair - 1) * PAIR
        skip = max(0, -begin)
        stop = min(at, begin + SPAN)
        ext = slice(begin + skip, stop)
        band = slice(skip, stop - begin)
        out[:, pair * PAIR : (pair + 1) * PAIR] = dot3(
            high[:, ext], low[:, ext], band_high[pair, band], band_low[pair, band]
        )


def apply_cols(parts, bands, width):
    rows = parts[0].shape[0]
    ext = pltpu.VMEM((rows, sum(p.shape[1] for p in parts)), jnp.bfloat16)
    args = [held(a) for a in (*parts, *bands)]
    return pl.pallas_call(
        cols_kernel,
        out_shape=jax.ShapeDtypeStruct((rows, width), jnp.float32),
        in_specs=[VMEM_SPEC] * len(args),
        out_specs=VMEM_SPEC,
        scratch_shapes=[ext, ext],
        compiler_params=pltpu.CompilerParams(vmem_limit_bytes=32 << 20),
        name="cols",
    )(*args)


def tail_kernel(west, east, band_high, band_low, part, out):
    last = band_high.shape[0] - 1

    def add(ref, pair, rows):
        h, l = split(ref[...])
        out[...] = part[...] + dot3(h, l, band_high[pair, rows], band_low[pair, rows])

    @pl.when(pl.program_id(0) == 0)
    def _():
        add(east, last, slice(SPAN - east.shape[1], SPAN))

    @pl.when(pl.program_id(0) == 1)
    def _():
        add(west, 0, slice(0, west.shape[1]))


def apply_tail(west, east, bands, part):
    rows, width = part.shape
    block = pl.BlockSpec((rows, PAIR), lambda i: (0, (1 - i) * (width // PAIR - 1)))
    args = [held(a) for a in (west, east, *bands)]
    return pl.pallas_call(
        tail_kernel,
        grid=(2,),
        out_shape=jax.ShapeDtypeStruct((rows, width), jnp.float32),
        in_specs=[VMEM_SPEC] * 4 + [block],
        out_specs=block,
        input_output_aliases={4: 0},
        compiler_params=pltpu.CompilerParams(vmem_limit_bytes=16 << 20),
        name="tail",
    )(*args, part)


def body(
    covariance, latitude_offset, longitude_offset, upwind, courant,
    longitude_diffusion, latitude_diffusion,
):
    block = covariance[0]
    rows, width = block.shape
    row_count, col_count = lax.axis_size("row"), lax.axis_size("col")
    forward = lambda n: [(i, i + 1) for i in range(n - 1)]
    backward = lambda n: [(i + 1, i) for i in range(n - 1)]

    chip_pairs = [(i, i ^ 1) for i in range(row_count)]
    cross_pairs = [((i + 1 ^ 1) - 1, i) for i in range(1, row_count - 1)]
    middle = row_count // 2
    last = row_count - 1
    middle_pairs = [(middle - 1, middle), (middle, middle - 1)]
    other_pairs = [pair for pair in cross_pairs if pair not in middle_pairs]
    copy_pairs = [(source ^ 1, target) for source, target in cross_pairs]

    fields = [
        a.reshape(NLAT, NLON)
        for a in (
            latitude_offset, longitude_offset, upwind, courant,
            longitude_diffusion, latitude_diffusion,
        )
    ]
    lat_row = (lax.axis_index("row") * (rows // NLON)).astype(jnp.int32).reshape(1)
    lat_col = (lax.axis_index("col") * (width // NLON)).astype(jnp.int32).reshape(1)

    starts = (0, width - PAIR, PAIR, width - 2 * PAIR)
    chip = lax.ppermute(block, "row", chip_pairs)
    own0, own1 = take_columns(in_hbm(block), pltpu.HBM, [(0, PAIR), (PAIR, 2 * PAIR)])
    (copy2,) = take_columns(chip, pl.ANY, [(2 * PAIR, width)])
    across0 = lax.ppermute(own0, "row", cross_pairs)
    ends = lax.ppermute(own1, "row", [(middle - 1, 0), (middle, last)])
    relay = lax.ppermute(ends, "row", [(0, middle), (last, middle - 1)])
    across1 = lax.ppermute(own1, "row", other_pairs)
    across2 = lax.ppermute(copy2, "row", copy_pairs)
    across = ([across0], [across2], [across1, relay], [across2])
    offset = (0, width - 3 * PAIR, 0, width - 4 * PAIR)
    row_bands = build_bands(lat_row, fields, rows // PAIR, True)
    half, side = [], []
    for k in range(4):
        sources = [block, chip] + across[k]
        begins = [starts[k]] * 2 + [offset[k]] * len(across[k])
        half.append(apply_rows(lat_row, PAIR, sources, begins, row_bands))
        pairs = forward(col_count) if k % 2 else backward(col_count)
        side.append(lax.ppermute(half[k], "col", pairs))
    col_bands = build_bands(lat_col, fields, width // PAIR, False)
    parts = [side[1], half[0], half[2], half[3], half[1], side[0]]
    part = apply_cols(parts, col_bands, width)
    return apply_tail(side[3], side[2], col_bands, part)[None]


def solution(mesh):
    in_specs = (P(None, "row", "col"), P(), P(), P(), P(), P(), P())
    out_specs = P(None, "row", "col")
    return jax.shard_map(
        body, mesh=mesh, in_specs=in_specs, out_specs=out_specs, check_vma=False
    )
```
